32 devices in a mesh: fsdp: 8 (over y, x, core), dp: 4 (over z).
Axes of the slice: x: 2, y: 2, z: 4, core: 2. Of those that a mesh axis runs over, the one named last changes fastest.
Arguments:
- tokens: bfloat16 [16384, 768], P(('fsdp', 'dp')), may hold values from -6 to 6
- segment_ids: int32 [128, 128], P(('fsdp', 'dp')), may hold values from 0 to 7, never falling along the last dimension, each value on 1 to 32 neighbouring positions
- cotangent: bfloat16 [16384, 768], P(('fsdp', 'dp')), may hold values from -6 to 6
- qkv_weight: float32 [2, 768, 2304], P(None, 'fsdp'), may hold values from -0.21875 to 0.21875
- out_weight: float32 [2, 768, 768], P(None, 'fsdp'), may hold values from -0.875 to 0.875
- in_weight: float32 [2, 768, 3072], P(None, 'fsdp'), may hold values from -0.21875 to 0.21875
- back_weight: float32 [2, 3072, 768], P(None, 'fsdp'), may hold values from -0.109375 to 0.109375
- vectors: float32 [2, 12, 768], P(None, None, 'fsdp'), may hold values from -0.5 to 1.4, as said below
- qkv_moments: float32 [2, 2, 768, 2304], P(None, None, 'fsdp'), as said below
- out_moments: float32 [2, 2, 768, 768], P(None, None, 'fsdp'), as said below
- in_moments: float32 [2, 2, 768, 3072], P(None, None, 'fsdp'), as said below
- back_moments: float32 [2, 2, 3072, 768], P(None, None, 'fsdp'), as said below
- vector_moments: float32 [2, 2, 12, 768], P(None, None, None, 'fsdp'), as said below
Outputs:
- activations: bfloat16 [16384, 768], P(('fsdp', 'dp'))
- input_grad: float32 [16384, 768], P(('fsdp', 'dp'))
- qkv_grad: float32 [2, 768, 2304], P(None, 'fsdp')
- out_grad: float32 [2, 768, 768], P(None, 'fsdp')
- in_grad: float32 [2, 768, 3072], P(None, 'fsdp')
- back_grad: float32 [2, 3072, 768], P(None, 'fsdp')
- vector_grad: float32 [2, 12, 768], P(None, None, 'fsdp')
- qkv_new: float32 [2, 768, 2304], P(None, 'fsdp')
- out_new: float32 [2, 768, 768], P(None, 'fsdp')
- in_new: float32 [2, 768, 3072], P(None, 'fsdp')
- back_new: float32 [2, 3072, 768], P(None, 'fsdp')
- vector_new: float32 [2, 12, 768], P(None, None, 'fsdp')
- qkv_state: float32 [2, 768, 2304], P(None, 'fsdp')
- out_state: float32 [2, 768, 768], P(None, 'fsdp')
- in_state: float32 [2, 768, 3072], P(None, 'fsdp')
- back_state: float32 [2, 3072, 768], P(None, 'fsdp')
- vector_state: float32 [2, 12, 768], P(None, None, 'fsdp')
The draws below stay inside these ranges and needn't reach their ends.
Inputs may be any that keep to these rules, and one draw needn't show every extreme that they name: `segment_ids`: within each packed row the numbers never fall and take every value 0 to 7, one per sentence; each sentence has 1 to 32 tokens and one has exactly 32. `vectors`: rows 3 and 10 of each layer are norm gains between 0.6 and 1.4; the other rows are biases between -0.5 and 0.5. `qkv_moments`: index 1 holds second moments, all positive. `out_moments`: index 1 holds second moments, all positive. `in_moments`: index 1 holds second moments, all positive. `back_moments`: index 1 holds second moments, all positive. `vector_moments`: index 1 holds second moments, all positive.
All inputs are finite; a program needn't handle non-finite values.
Results may differ from the reference program's by a relative error of at most 0.02.
Values may be sent and summed in bfloat16 or wider, within the bound.
A program may use at most 256 MiB of HBM per device.

```python
import math
import jax
import jax.numpy as jnp
import numpy as np
from jax import lax

D = 768
HEADS = 12
HEAD_DIM = 64
FF = 3072
ROW_LEN = 128
SEGS = 8
MOST_SEG = 32
LAYERS = 2
STEP = 3
ROWS = 128
TOKENS = 16384


def moment_pair(key, full_shape, share):
    moment_level = TOKENS * share
    first_moment = jnp.clip(jax.random.normal(jax.random.fold_in(key, 11), full_shape, jnp.float32), -4.0, 4.0) * math.sqrt(moment_level)
    spread_ratio = jnp.exp(jax.random.uniform(jax.random.fold_in(key, 12), full_shape, jnp.float32, minval=math.log(0.5), maxval=math.log(8.0)))
    return jnp.stack([first_moment, spread_ratio * moment_level]).astype(jnp.float32)


def draw_vectors(key, part):
    full_shape = (LAYERS, 12, D)
    biases = jax.random.uniform(jax.random.fold_in(key, 21), full_shape, jnp.float32, minval=-0.5, maxval=0.5)
    gains = jax.random.uniform(jax.random.fold_in(key, 22), full_shape, jnp.float32, minval=0.6, maxval=1.4)
    row_index = jnp.arange(12)[None, :, None]
    return jnp.where((row_index == 3) | (row_index == 10), gains, biases).astype(jnp.float32)


def draw_qkv_moments(key, part):
    return moment_pair(key, (LAYERS, D, 3 * D), 0.25)


def draw_out_moments(key, part):
    return moment_pair(key, (LAYERS, D, D), 0.0625)


def draw_in_moments(key, part):
    return moment_pair(key, (LAYERS, D, FF), 0.0625)


def draw_back_moments(key, part):
    return moment_pair(key, (LAYERS, FF, D), 0.25)


def draw_vector_moments(key, part):
    return moment_pair(key, (LAYERS, 12, D), 0.25)


def block_scale(key, extent, split, least, largest):
    factor_of, own = 1.0, jax.random.fold_in(key, 6)
    for position, blocks in split:
        draws = jnp.exp(jax.random.uniform(jax.random.fold_in(own, position), (blocks,), jnp.float32, least / len(split), largest / len(split)))
        factor_of = factor_of * jnp.repeat(draws, extent[position] // blocks).reshape([-1 if axis == position else 1 for axis in range(len(extent))])
    return factor_of


def profile(count, total, bound, lean):
    loads = [(1 << 20) // math.isqrt(grade ** lean) + 1 for grade in range(2, count + 1)]
    spare, counts = total - bound - (count - 1), [1] * (count - 1)
    while spare > 0:
        movable = [i for i in range(count - 1) if counts[i] < bound]
        pool, left = sum([loads[i] for i in movable]), spare
        for i in movable:
            extra = min(bound - counts[i], max(1, left * loads[i] // pool), spare)
            counts[i] = counts[i] + extra
            spare = spare - extra
    return np.array([bound] + counts)


def uneven_parts(rng, count, total, most, skew):
    if count == 2:
        one = jax.random.randint(rng, (), max(1, total - most), min(most, total - 1) + 1)
        return jnp.stack([one, total - one])
    tallies = jnp.asarray(profile(count, total, most, skew), jnp.int32)
    couples = (count - 1) // 2
    giver, taker = tallies[1:1 + 2 * couples:2], tallies[2:2 + 2 * couples:2]
    margin = jnp.minimum(giver - 1, most - taker)
    shifted = jax.random.randint(jax.random.fold_in(rng, 1), (couples,), 0, 1 << 20) % (margin + 1)
    tallies = tallies.at[1:1 + 2 * couples:2].set(giver - shifted).at[2:2 + 2 * couples:2].set(taker + shifted)
    return tallies[jax.random.permutation(jax.random.fold_in(rng, 2), count)]


def noise(stream_key, extent, spread, limit, pieces=(), kind=jnp.bfloat16):
    loudness = block_scale(stream_key, extent, pieces, -0.22, 0.18) if pieces else 1.0
    drawn = jax.random.normal(stream_key, extent, jnp.float32) * spread * loudness
    return jnp.minimum(jnp.maximum(drawn, -limit), limit).astype(kind)


def setup_inputs(seed: int = 0) -> dict:
    seeds = jax.random.split(jax.random.key(seed), 14)
    tokens = noise(seeds[0], (TOKENS, D), 1.0, 6.0, ((0, 32),))
    segment_ids = jax.vmap(lambda own: jnp.searchsorted(jnp.cumsum(uneven_parts(own, SEGS, ROW_LEN, MOST_SEG, 1)), jnp.arange(ROW_LEN), side="right"))(jax.random.split(seeds[1], ROWS)).reshape((ROWS, ROW_LEN)).astype(jnp.int32)
    cotangent = noise(seeds[2], (TOKENS, D), 1.0, 6.0, ((0, 32),))
    qkv_weight = noise(seeds[3], (LAYERS, D, 3 * D), D ** -0.5, 0.21875, ((1, 8),), jnp.float32)
    out_weight = noise(seeds[4], (LAYERS, D, D), (D // 16) ** -0.5, 0.875, ((1, 8),), jnp.float32)
    in_weight = noise(seeds[5], (LAYERS, D, FF), D ** -0.5, 0.21875, ((1, 8),), jnp.float32)
    back_weight = noise(seeds[6], (LAYERS, FF, D), FF ** -0.5, 0.109375, ((1, 8),), jnp.float32)
    vectors = draw_vectors(jax.random.fold_in(seeds[13], 71), 0)
    qkv_moments = draw_qkv_moments(jax.random.fold_in(seeds[13], 71), 0)
    out_moments = draw_out_moments(jax.random.fold_in(seeds[13], 71), 0)
    in_moments = draw_in_moments(jax.random.fold_in(seeds[13], 71), 0)
    back_moments = draw_back_moments(jax.random.fold_in(seeds[13], 71), 0)
    vector_moments = draw_vector_moments(jax.random.fold_in(seeds[13], 71), 0)
    return dict(tokens=tokens, segment_ids=segment_ids, cotangent=cotangent, qkv_weight=qkv_weight, out_weight=out_weight, in_weight=in_weight, back_weight=back_weight, vectors=vectors, qkv_moments=qkv_moments, out_moments=out_moments, in_moments=in_moments, back_moments=back_moments, vector_moments=vector_moments)


EPSILON = 1e-05
NEGATIVE = -1000000000.0
BETA_FIRST = 0.5
BETA_SECOND = 0.5
WEIGHT_DECAY = 0.01
ADAM_EPSILON = 1e-08
RATE_MATRIX = 0.06
RATE_VECTOR = 0.5
HIGHEST = lax.Precision.HIGHEST

@jax.custom_vjp
def low(v):
    return lax.optimization_barrier(v.astype(jnp.bfloat16)).astype(jnp.float32)

@jax.custom_vjp
def low_back(v):
    return v

def low_keep(v):
    return (low(v), None)

def low_pass(kept, grad):
    return (grad,)

def back_keep(v):
    return (v, None)

def back_low(kept, grad):
    return (low(grad),)
low.defvjp(low_keep, low_pass)
low_back.defvjp(back_keep, back_low)

def layer_norm(values, gain_row, shift_row):
    centered = values - lax.optimization_barrier(jnp.mean(values, axis=-1, keepdims=True))
    scaled = centered * lax.rsqrt(lax.optimization_barrier(jnp.mean(centered * centered, axis=-1, keepdims=True)) + EPSILON)
    return scaled * gain_row + shift_row

def encoder_layer(hidden, segment_block, weights):
    qkv_used, out_used, in_used, back_used, vector = weights
    row_count = segment_block.shape[0]
    bias_qkv = jnp.concatenate([vector[0], jnp.zeros((D,), vector.dtype), vector[1]])
    joined = low_back(low(jnp.dot(low(hidden), qkv_used, precision=HIGHEST) + bias_qkv))
    joined = joined.reshape(row_count, ROW_LEN, 3, HEADS, HEAD_DIM)
    queries = joined[:, :, 0]
    key_part = joined[:, :, 1]
    value_part = joined[:, :, 2]
    raw_scores = jnp.einsum('rqhe,rkhe->rhqk', queries, key_part, precision=HIGHEST) * HEAD_DIM ** (-0.5)
    same_segment = (segment_block[:, :, None] == segment_block[:, None, :])[:, None]
    scores = jnp.where(same_segment, low_back(raw_scores), NEGATIVE)
    probs_full = jax.nn.softmax(scores, axis=-1)
    attended = jnp.einsum('rhqk,rkhe->rqhe', low(probs_full), value_part, precision=HIGHEST)
    attended = low_back(low(attended.reshape(row_count * ROW_LEN, D)))
    branch = low_back(jnp.dot(attended, out_used, precision=HIGHEST)) + vector[2]
    first_norm = layer_norm(hidden + branch, vector[3], vector[4])
    inner_pre = low_back(jnp.dot(low(first_norm), in_used, precision=HIGHEST) + vector[5:9].reshape(FF))
    active = low(jax.nn.gelu(inner_pre, approximate=False))
    outer_out = low_back(jnp.dot(active, back_used, precision=HIGHEST)) + vector[9]
    return layer_norm(first_norm + outer_out, vector[10], vector[11])

def network(params, hidden, segment_block):
    for layer_at in range(LAYERS):
        weights = tuple((low(stacked[layer_at]) for stacked in params))
        hidden = encoder_layer(hidden, segment_block, weights)
    return hidden

def adam_update(weight, gradient, moments, step_rate):
    first_moment = BETA_FIRST * moments[0] + (1.0 - BETA_FIRST) * gradient
    second_moment = BETA_SECOND * moments[1] + (1.0 - BETA_SECOND) * gradient * gradient
    first_hat = first_moment / (1.0 - BETA_FIRST ** STEP)
    second_hat = second_moment / (1.0 - BETA_SECOND ** STEP)
    updated = weight - step_rate * (first_hat / (jnp.sqrt(second_hat) + ADAM_EPSILON) + WEIGHT_DECAY * weight)
    return (updated, second_moment)

def reference(tokens, segment_ids, cotangent, qkv_weight, out_weight, in_weight, back_weight, vectors, qkv_moments, out_moments, in_moments, back_moments, vector_moments):
    params = (qkv_weight, out_weight, in_weight, back_weight, vectors)
    group_rows = 32
    steps_count = ROWS // group_rows
    inputs = tokens.astype(jnp.float32).reshape(steps_count, group_rows * ROW_LEN, D)
    segment_groups = segment_ids.reshape(steps_count, group_rows, ROW_LEN)
    cotangent_groups = cotangent.astype(jnp.float32).reshape(steps_count, group_rows * ROW_LEN, D)

    def scan_step(totals, scan_item):
        hidden, segment_block, cotangent_block = scan_item

        def forward(param_set, values):
            return network(param_set, values, segment_block)
        output, pullback = jax.vjp(forward, params, hidden)
        weight_grads, grad_input = pullback(cotangent_block)
        totals = jax.tree.map(lambda running, addend: running + addend, totals, weight_grads)
        return (totals, (output, grad_input))
    zeros_start = jax.tree.map(jnp.zeros_like, params)
    totals, (outputs, grad_inputs) = lax.scan(scan_step, zeros_start, (inputs, segment_groups, cotangent_groups))
    qkv_next, qkv_state = adam_update(qkv_weight, totals[0], qkv_moments, RATE_MATRIX)
    out_next, out_state = adam_update(out_weight, totals[1], out_moments, RATE_MATRIX)
    in_next, in_state = adam_update(in_weight, totals[2], in_moments, RATE_MATRIX)
    back_next, back_state = adam_update(back_weight, totals[3], back_moments, RATE_MATRIX)
    vector_next, vector_state = adam_update(vectors, totals[4], vector_moments, RATE_VECTOR)
    return (outputs.reshape(TOKENS, D).astype(jnp.bfloat16), grad_inputs.reshape(TOKENS, D), totals[0], totals[1], totals[2], totals[3], totals[4], qkv_next, out_next, in_next, back_next, vector_next, qkv_state, out_state, in_state, back_state, vector_state)
```

```python
import jax
import jax.numpy as jnp
from jax import lax
from jax.experimental import pallas as pl
from jax.experimental.pallas import tpu as pltpu
from jax.sharding import PartitionSpec as P

HEADS = 12
HEAD_DIM = 64
LAYERS = 2
STEP = 3
ROW = 128
LANES = 128

EPSILON = 1e-05
NEGATIVE = -1000000000.0
BETA_FIRST = 0.5
BETA_SECOND = 0.5
WEIGHT_DECAY = 0.01
ADAM_EPSILON = 1e-08
RATE_MATRIX = 0.06
RATE_VECTOR = 0.5
MESH_ID = pl.DeviceIdType.MESH
BF16 = jnp.bfloat16
F32 = jnp.float32


class Place:
    def __init__(self):
        f = lax.axis_index("fsdp")
        z = lax.axis_index("dp")
        core = lax.rem(f, 2)
        x = lax.rem(lax.div(f, 2), 2)
        y = lax.div(f, 4)
        self.f, self.z, self.core, self.x, self.y = f, z, core, x, y
        self.fc = f + 1 - 2 * core
        self.fx = f + 2 - 4 * x
        self.fy = f + 4 - 8 * y
        self.fd = self.fx + 4 - 8 * y
        self.q = lax.rem(z, 2)
        self.to_c = {"fsdp": self.fc}
        self.to_x = {"fsdp": self.fx}
        self.to_y = {"fsdp": self.fy}
        self.to_z = {"dp": z + 1 - 2 * self.q}


def greet(partners):
    barrier = pltpu.get_barrier_semaphore()
    for partner in partners:
        pl.semaphore_signal(barrier, inc=1, device_id=partner, device_id_type=MESH_ID)
    pl.semaphore_wait(barrier, len(partners))


def norm_rows(values, gain_row, shift_row):
    centered = values - jnp.mean(values, axis=-1, keepdims=True)
    inverse = lax.rsqrt(jnp.mean(centered * centered, axis=-1, keepdims=True) + EPSILON)
    scaled = centered * inverse
    return scaled * gain_row + shift_row, scaled, inverse


def gelu_pair(value):
    cdf = 0.5 * (1.0 + lax.erf(value * 0.7071067811865476))
    slope = cdf + value * (0.3989422804014327 * jnp.exp(-0.5 * value * value))
    return value * cdf, slope


COPY_KINDS = 15
VEC_KINDS = 7


def forward_kernel(
    tok_ref, seg_ref, vec_ref, own_q, own_o, own_i, own_b,
    act_out, wq_out, wo_out, wi_out, wb_out, vec_out,
    joined_out, att_out, xh1_out, r1_out, flow_out, active_out, slope_out, xh2_out, r2_out, hlow_out,
    wq0, wo0, wi0, wb0, wq1, wo1, wi1, wb1, vslots, vec,
    hid, hlow, joined, att, first, xh1, r1, flow, active, slope, xh2, r2, mask,
    send_sem, recv_sem, own_sem, wout_sem, save_sem,
):
    here = Place()
    owns = (own_q, own_o, own_i, own_b)
    bufs = ((wq0, wo0, wi0, wb0), (wq1, wo1, wi1, wb1))
    wouts = (wq_out, wo_out, wi_out, wb_out)
    f, fx, fy, fd = here.f, here.fx, here.fy, here.fd
    greet((here.to_c, here.to_x, here.to_y, here.to_z))

    started = []

    def make(p, kind):
        layer, kind_at = divmod(p, 4)
        own, buf = owns[kind_at].at[layer], bufs[layer][kind_at]
        rows, cols = own.shape
        third = cols // 3
        c_xy = pl.multiple_of(here.q * third, LANES)
        c_b = pl.multiple_of(c_xy + third, LANES)
        c_z = pl.multiple_of(here.q * (2 * third), LANES)
        c_w = pl.multiple_of((1 - here.q) * (2 * third), LANES)

        def win(owner, col, width):
            return buf.at[pl.ds(pl.multiple_of(owner * rows, 32), rows), pl.ds(col, width)]

        two = 2 * third
        table = {
            0: (own, win(f, 0, cols), here.to_c),
            1: (own.at[:, pl.ds(c_xy, two)], win(f, c_xy, two), here.to_x),
            2: (own.at[:, pl.ds(c_xy, two)], win(f, c_xy, two), here.to_y),
            3: (win(fx, c_xy, two), win(fx, c_xy, two), here.to_c),
            4: (win(fx, c_xy, third), win(fx, c_xy, third), here.to_y),
            5: (win(fx, c_z, third), win(fx, c_z, third), here.to_z),
            6: (win(fy, c_xy, two), win(fy, c_xy, two), here.to_c),
            7: (win(fy, c_b, third), win(fy, c_b, third), here.to_x),
            8: (win(fy, c_z, third), win(fy, c_z, third), here.to_z),
            9: (win(fd, c_xy, third), win(fd, c_xy, third), here.to_c),
            10: (win(fd, c_b, third), win(fd, c_b, third), here.to_c),
            11: (win(fd, c_z, third), win(fd, c_z, third), here.to_z),
            12: (win(fx, c_w, third), win(fx, c_w, third), here.to_c),
            13: (win(fy, c_w, third), win(fy, c_w, third), here.to_c),
            14: (win(fd, c_w, third), win(fd, c_w, third), here.to_c),
        }
        src, dst, dev = table[kind]
        slot = p * COPY_KINDS + kind
        return pltpu.make_async_remote_copy(
            src_ref=src, dst_ref=dst, send_sem=send_sem.at[slot], recv_sem=recv_sem.at[slot],
            device_id=dev, device_id_type=MESH_ID,
        )

    copies = {}

    def start(p, *kinds):
        for kind in kinds:
            copy = make(p, kind)
            copy.start()
            copies[p, kind] = copy
            started.append(copy)

    def arrived(p, *kinds):
        for kind in kinds:
            copies[p, kind].wait_recv()

    def local_own(p):
        layer, kind_at = divmod(p, 4)
        own, buf = owns[kind_at].at[layer], bufs[layer][kind_at]
        rows = own.shape[0]
        return pltpu.make_async_copy(
            own, buf.at[pl.ds(pl.multiple_of(f * rows, 32), rows)], own_sem.at[p]
        )

    def send_own(p):
        if p < 8:
            start(p, 1, 2, 0)
            local_own(p).start()

    def stage_one(p):
        if p < 8:
            arrived(p, 1, 2)
            start(p, 4, 7, 5, 8, 3, 6)

    def stage_two(p):
        arrived(p, 4, 7)
        start(p, 11, 9, 10)

    def stage_three(p):
        arrived(p, 5, 8, 11)
        start(p, 12, 13, 14)

    wcopies = []

    def stage_four(p):
        layer, kind_at = divmod(p, 4)
        local_own(p).wait()
        arrived(p, 0, 3, 6, 9, 10, 12, 13, 14)
        copy = pltpu.make_async_copy(bufs[layer][kind_at], wouts[kind_at].at[layer], wout_sem.at[p])
        copy.start()
        wcopies.append(copy)

    def advance(p):
        stage_one(p + 1)
        send_own(p + 3)
        stage_two(p)
        stage_three(p)
        stage_four(p)

    vslots[pl.ds(f, 1)] = vec_ref[...][None]

    def vcopy(kind):
        owner, dev = {
            0: (f, here.to_x), 1: (f, here.to_y), 2: (f, here.to_c),
            3: (fx, here.to_y), 4: (fx, here.to_c), 5: (fy, here.to_c), 6: (fd, here.to_c),
        }[kind]
        slot = 8 * COPY_KINDS + kind
        return pltpu.make_async_remote_copy(
            src_ref=vslots.at[owner], dst_ref=vslots.at[owner], send_sem=send_sem.at[slot],
            recv_sem=recv_sem.at[slot], device_id=dev, device_id_type=MESH_ID,
        )

    vc = [vcopy(kind) for kind in range(VEC_KINDS)]
    started.extend(vc)
    for kind in (0, 1, 2):
        vc[kind].start()
    send_own(0)
    send_own(1)
    send_own(2)

    rows_here = seg_ref.shape[0]
    for r in range(rows_here):
        wide = jnp.broadcast_to(seg_ref[r : r + 1, :].astype(F32), (ROW, ROW))
        mask[r] = jnp.where(wide == wide.T, 1.0, 0.0)

    vc[0].wait_recv()
    vc[1].wait_recv()
    for kind in (3, 4, 5):
        vc[kind].start()
    vc[3].wait_recv()
    vc[6].start()
    for kind in (2, 4, 5, 6):
        vc[kind].wait_recv()
    width = vec.shape[1]
    share = width // 8
    lane = lax.broadcasted_iota(jnp.int32, (LANES, width), 0)
    column = lax.broadcasted_iota(jnp.int32, (LANES, width), 1)
    whole = jnp.zeros(vec.shape, F32)
    for owner in range(8):
        pick = (column == lane + owner * share) & (lane < share)
        whole = whole + jnp.dot(
            vslots[owner], jnp.where(pick, 1.0, 0.0).astype(BF16), preferred_element_type=F32
        )
    vec[...] = whole

    tokens = hid.shape[0]
    saves = {}

    def save(layer, at, src, dst):
        copy = pltpu.make_async_copy(src, dst, save_sem.at[layer, at])
        copy.start()
        saves[layer, at] = copy

    def saved(layer, *ats):
        if layer >= 0:
            for at in ats:
                saves[layer, at].wait()

    stage_one(0)
    half = tokens // 2
    for layer in range(LAYERS):
        wq, wo, wi, wb = bufs[layer]
        base = 12 * layer

        def row(at):
            return vec[base + at : base + at + 1, :]

        low_ref = tok_ref if layer == 0 else hlow
        advance(4 * layer)
        saved(layer - 1, 0)
        for part in range(3):
            bias = row(0) if part == 0 else row(1)

            def qkv_tile(n, carry, part=part, bias=bias):
                at = pl.multiple_of(n * half, half)
                acc = jnp.dot(
                    low_ref[pl.ds(at, half), :], wq[:, part * width : (part + 1) * width],
                    preferred_element_type=F32,
                )
                if part != 1:
                    acc = acc + bias
                joined[pl.ds(at, half), part * width : (part + 1) * width] = acc.astype(BF16)
                return carry

            lax.fori_loop(0, 2, qkv_tile, 0)
        save(layer, 0, joined, joined_out.at[layer])
        saved(layer - 1, 1)

        def attend(step, carry):
            r = lax.div(step, HEADS // 2)
            j = lax.rem(step, HEADS // 2)
            rows = pl.ds(pl.multiple_of(r * ROW, ROW), ROW)

            def cols(part):
                return pl.ds(pl.multiple_of(part * width + j * LANES, LANES), LANES)

            query, keys, value = (joined[rows, cols(part)] for part in range(3))
            first_head = lax.broadcasted_iota(jnp.int32, (ROW, LANES), 1) < HEAD_DIM
            nil = jnp.zeros_like(query)
            both = jnp.concatenate(
                [jnp.where(first_head, query, nil), jnp.where(first_head, nil, query)], axis=0
            )
            scores = lax.dot_general(
                both, keys, (((1,), (1,)), ((), ())), preferred_element_type=F32
            ) * HEAD_DIM ** (-0.5)
            seen = mask[pl.ds(r, 1)][0]
            scores = jnp.where(jnp.concatenate([seen, seen], axis=0) > 0.5, scores, NEGATIVE)
            top = jnp.max(scores, axis=-1, keepdims=True)
            grown = jnp.exp(scores - top)
            probs = grown / jnp.sum(grown, axis=-1, keepdims=True)
            mixed = jnp.dot(probs.astype(BF16), value, preferred_element_type=F32)
            att[rows, pl.ds(pl.multiple_of(j * LANES, LANES), LANES)] = jnp.where(
                first_head, mixed[:ROW], mixed[ROW:]
            ).astype(BF16)
            return carry

        lax.fori_loop(0, rows_here * (HEADS // 2), attend, 0)
        save(layer, 1, att, att_out.at[layer])
        advance(4 * layer + 1)
        saved(layer - 1, 2, 3, 4)

        def out_tile(n, carry):
            rows = pl.ds(pl.multiple_of(n * ROW, ROW), ROW)
            branch = jnp.dot(att[rows, :], wo[...], preferred_element_type=F32) + row(2)
            before = tok_ref[rows, :].astype(F32) if layer == 0 else hid[rows, :]
            normed, scaled, inverse = norm_rows(before + branch, row(3), row(4))
            first[rows, :] = normed
            flow[rows, :] = normed.astype(BF16)
            xh1[rows, :] = scaled
            r1[rows, :] = jnp.broadcast_to(inverse, (ROW, LANES))
            return carry

        lax.fori_loop(0, tokens // ROW, out_tile, 0)
        save(layer, 2, xh1, xh1_out.at[layer])
        save(layer, 3, r1, r1_out.at[layer])
        save(layer, 4, flow, flow_out.at[layer])
        advance(4 * layer + 2)
        saved(layer - 1, 5, 6)
        parts = wi.shape[1] // width
        tile = 256
        for part in range(parts):
            bias_row = row(5 + part)
            for sub in range(width // tile):
                bias = bias_row[:, sub * tile : (sub + 1) * tile]
                cols = slice(part * width + sub * tile, part * width + (sub + 1) * tile)

                def in_tile(n, carry, cols=cols, bias=bias):
                    rows = pl.ds(pl.multiple_of(n * half, half), half)
                    inner = jnp.dot(flow[rows, :], wi[:, cols], preferred_element_type=F32) + bias
                    value, change = gelu_pair(inner)
                    active[rows, cols] = value.astype(BF16)
                    slope[rows, cols] = change.astype(BF16)
                    return carry

                lax.fori_loop(0, 2, in_tile, 0)
        save(layer, 5, active, active_out.at[layer])
        save(layer, 6, slope, slope_out.at[layer])
        advance(4 * layer + 3)
        saved(layer - 1, 7, 8)

        def back_tile(n, carry):
            rows = pl.ds(pl.multiple_of(n * ROW, ROW), ROW)
            outer = jnp.dot(active[rows, :], wb[...], preferred_element_type=F32) + row(9)
            normed, scaled, inverse = norm_rows(first[rows, :] + outer, row(10), row(11))
            xh2[rows, :] = scaled
            r2[rows, :] = jnp.broadcast_to(inverse, (ROW, LANES))
            if layer == LAYERS - 1:
                act_out[rows, :] = normed.astype(BF16)
            else:
                hid[rows, :] = normed
                hlow[rows, :] = normed.astype(BF16)
            return carry

        lax.fori_loop(0, tokens // ROW, back_tile, 0)
        save(layer, 7, xh2, xh2_out.at[layer])
        save(layer, 8, r2, r2_out.at[layer])
        if layer == 0:
            save(layer, 9, hlow, hlow_out)
    vec_save = pltpu.make_async_copy(vec, vec_out, save_sem.at[1, 9])
    vec_save.start()
    for copy in started:
        copy.wait_send()
    for copy in wcopies:
        copy.wait()
    saved(0, 9)
    saved(1, *range(9))
    vec_save.wait()


def forward(tokens, segment_ids, vec_low, qkv_low, out_low, in_low, back_low):
    count, width = tokens.shape
    ff = in_low.shape[2]
    any_spec = pl.BlockSpec(memory_space=pltpu.HBM)
    vmem = pl.BlockSpec(memory_space=pltpu.VMEM)

    def shape(dims, kind):
        return jax.ShapeDtypeStruct(dims, kind)

    out_shape = (
        shape((count, width), BF16),
        shape((LAYERS, width, 3 * width), BF16),
        shape((LAYERS, width, width), BF16),
        shape((LAYERS, width, ff), BF16),
        shape((LAYERS, ff, width), BF16),
        shape((vec_low.shape[0], width), F32),
        shape((LAYERS, count, 3 * width), BF16),
        shape((LAYERS, count, width), BF16),
        shape((LAYERS, count, width), F32),
        shape((LAYERS, count, LANES), F32),
        shape((LAYERS, count, width), BF16),
        shape((LAYERS, count, ff), BF16),
        shape((LAYERS, count, ff), BF16),
        shape((LAYERS, count, width), F32),
        shape((LAYERS, count, LANES), F32),
        shape((count, width), BF16),
    )
    weights = [
        pltpu.VMEM((width, 3 * width), BF16), pltpu.VMEM((width, width), BF16),
        pltpu.VMEM((width, ff), BF16), pltpu.VMEM((ff, width), BF16),
    ]
    scratch = weights * LAYERS + [
        pltpu.VMEM((8,) + vec_low.shape, BF16),
        pltpu.VMEM((vec_low.shape[0], width), F32),
        pltpu.VMEM((count, width), F32),
        pltpu.VMEM((count, width), BF16),
        pltpu.VMEM((count, 3 * width), BF16),
        pltpu.VMEM((count, width), BF16),
        pltpu.VMEM((count, width), F32),
        pltpu.VMEM((count, width), F32),
        pltpu.VMEM((count, LANES), F32),
        pltpu.VMEM((count, width), BF16),
        pltpu.VMEM((count, ff), BF16),
        pltpu.VMEM((count, ff), BF16),
        pltpu.VMEM((count, width), F32),
        pltpu.VMEM((count, LANES), F32),
        pltpu.VMEM((segment_ids.shape[0], ROW, ROW), F32),
        pltpu.SemaphoreType.DMA((8 * COPY_KINDS + VEC_KINDS,)),
        pltpu.SemaphoreType.DMA((8 * COPY_KINDS + VEC_KINDS,)),
        pltpu.SemaphoreType.DMA((8,)),
        pltpu.SemaphoreType.DMA((8,)),
        pltpu.SemaphoreType.DMA((LAYERS, 10)),
    ]
    return pl.pallas_call(
        forward_kernel,
        name="forward",
        out_shape=out_shape,
        in_specs=[vmem, vmem, vmem] + [any_spec] * 4,
        out_specs=[vmem] + [any_spec] * (len(out_shape) - 1),
        scratch_shapes=scratch,
        compiler_params=pltpu.CompilerParams(
            collective_id=0, has_side_effects=True, vmem_limit_bytes=60 << 20
        ),
    )(tokens, segment_ids, vec_low, qkv_low, out_low, in_low, back_low)


def norm_forward(values, gain_row, shift_row):
    centered = values - jnp.mean(values, axis=-1, keepdims=True)
    inverse = lax.rsqrt(jnp.mean(centered * centered, axis=-1, keepdims=True) + EPSILON)
    scaled = centered * inverse
    return (scaled * gain_row + shift_row, scaled, inverse)


def norm_backward(grad_out, scaled, inverse, gain_row):
    grad_scaled = grad_out * gain_row
    grad_in = inverse * (
        grad_scaled
        - jnp.mean(grad_scaled, axis=-1, keepdims=True)
        - scaled * jnp.mean(grad_scaled * scaled, axis=-1, keepdims=True)
    )
    return (grad_in, jnp.sum(grad_out * scaled, axis=0), jnp.sum(grad_out, axis=0))


def score_block(queries, key_rows, same_segment):
    scores = jnp.einsum(
        "rqhe,rkhe->rhqk", queries, key_rows, preferred_element_type=jnp.float32
    ) * HEAD_DIM ** (-0.5)
    return jnp.where(same_segment, scores, NEGATIVE)


def layer_forward(hidden, same_segment, weights):
    qkv_used, out_used, in_used, back_used, vector_low = weights
    vector = vector_low.astype(jnp.float32)
    row_count = same_segment.shape[0]
    model_width = out_used.shape[0]
    hidden_low = hidden.astype(jnp.bfloat16)
    bias_qkv = jnp.concatenate([vector[0], jnp.zeros_like(vector[0]), vector[1]])
    joined = (jnp.dot(hidden_low, qkv_used, preferred_element_type=jnp.float32) + bias_qkv).astype(
        jnp.bfloat16
    )
    split_qkv = joined.reshape(row_count, -1, 3, HEADS, HEAD_DIM)
    scores = score_block(split_qkv[:, :, 0], split_qkv[:, :, 1], same_segment)
    row_top = jnp.max(scores, axis=-1, keepdims=True)
    log_total = row_top + jnp.log(jnp.sum(jnp.exp(scores - row_top), axis=-1, keepdims=True))
    prob_low = jnp.exp(scores - log_total).astype(jnp.bfloat16)
    attended = jnp.einsum(
        "rhqk,rkhe->rqhe", prob_low, split_qkv[:, :, 2], preferred_element_type=jnp.float32
    )
    attended_low = attended.reshape(-1, model_width).astype(jnp.bfloat16)
    branch = jnp.dot(attended_low, out_used, preferred_element_type=jnp.float32) + vector[2]
    first_norm, scaled_one, inverse_one = norm_forward(hidden + branch, vector[3], vector[4])
    first_low = first_norm.astype(jnp.bfloat16)
    inner_pre = jnp.dot(first_low, in_used, preferred_element_type=jnp.float32) + vector[
        5:9
    ].reshape(-1)
    active_low = jax.nn.gelu(inner_pre, approximate=False).astype(jnp.bfloat16)
    outer_out = jnp.dot(active_low, back_used, preferred_element_type=jnp.float32) + vector[9]
    output, scaled_two, inverse_two = norm_forward(first_norm + outer_out, vector[10], vector[11])
    kept_state = (
        hidden_low,
        joined,
        log_total,
        attended_low,
        scaled_one,
        inverse_one,
        first_low,
        inner_pre,
        active_low,
        scaled_two,
        inverse_two,
    )
    return (output, kept_state)


def layer_backward(grad_out, same_segment, weights, kept_state):
    qkv_used, out_used, in_used, back_used, vector_low = weights
    vector = vector_low.astype(jnp.float32)
    (
        hidden_low,
        joined,
        log_total,
        attended_low,
        scaled_one,
        inverse_one,
        first_low,
        inner_pre,
        active_low,
        scaled_two,
        inverse_two,
    ) = kept_state
    row_count = same_segment.shape[0]
    model_width = out_used.shape[0]
    grad_two, gain_two_grad, shift_two_grad = norm_backward(
        grad_out, scaled_two, inverse_two, vector[10]
    )
    grad_outer = grad_two.astype(jnp.bfloat16)
    back_bias_grad = jnp.sum(grad_two, axis=0)
    back_weight_grad = jnp.einsum(
        "tf,td->fd", active_low, grad_outer, preferred_element_type=jnp.float32
    )
    grad_active = jnp.einsum("td,fd->tf", grad_outer, back_used, preferred_element_type=jnp.float32)
    if inner_pre.dtype == BF16:
        grad_inner = (grad_active * inner_pre.astype(F32)).astype(BF16)
    else:
        gelu_value, gelu_pull = jax.vjp(
            lambda values: jax.nn.gelu(values, approximate=False), inner_pre
        )
        grad_inner = gelu_pull(grad_active)[0].astype(jnp.bfloat16)
    in_bias_grad = jnp.sum(grad_inner, axis=0, dtype=jnp.float32)
    in_weight_grad = jnp.einsum(
        "td,tf->df", first_low, grad_inner, preferred_element_type=jnp.float32
    )
    grad_first = grad_two + jnp.einsum(
        "tf,df->td", grad_inner, in_used, preferred_element_type=jnp.float32
    )
    grad_one, gain_one_grad, shift_one_grad = norm_backward(
        grad_first, scaled_one, inverse_one, vector[3]
    )
    grad_branch = grad_one.astype(jnp.bfloat16)
    out_bias_grad = jnp.sum(grad_one, axis=0)
    out_weight_grad = jnp.einsum(
        "td,te->de", attended_low, grad_branch, preferred_element_type=jnp.float32
    )
    grad_mixed = jnp.einsum("te,de->td", grad_branch, out_used, preferred_element_type=jnp.float32)
    grad_mixed = grad_mixed.astype(jnp.bfloat16).reshape(row_count, -1, HEADS, HEAD_DIM)
    split_qkv = joined.reshape(row_count, -1, 3, HEADS, HEAD_DIM)
    queries = split_qkv[:, :, 0]
    key_rows = split_qkv[:, :, 1]
    value_rows = split_qkv[:, :, 2]
    prob_full = jnp.exp(score_block(queries, key_rows, same_segment) - log_total)
    prob_low = prob_full.astype(jnp.bfloat16)
    grad_values = jnp.einsum(
        "rhqk,rqhe->rkhe", prob_low, grad_mixed, preferred_element_type=jnp.float32
    )
    grad_probs = jnp.einsum(
        "rqhe,rkhe->rhqk", grad_mixed, value_rows, preferred_element_type=jnp.float32
    )
    centred = jnp.sum(prob_full * grad_probs, axis=-1, keepdims=True)
    grad_scores = (prob_full * (grad_probs - centred)).astype(jnp.bfloat16)
    grad_queries = jnp.einsum(
        "rhqk,rkhe->rqhe", grad_scores, key_rows, preferred_element_type=jnp.float32
    ) * HEAD_DIM ** (-0.5)
    grad_keys = jnp.einsum(
        "rhqk,rqhe->rkhe", grad_scores, queries, preferred_element_type=jnp.float32
    ) * HEAD_DIM ** (-0.5)
    grad_joined = (
        jnp.stack([grad_queries, grad_keys, grad_values], axis=2)
        .reshape(-1, 3 * model_width)
        .astype(jnp.bfloat16)
    )
    qkv_bias_grad = jnp.sum(grad_joined, axis=0, dtype=jnp.float32)
    qkv_weight_grad = jnp.einsum(
        "td,tc->dc", hidden_low, grad_joined, preferred_element_type=jnp.float32
    )
    grad_hidden = grad_one + jnp.einsum(
        "tc,dc->td", grad_joined, qkv_used, preferred_element_type=jnp.float32
    )
    vector_grad = jnp.concatenate(
        [
            qkv_bias_grad[:model_width][None],
            qkv_bias_grad[2 * model_width :][None],
            out_bias_grad[None],
            gain_one_grad[None],
            shift_one_grad[None],
            in_bias_grad.reshape(4, model_width),
            back_bias_grad[None],
            gain_two_grad[None],
            shift_two_grad[None],
        ],
        axis=0,
    )
    return (
        grad_hidden,
        (qkv_weight_grad, out_weight_grad, in_weight_grad, back_weight_grad, vector_grad),
    )


def adam_step(weight, gradient, moment_one, moment_two, step_rate):
    first_moment = BETA_FIRST * moment_one + (1.0 - BETA_FIRST) * gradient
    second_moment = BETA_SECOND * moment_two + (1.0 - BETA_SECOND) * gradient * gradient
    first_hat = first_moment / (1.0 - BETA_FIRST**STEP)
    second_hat = second_moment / (1.0 - BETA_SECOND**STEP)
    updated = weight - step_rate * (
        first_hat / (jnp.sqrt(second_hat) + ADAM_EPSILON) + WEIGHT_DECAY * weight
    )
    return jnp.stack([gradient, updated, second_moment])


def update_layer(summed, masters, moments, layer_at):
    outcome = []
    for kind_at in range(5):
        step_rate = RATE_VECTOR if kind_at == 4 else RATE_MATRIX
        outcome.append(
            adam_step(
                masters[kind_at][layer_at],
                summed[kind_at],
                moments[kind_at][0, layer_at],
                moments[kind_at][1, layer_at],
                step_rate,
            )
        )
    return outcome


def local_parts(masters, layer_at):
    return tuple((master[layer_at].astype(jnp.bfloat16) for master in masters))


def collect(results, kind_at, member):
    return jnp.stack([layer_result[kind_at][member] for layer_result in results])


def on_device_any(
    tokens,
    segment_ids,
    cotangent,
    qkv_weight,
    out_weight,
    in_weight,
    back_weight,
    vectors,
    qkv_moments,
    out_moments,
    in_moments,
    back_moments,
    vector_moments,
):
    masters = (qkv_weight, out_weight, in_weight, back_weight, vectors)
    moments = (qkv_moments, out_moments, in_moments, back_moments, vector_moments)
    same_segment = (segment_ids[:, :, None] == segment_ids[:, None, :])[:, None]
    hidden = tokens.astype(jnp.float32)
    saved_states = []
    for layer_at in range(LAYERS):
        parts_now = local_parts(masters, layer_at)
        weights = (
            lax.all_gather(parts_now[0], "fsdp", axis=0, tiled=True),
            lax.all_gather(parts_now[1], "fsdp", axis=0, tiled=True),
            lax.all_gather(parts_now[2], "fsdp", axis=0, tiled=True),
            lax.all_gather(parts_now[3], "fsdp", axis=0, tiled=True),
            lax.all_gather(parts_now[4], "fsdp", axis=1, tiled=True),
        )
        hidden, kept_state = layer_forward(hidden, same_segment, weights)
        saved_states.append(kept_state)
    activations = hidden.astype(jnp.bfloat16)
    grad_hidden = cotangent.astype(jnp.float32)
    results = [None] * LAYERS
    for layer_at in reversed(range(LAYERS)):
        parts_now = local_parts(masters, layer_at)
        weights = (
            lax.all_gather(parts_now[0], "fsdp", axis=0, tiled=True),
            lax.all_gather(parts_now[1], "fsdp", axis=0, tiled=True),
            lax.all_gather(parts_now[2], "fsdp", axis=0, tiled=True),
            lax.all_gather(parts_now[3], "fsdp", axis=0, tiled=True),
            lax.all_gather(parts_now[4], "fsdp", axis=1, tiled=True),
        )
        grad_hidden, weight_grads = layer_backward(
            grad_hidden, same_segment, weights, saved_states[layer_at]
        )
        shards = (
            lax.psum_scatter(
                weight_grads[0].astype(jnp.bfloat16), "fsdp", scatter_dimension=0, tiled=True
            ).astype(jnp.float32),
            lax.psum_scatter(
                weight_grads[1].astype(jnp.bfloat16), "fsdp", scatter_dimension=0, tiled=True
            ).astype(jnp.float32),
            lax.psum_scatter(
                weight_grads[2].astype(jnp.bfloat16), "fsdp", scatter_dimension=0, tiled=True
            ).astype(jnp.float32),
            lax.psum_scatter(
                weight_grads[3].astype(jnp.bfloat16), "fsdp", scatter_dimension=0, tiled=True
            ).astype(jnp.float32),
            lax.psum_scatter(
                weight_grads[4].astype(jnp.bfloat16), "fsdp", scatter_dimension=1, tiled=True
            ).astype(jnp.float32),
        )
        totals = (
            lax.psum(shards[0].astype(jnp.bfloat16), "dp").astype(jnp.float32),
            lax.psum(shards[1].astype(jnp.bfloat16), "dp").astype(jnp.float32),
            lax.psum(shards[2].astype(jnp.bfloat16), "dp").astype(jnp.float32),
            lax.psum(shards[3].astype(jnp.bfloat16), "dp").astype(jnp.float32),
            lax.psum(shards[4].astype(jnp.bfloat16), "dp").astype(jnp.float32),
        )
        results[layer_at] = update_layer(totals, masters, moments, layer_at)
    return (
        activations,
        grad_hidden,
        collect(results, 0, 0),
        collect(results, 1, 0),
        collect(results, 2, 0),
        collect(results, 3, 0),
        collect(results, 4, 0),
        collect(results, 0, 1),
        collect(results, 1, 1),
        collect(results, 2, 1),
        collect(results, 3, 1),
        collect(results, 4, 1),
        collect(results, 0, 2),
        collect(results, 1, 2),
        collect(results, 2, 2),
        collect(results, 3, 2),
        collect(results, 4, 2),
    )


def split_heads(joined, rows):
    return joined.reshape(rows, -1, 3, HEADS, HEAD_DIM)


def on_device(
    tokens,
    segment_ids,
    cotangent,
    qkv_weight,
    out_weight,
    in_weight,
    back_weight,
    vectors,
    qkv_moments,
    out_moments,
    in_moments,
    back_moments,
    vector_moments,
):
    masters = (qkv_weight, out_weight, in_weight, back_weight, vectors)
    moments = (qkv_moments, out_moments, in_moments, back_moments, vector_moments)
    same_segment = (segment_ids[:, :, None] == segment_ids[:, None, :])[:, None]
    share = vectors.shape[2]
    vec_low = jnp.pad(vectors.reshape(-1, share), ((0, 8), (0, LANES - share))).astype(BF16)
    (
        activations, wq, wo, wi, wb, vec,
        joined, att, xh1, r1, flow, active, slope, xh2, r2, hlow,
    ) = forward(
        tokens, segment_ids, vec_low, qkv_weight.astype(BF16), out_weight.astype(BF16),
        in_weight.astype(BF16), back_weight.astype(BF16),
    )
    grad_hidden = cotangent.astype(jnp.float32)
    results = [None] * LAYERS
    rows = segment_ids.shape[0]
    for layer_at in reversed(range(LAYERS)):
        split_qkv = split_heads(joined[layer_at], rows)
        scores = score_block(split_qkv[:, :, 0], split_qkv[:, :, 1], same_segment)
        row_top = jnp.max(scores, axis=-1, keepdims=True)
        log_total = row_top + jnp.log(jnp.sum(jnp.exp(scores - row_top), axis=-1, keepdims=True))
        kept = (
            tokens if layer_at == 0 else hlow, joined[layer_at], log_total, att[layer_at],
            xh1[layer_at], r1[layer_at][:, :1], flow[layer_at], slope[layer_at], active[layer_at],
            xh2[layer_at], r2[layer_at][:, :1],
        )
        weights = (
            wq[layer_at], wo[layer_at], wi[layer_at], wb[layer_at],
            vec[12 * layer_at : 12 * layer_at + 12],
        )
        grad_hidden, weight_grads = layer_backward(grad_hidden, same_segment, weights, kept)
        shards = (
            lax.psum_scatter(
                weight_grads[0].astype(jnp.bfloat16), "fsdp", scatter_dimension=0, tiled=True
            ).astype(jnp.float32),
            lax.psum_scatter(
                weight_grads[1].astype(jnp.bfloat16), "fsdp", scatter_dimension=0, tiled=True
            ).astype(jnp.float32),
            lax.psum_scatter(
                weight_grads[2].astype(jnp.bfloat16), "fsdp", scatter_dimension=0, tiled=True
            ).astype(jnp.float32),
            lax.psum_scatter(
                weight_grads[3].astype(jnp.bfloat16), "fsdp", scatter_dimension=0, tiled=True
            ).astype(jnp.float32),
            lax.psum_scatter(
                weight_grads[4].astype(jnp.bfloat16), "fsdp", scatter_dimension=1, tiled=True
            ).astype(jnp.float32),
        )
        totals = (
            lax.psum(shards[0].astype(jnp.bfloat16), "dp").astype(jnp.float32),
            lax.psum(shards[1].astype(jnp.bfloat16), "dp").astype(jnp.float32),
            lax.psum(shards[2].astype(jnp.bfloat16), "dp").astype(jnp.float32),
            lax.psum(shards[3].astype(jnp.bfloat16), "dp").astype(jnp.float32),
            lax.psum(shards[4].astype(jnp.bfloat16), "dp").astype(jnp.float32),
        )
        results[layer_at] = update_layer(totals, masters, moments, layer_at)
    return (
        activations,
        grad_hidden,
        collect(results, 0, 0),
        collect(results, 1, 0),
        collect(results, 2, 0),
        collect(results, 3, 0),
        collect(results, 4, 0),
        collect(results, 0, 1),
        collect(results, 1, 1),
        collect(results, 2, 1),
        collect(results, 3, 1),
        collect(results, 4, 1),
        collect(results, 0, 2),
        collect(results, 1, 2),
        collect(results, 2, 2),
        collect(results, 3, 2),
        collect(results, 4, 2),
    )


def solution(mesh):
    in_specs = (
        P(("fsdp", "dp"), None),
        P(("fsdp", "dp"), None),
        P(("fsdp", "dp"), None),
        P(None, "fsdp", None),
        P(None, "fsdp", None),
        P(None, "fsdp", None),
        P(None, "fsdp", None),
        P(None, None, "fsdp"),
        P(None, None, "fsdp", None),
        P(None, None, "fsdp", None),
        P(None, None, "fsdp", None),
        P(None, None, "fsdp", None),
        P(None, None, None, "fsdp"),
    )
    out_specs = (
        P(("fsdp", "dp"), None),
        P(("fsdp", "dp"), None),
        P(None, "fsdp", None),
        P(None, "fsdp", None),
        P(None, "fsdp", None),
        P(None, "fsdp", None),
        P(None, None, "fsdp"),
        P(None, "fsdp", None),
        P(None, "fsdp", None),
        P(None, "fsdp", None),
        P(None, "fsdp", None),
        P(None, None, "fsdp"),
        P(None, "fsdp", None),
        P(None, "fsdp", None),
        P(None, "fsdp", None),
        P(None, "fsdp", None),
        P(None, None, "fsdp"),
    )
    body = on_device if dict(mesh.shape) == {"fsdp": 8, "dp": 4} else on_device_any
    return jax.shard_map(
        body, mesh=mesh, in_specs=in_specs, out_specs=out_specs, check_vma=False
    )
```

```python
import jax
import jax.numpy as jnp
from jax import lax
from jax.experimental import pallas as pl
from jax.experimental.pallas import tpu as pltpu
from jax.sharding import PartitionSpec as P

HEADS = 12
HEAD_DIM = 64
LAYERS = 2
STEP = 3
ROW = 128
LANES = 128

EPSILON = 1e-05
NEGATIVE = -1000000000.0
BETA_FIRST = 0.5
BETA_SECOND = 0.5
WEIGHT_DECAY = 0.01
ADAM_EPSILON = 1e-08
RATE_MATRIX = 0.06
RATE_VECTOR = 0.5
MESH_ID = pl.DeviceIdType.MESH
BF16 = jnp.bfloat16
F32 = jnp.float32


class Place:
    def __init__(self):
        f = lax.axis_index("fsdp")
        z = lax.axis_index("dp")
        core = lax.rem(f, 2)
        x = lax.rem(lax.div(f, 2), 2)
        y = lax.div(f, 4)
        self.f, self.z, self.core, self.x, self.y = f, z, core, x, y
        self.fc = f + 1 - 2 * core
        self.fx = f + 2 - 4 * x
        self.fy = f + 4 - 8 * y
        self.fd = self.fx + 4 - 8 * y
        self.q = lax.rem(z, 2)
        self.to_c = {"fsdp": self.fc}
        self.to_x = {"fsdp": self.fx}
        self.to_y = {"fsdp": self.fy}
        self.to_z = {"dp": z + 1 - 2 * self.q}


def greet(partners):
    barrier = pltpu.get_barrier_semaphore()
    for partner in partners:
        pl.semaphore_signal(barrier, inc=1, device_id=partner, device_id_type=MESH_ID)
    pl.semaphore_wait(barrier, len(partners))


def norm_rows(values, gain_row, shift_row):
    centered = values - jnp.mean(values, axis=-1, keepdims=True)
    inverse = lax.rsqrt(jnp.mean(centered * centered, axis=-1, keepdims=True) + EPSILON)
    scaled = centered * inverse
    return scaled * gain_row + shift_row, scaled, inverse


def gelu_pair(value):
    cdf = 0.5 * (1.0 + lax.erf(value * 0.7071067811865476))
    slope = cdf + value * (0.3989422804014327 * jnp.exp(-0.5 * value * value))
    return value * cdf, slope


COPY_KINDS = 15
VEC_KINDS = 7


def forward_kernel(
    tok_ref, seg_ref, vec_ref, own_q, own_o, own_i, own_b,
    act_out, wq_out, wo_out, wi_out, wb_out, vec_out,
    joined_out, att_out, xh1_out, r1_out, flow_out, active_out, slope_out, xh2_out, r2_out, hlow_out,
    wq0, wo0, wi0, wb0, wq1, wo1, wi1, wb1, vslots, vec,
    hid, hlow, joined, att, first, xh1, r1, flow, active, slope, xh2, r2, mask,
    send_sem, recv_sem, own_sem, wout_sem, save_sem,
):
    here = Place()
    owns = (own_q, own_o, own_i, own_b)
    bufs = ((wq0, wo0, wi0, wb0), (wq1, wo1, wi1, wb1))
    wouts = (wq_out, wo_out, wi_out, wb_out)
    f, fx, fy, fd = here.f, here.fx, here.fy, here.fd
    greet((here.to_c, here.to_x, here.to_y, here.to_z))

    started = []

    def make(p, kind):
        layer, kind_at = divmod(p, 4)
        own, buf = owns[kind_at].at[layer], bufs[layer][kind_at]
        rows, cols = own.shape
        third = cols // 3
        c_xy = pl.multiple_of(here.q * third, LANES)
        c_b = pl.multiple_of(c_xy + third, LANES)
        c_z = pl.multiple_of(here.q * (2 * third), LANES)
        c_w = pl.multiple_of((1 - here.q) * (2 * third), LANES)

        def win(owner, col, width):
            return buf.at[pl.ds(pl.multiple_of(owner * rows, 32), rows), pl.ds(col, width)]

        two = 2 * third
        table = {
            0: (own, win(f, 0, cols), here.to_c),
            1: (own.at[:, pl.ds(c_xy, two)], win(f, c_xy, two), here.to_x),
            2: (own.at[:, pl.ds(c_xy, two)], win(f, c_xy, two), here.to_y),
            3: (win(fx, c_xy, two), win(fx, c_xy, two), here.to_c),
            4: (win(fx, c_xy, third), win(fx, c_xy, third), here.to_y),
            5: (win(fx, c_z, third), win(fx, c_z, third), here.to_z),
            6: (win(fy, c_xy, two), win(fy, c_xy, two), here.to_c),
            7: (win(fy, c_b, third), win(fy, c_b, third), here.to_x),
            8: (win(fy, c_z, third), win(fy, c_z, third), here.to_z),
            9: (win(fd, c_xy, third), win(fd, c_xy, third), here.to_c),
            10: (win(fd, c_b, third), win(fd, c_b, third), here.to_c),
            11: (win(fd, c_z, third), win(fd, c_z, third), here.to_z),
            12: (win(fx, c_w, third), win(fx, c_w, third), here.to_c),
            13: (win(fy, c_w, third), win(fy, c_w, third), here.to_c),
            14: (win(fd, c_w, third), win(fd, c_w, third), here.to_c),
        }
        src, dst, dev = table[kind]
        slot = p * COPY_KINDS + kind
        return pltpu.make_async_remote_copy(
            src_ref=src, dst_ref=dst, send_sem=send_sem.at[slot], recv_sem=recv_sem.at[slot],
            device_id=dev, device_id_type=MESH_ID,
        )

    copies = {}

    def start(p, *kinds):
        for kind in kinds:
            copy = make(p, kind)
            copy.start()
            copies[p, kind] = copy
            started.append(copy)

    def arrived(p, *kinds):
        for kind in kinds:
            copies[p, kind].wait_recv()

    def local_own(p):
        layer, kind_at = divmod(p, 4)
        own, buf = owns[kind_at].at[layer], bufs[layer][kind_at]
        rows = own.shape[0]
        return pltpu.make_async_copy(
            own, buf.at[pl.ds(pl.multiple_of(f * rows, 32), rows)], own_sem.at[p]
        )

    def send_own(p):
        if p < 8:
            start(p, 1, 2, 0)
            local_own(p).start()

    def stage_one(p):
        if p < 8:
            arrived(p, 1, 2)
            start(p, 4, 7, 5, 8, 3, 6)

    def stage_two(p):
        if p < 8:
            arrived(p, 4, 7)
            start(p, 11, 9, 10)

    def stage_three(p):
        arrived(p, 5, 8, 11)
        start(p, 12, 13, 14)

    wcopies = []

    def stage_four(p):
        layer, kind_at = divmod(p, 4)
        local_own(p).wait()
        arrived(p, 0, 3, 6, 9, 10, 12, 13, 14)
        copy = pltpu.make_async_copy(bufs[layer][kind_at], wouts[kind_at].at[layer], wout_sem.at[p])
        copy.start()
        wcopies.append(copy)

    def advance(p):
        stage_one(p + 2)
        send_own(p + 4)
        stage_two(p + 1)
        stage_three(p)
        stage_four(p)

    vslots[pl.ds(f, 1)] = vec_ref[...][None]

    def vcopy(kind):
        owner, dev = {
            0: (f, here.to_x), 1: (f, here.to_y), 2: (f, here.to_c),
            3: (fx, here.to_y), 4: (fx, here.to_c), 5: (fy, here.to_c), 6: (fd, here.to_c),
        }[kind]
        slot = 8 * COPY_KINDS + kind
        return pltpu.make_async_remote_copy(
            src_ref=vslots.at[owner], dst_ref=vslots.at[owner], send_sem=send_sem.at[slot],
            recv_sem=recv_sem.at[slot], device_id=dev, device_id_type=MESH_ID,
        )

    vc = [vcopy(kind) for kind in range(VEC_KINDS)]
    started.extend(vc)
    for kind in (0, 1, 2):
        vc[kind].start()
    send_own(0)
    send_own(1)
    send_own(2)

    rows_here = seg_ref.shape[0]
    for r in range(rows_here):
        wide = jnp.broadcast_to(seg_ref[r : r + 1, :].astype(F32), (ROW, ROW))
        mask[r] = jnp.where(wide == wide.T, 1.0, 0.0)

    vc[0].wait_recv()
    vc[1].wait_recv()
    for kind in (3, 4, 5):
        vc[kind].start()
    vc[3].wait_recv()
    vc[6].start()
    for kind in (2, 4, 5, 6):
        vc[kind].wait_recv()
    width = vec.shape[1]
    share = width // 8
    lane = lax.broadcasted_iota(jnp.int32, (LANES, width), 0)
    column = lax.broadcasted_iota(jnp.int32, (LANES, width), 1)
    whole = jnp.zeros(vec.shape, F32)
    for owner in range(8):
        pick = (column == lane + owner * share) & (lane < share)
        whole = whole + jnp.dot(
            vslots[owner], jnp.where(pick, 1.0, 0.0).astype(BF16), preferred_element_type=F32
        )
    vec[...] = whole

    tokens = hid.shape[0]
    saves = {}

    def save(layer, at, src, dst):
        copy = pltpu.make_async_copy(src, dst, save_sem.at[layer, at])
        copy.start()
        saves[layer, at] = copy

    def saved(layer, *ats):
        if layer >= 0:
            for at in ats:
                saves[layer, at].wait()

    stage_one(0)
    send_own(3)
    stage_one(1)
    stage_two(0)
    half = tokens // 2
    for layer in range(LAYERS):
        wq, wo, wi, wb = bufs[layer]
        base = 12 * layer

        def row(at):
            return vec[base + at : base + at + 1, :]

        low_ref = tok_ref if layer == 0 else hlow
        advance(4 * layer)
        saved(layer - 1, 0)
        for part in range(3):
            bias = row(0) if part == 0 else row(1)

            def qkv_tile(n, carry, part=part, bias=bias):
                at = pl.multiple_of(n * half, half)
                acc = jnp.dot(
                    low_ref[pl.ds(at, half), :], wq[:, part * width : (part + 1) * width],
                    preferred_element_type=F32,
                )
                if part != 1:
                    acc = acc + bias
                joined[pl.ds(at, half), part * width : (part + 1) * width] = acc.astype(BF16)
                return carry

            lax.fori_loop(0, 2, qkv_tile, 0)
        save(layer, 0, joined, joined_out.at[layer])
        saved(layer - 1, 1)

        def attend(r, carry):
            rows = pl.ds(pl.multiple_of(r * ROW, ROW), ROW)
            first_head = lax.broadcasted_iota(jnp.int32, (ROW, LANES), 1) < HEAD_DIM
            seen = mask[pl.ds(r, 1)][0]
            seen = jnp.concatenate([seen, seen], axis=0) > 0.5
            for j in range(HEADS // 2):
                query, keys, value = (
                    joined[rows, part * width + j * LANES : part * width + (j + 1) * LANES]
                    for part in range(3)
                )
                nil = jnp.zeros_like(query)
                both = jnp.concatenate(
                    [jnp.where(first_head, query, nil), jnp.where(first_head, nil, query)], axis=0
                )
                scores = lax.dot_general(
                    both, keys, (((1,), (1,)), ((), ())), preferred_element_type=F32
                ) * HEAD_DIM ** (-0.5)
                scores = jnp.where(seen, scores, NEGATIVE)
                top = jnp.max(scores, axis=-1, keepdims=True)
                grown = jnp.exp(scores - top)
                probs = grown * (1.0 / jnp.sum(grown, axis=-1, keepdims=True))
                mixed = jnp.dot(probs.astype(BF16), value, preferred_element_type=F32)
                att[rows, j * LANES : (j + 1) * LANES] = jnp.where(
                    first_head, mixed[:ROW], mixed[ROW:]
                ).astype(BF16)
            return carry

        lax.fori_loop(0, rows_here, attend, 0)
        save(layer, 1, att, att_out.at[layer])
        advance(4 * layer + 1)
        saved(layer - 1, 2, 3, 4)

        def out_tile(n, carry):
            rows = pl.ds(pl.multiple_of(n * ROW, ROW), ROW)
            branch = jnp.dot(att[rows, :], wo[...], preferred_element_type=F32) + row(2)
            before = tok_ref[rows, :].astype(F32) if layer == 0 else hid[rows, :]
            normed, scaled, inverse = norm_rows(before + branch, row(3), row(4))
            first[rows, :] = normed
            flow[rows, :] = normed.astype(BF16)
            xh1[rows, :] = scaled
            r1[rows, :] = jnp.broadcast_to(inverse, (ROW, LANES))
            return carry

        lax.fori_loop(0, tokens // ROW, out_tile, 0)
        save(layer, 2, xh1, xh1_out.at[layer])
        save(layer, 3, r1, r1_out.at[layer])
        save(layer, 4, flow, flow_out.at[layer])
        advance(4 * layer + 2)
        saved(layer - 1, 5, 6)
        parts = wi.shape[1] // width
        tile = 256
        for part in range(parts):
            bias_row = row(5 + part)
            for sub in range(width // tile):
                bias = bias_row[:, sub * tile : (sub + 1) * tile]
                cols = slice(part * width + sub * tile, part * width + (sub + 1) * tile)

                def in_tile(n, carry, cols=cols, bias=bias):
                    rows = pl.ds(pl.multiple_of(n * half, half), half)
                    inner = jnp.dot(flow[rows, :], wi[:, cols], preferred_element_type=F32) + bias
                    value, change = gelu_pair(inner)
                    active[rows, cols] = value.astype(BF16)
                    slope[rows, cols] = change.astype(BF16)
                    return carry

                lax.fori_loop(0, 2, in_tile, 0)
        save(layer, 5, active, active_out.at[layer])
        save(layer, 6, slope, slope_out.at[layer])
        advance(4 * layer + 3)
        saved(layer - 1, 7, 8)

        def back_tile(n, carry):
            rows = pl.ds(pl.multiple_of(n * ROW, ROW), ROW)
            outer = jnp.dot(active[rows, :], wb[...], preferred_element_type=F32) + row(9)
            normed, scaled, inverse = norm_rows(first[rows, :] + outer, row(10), row(11))
            xh2[rows, :] = scaled
            r2[rows, :] = jnp.broadcast_to(inverse, (ROW, LANES))
            if layer == LAYERS - 1:
                act_out[rows, :] = normed.astype(BF16)
            else:
                hid[rows, :] = normed
                hlow[rows, :] = normed.astype(BF16)
            return carry

        lax.fori_loop(0, tokens // ROW, back_tile, 0)
        save(layer, 7, xh2, xh2_out.at[layer])
        save(layer, 8, r2, r2_out.at[layer])
        if layer == 0:
            save(layer, 9, hlow, hlow_out)
    vec_save = pltpu.make_async_copy(vec, vec_out, save_sem.at[1, 9])
    vec_save.start()
    for copy in started:
        copy.wait_send()
    for copy in wcopies:
        copy.wait()
    saved(0, 9)
    saved(1, *range(9))
    vec_save.wait()


def forward(tokens, segment_ids, vec_low, qkv_low, out_low, in_low, back_low):
    count, width = tokens.shape
    ff = in_low.shape[2]
    any_spec = pl.BlockSpec(memory_space=pltpu.HBM)
    vmem = pl.BlockSpec(memory_space=pltpu.VMEM)

    def shape(dims, kind):
        return jax.ShapeDtypeStruct(dims, kind)

    out_shape = (
        shape((count, width), BF16),
        shape((LAYERS, width, 3 * width), BF16),
        shape((LAYERS, width, width), BF16),
        shape((LAYERS, width, ff), BF16),
        shape((LAYERS, ff, width), BF16),
        shape((vec_low.shape[0], width), F32),
        shape((LAYERS, count, 3 * width), BF16),
        shape((LAYERS, count, width), BF16),
        shape((LAYERS, count, width), F32),
        shape((LAYERS, count, LANES), F32),
        shape((LAYERS, count, width), BF16),
        shape((LAYERS, count, ff), BF16),
        shape((LAYERS, count, ff), BF16),
        shape((LAYERS, count, width), F32),
        shape((LAYERS, count, LANES), F32),
        shape((count, width), BF16),
    )
    weights = [
        pltpu.VMEM((width, 3 * width), BF16), pltpu.VMEM((width, width), BF16),
        pltpu.VMEM((width, ff), BF16), pltpu.VMEM((ff, width), BF16),
    ]
    scratch = weights * LAYERS + [
        pltpu.VMEM((8,) + vec_low.shape, BF16),
        pltpu.VMEM((vec_low.shape[0], width), F32),
        pltpu.VMEM((count, width), F32),
        pltpu.VMEM((count, width), BF16),
        pltpu.VMEM((count, 3 * width), BF16),
        pltpu.VMEM((count, width), BF16),
        pltpu.VMEM((count, width), F32),
        pltpu.VMEM((count, width), F32),
        pltpu.VMEM((count, LANES), F32),
        pltpu.VMEM((count, width), BF16),
        pltpu.VMEM((count, ff), BF16),
        pltpu.VMEM((count, ff), BF16),
        pltpu.VMEM((count, width), F32),
        pltpu.VMEM((count, LANES), F32),
        pltpu.VMEM((segment_ids.shape[0], ROW, ROW), F32),
        pltpu.SemaphoreType.DMA((8 * COPY_KINDS + VEC_KINDS,)),
        pltpu.SemaphoreType.DMA((8 * COPY_KINDS + VEC_KINDS,)),
        pltpu.SemaphoreType.DMA((8,)),
        pltpu.SemaphoreType.DMA((8,)),
        pltpu.SemaphoreType.DMA((LAYERS, 10)),
    ]
    return pl.pallas_call(
        forward_kernel,
        name="forward",
        out_shape=out_shape,
        in_specs=[vmem, vmem, vmem] + [any_spec] * 4,
        out_specs=[vmem] + [any_spec] * (len(out_shape) - 1),
        scratch_shapes=scratch,
        compiler_params=pltpu.CompilerParams(
            collective_id=0, has_side_effects=True, vmem_limit_bytes=60 << 20
        ),
    )(tokens, segment_ids, vec_low, qkv_low, out_low, in_low, back_low)


DEPTH = 4
Z_DEPTH = 6
CHUNKS = 12


def backward_kernel(
    cot_ref, seg_ref, vec_ref, tok_in, hlow_in, wq_in, wo_in, wi_in, wb_in,
    joined_in, att_in, xh1_in, r1_in, flow_in, active_in, slope_in, xh2_in, r2_in,
    grad_ref, total_ref, vtotal_ref,
    wq, wo, wi, wb, joined, att, xh1, r1, flow, active, slope, xh2, r2, hin,
    ring, got_d, got_a, got_b, got_z1, got_z2, part_sum, gtwo, glow, dvec, dbin, mask,
    vsend, vgot_d, vgot_a, vgot_b, vgot_z1, vgot_z2,
    load_sem, d_send, d_recv, a_send, a_recv, b_send, b_recv, z_send, z_recv, v_send, v_recv,
):
    here = Place()
    tokens, width = gtwo.shape
    ff = active.shape[1]
    rows_per, half_cols = ring.shape[4], width // 2
    core, x, y = here.core, here.x, here.y
    other_core, other_x, other_y = 1 - core, 1 - x, 1 - y
    to_mid = {"dp": 3 - here.z}
    inner = lax.rem(here.z + 1, 4) >= 2
    outer = jnp.logical_not(inner)
    last_chunk = LAYERS * CHUNKS
    greet((here.to_c, here.to_x, here.to_y, here.to_z, to_mid))

    sources = {
        "xh2": (xh2_in, xh2), "r2": (r2_in, r2), "active": (active_in, active), "wb": (wb_in, wb),
        "slope": (slope_in, slope), "flow": (flow_in, flow), "wi": (wi_in, wi),
        "xh1": (xh1_in, xh1), "r1": (r1_in, r1), "att": (att_in, att), "wo": (wo_in, wo),
        "joined": (joined_in, joined), "hin": (None, hin), "wq": (wq_in, wq),
    }
    order = list(sources)

    def load(layer, name):
        src, dst = sources[name]
        if name == "hin":
            src = tok_in if layer == 0 else hlow_in
        else:
            src = src.at[layer]
        return pltpu.make_async_copy(src, dst, load_sem.at[order.index(name)])

    for name in order:
        load(LAYERS - 1, name).start()

    def need(layer, *names):
        for name in names:
            load(layer, name).wait()

    def release(layer, *names):
        if layer > 0:
            for name in names:
                load(layer - 1, name).start()

    rows_here = seg_ref.shape[0]
    for r in range(rows_here):
        wide = jnp.broadcast_to(seg_ref[r : r + 1, :].astype(F32), (ROW, ROW))
        mask[r] = jnp.where(wide == wide.T, 1.0, 0.0)
    dvec[...] = jnp.zeros_like(dvec)

    def remote(src, dst, send, recv, device):
        return pltpu.make_async_remote_copy(
            src_ref=src, dst_ref=dst, send_sem=send, recv_sem=recv, device_id=device,
            device_id_type=MESH_ID,
        )

    low_cols, high_cols = pl.ds(0, half_cols), pl.ds(half_cols, half_cols)

    def copy_d(n):
        b, s = n % DEPTH, n % CHUNKS
        return remote(ring.at[s, other_core], got_d.at[b], d_send.at[b], d_recv.at[b], here.to_c)

    def copy_a(n, side):
        b, s = n % DEPTH, n % CHUNKS
        if side == 0:
            src, dev = ring.at[s, core, :, other_x, :, low_cols], here.to_x
        else:
            src, dev = ring.at[s, core, other_y, :, :, high_cols], here.to_y
        return remote(src, got_a.at[b, side], a_send.at[b, side], a_recv.at[b, side], dev)

    def copy_b(n, side):
        b, s = n % DEPTH, n % CHUNKS
        if side == 0:
            src, dev = ring.at[s, core, other_y, x, :, low_cols], here.to_y
        else:
            src, dev = ring.at[s, core, y, other_x, :, high_cols], here.to_x
        return remote(src, got_b.at[b, side], b_send.at[b, side], b_recv.at[b, side], dev)

    def copy_z(n, hop):
        b, far = n % DEPTH, n % Z_DEPTH
        if hop == 0:
            src, dst, dev, sem = part_sum.at[b], got_z1.at[far], here.to_z, far
        elif hop == 1:
            src, dst, dev, sem = part_sum.at[b], got_z2.at[b], to_mid, Z_DEPTH + b
        else:
            src, dst, dev, sem = total_ref.at[n], total_ref.at[n], here.to_z, Z_DEPTH + DEPTH + n
        return remote(src, dst, z_send.at[sem], z_recv.at[sem], dev)

    def added(a, b):
        return (a.astype(F32) + b.astype(F32)).astype(BF16)

    def stage0(n):
        copy_d(n).start()

    def stage1(n):
        b, s = n % DEPTH, n % CHUNKS
        copy_d(n).wait_recv()

        def add_shard(i, carry):
            iy, ix = lax.div(i, 2), lax.rem(i, 2)
            ring[s, core, iy, ix] = added(ring[s, core, iy, ix], got_d[b, iy, ix])
            return carry

        lax.fori_loop(0, 4, add_shard, 0)
        copy_a(n, 0).start()
        copy_a(n, 1).start()

    def stage2(n):
        b, s = n % DEPTH, n % CHUNKS
        copy_d(n).wait_send()
        copy_a(n, 0).wait_recv()
        for i in range(2):
            ring[s, core, i, x, :, low_cols] = added(
                ring[s, core, i, x, :, low_cols], got_a[b, 0, i]
            )
        copy_b(n, 0).start()
        copy_a(n, 1).wait_recv()
        for i in range(2):
            ring[s, core, y, i, :, high_cols] = added(
                ring[s, core, y, i, :, high_cols], got_a[b, 1, i]
            )
        copy_b(n, 1).start()

    def stage3(n):
        b, s = n % DEPTH, n % CHUNKS
        if n >= Z_DEPTH:
            @pl.when(outer)
            def _():
                copy_z(n - Z_DEPTH, 2).wait_recv()

        copy_a(n, 0).wait_send()
        copy_a(n, 1).wait_send()
        copy_b(n, 0).wait_recv()
        part_sum[b, :, low_cols] = added(ring[s, core, y, x, :, low_cols], got_b[b, 0])
        copy_b(n, 1).wait_recv()
        part_sum[b, :, high_cols] = added(ring[s, core, y, x, :, high_cols], got_b[b, 1])

        @pl.when(outer)
        def _():
            copy_z(n, 0).start()

    def stage4(n):
        b = n % DEPTH
        copy_b(n, 0).wait_send()
        copy_b(n, 1).wait_send()

        @pl.when(outer)
        def _():
            copy_z(n, 0).wait_send()

        @pl.when(inner)
        def _():
            copy_z(n, 0).wait_recv()
            part_sum[b] = added(part_sum[b], got_z1[n % Z_DEPTH])
            copy_z(n, 1).start()

    def stage5(n):
        b = n % DEPTH

        @pl.when(inner)
        def _():
            if n >= DEPTH:
                copy_z(n - DEPTH, 2).wait_send()
            copy_z(n, 1).wait_recv()
            copy_z(n, 1).wait_send()
            total_ref[n] = added(part_sum[b], got_z2[b])
            copy_z(n, 2).start()

    stages = (stage0, stage1, stage2, stage3, stage4, stage5)

    def vcopy(at):
        src, dst, dev = (
            (vsend.at[other_core], vgot_d, here.to_c),
            (vsend.at[core, :, other_x], vgot_a, here.to_x),
            (vsend.at[core, other_y, x], vgot_b, here.to_y),
            (vsend.at[core, y, x], vgot_z1, here.to_z),
            (vsend.at[core, y, x], vgot_z2, to_mid),
            (vtotal_ref, vtotal_ref, here.to_z),
        )[at]
        return remote(src, dst, v_send.at[at], v_recv.at[at], dev)

    def vstage(at):
        if at == 0:
            share = width // 8
            lane = lax.broadcasted_iota(jnp.int32, (width, LANES), 1)
            column = lax.broadcasted_iota(jnp.int32, (width, LANES), 0)
            low = dvec[...].astype(BF16)
            for owner in range(8):
                pick = (column == lane + owner * share) & (lane < share)
                vsend[owner % 2, owner // 4, (owner // 2) % 2] = jnp.dot(
                    low, jnp.where(pick, 1.0, 0.0).astype(BF16), preferred_element_type=F32
                ).astype(BF16)
            vcopy(0).start()
        elif at == 1:
            vcopy(0).wait_recv()
            for i in range(4):
                vsend[core, i // 2, i % 2] = added(vsend[core, i // 2, i % 2], vgot_d[i // 2, i % 2])
            vcopy(1).start()
        elif at == 2:
            vcopy(1).wait_recv()
            for i in range(2):
                vsend[core, i, x] = added(vsend[core, i, x], vgot_a[i])
            vcopy(2).start()
        elif at == 3:
            vcopy(2).wait_recv()
            vsend[core, y, x] = added(vsend[core, y, x], vgot_b[...])

            @pl.when(outer)
            def _():
                vcopy(3).start()
        elif at == 4:
            @pl.when(inner)
            def _():
                vcopy(3).wait_recv()
                vsend[core, y, x] = added(vsend[core, y, x], vgot_z1[...])
                vcopy(4).start()
        elif at == 5:
            @pl.when(inner)
            def _():
                vcopy(4).wait_recv()
                vcopy(4).wait_send()
                vtotal_ref[...] = added(vsend[core, y, x], vgot_z2[...])
                vcopy(5).start()
                vcopy(5).wait_send()

            @pl.when(outer)
            def _():
                vcopy(3).wait_send()
                vcopy(5).wait_recv()

            for early in range(3):
                vcopy(early).wait_send()

    tile = 64
    half = tokens // 2

    def norm_back(layer, first_row, grad_in, scaled, inverse, grad_out, bias_row):
        base = 12 * layer
        gain = vec_ref[base + first_row : base + first_row + 1, :]

        def step(n, carry):
            rows = pl.ds(pl.multiple_of(n * tile, tile), tile)
            grad = grad_in[rows, :]
            hat = scaled[rows, :]
            lifted = grad * gain
            left = jnp.mean(lifted, axis=-1, keepdims=True)
            right = jnp.mean(lifted * hat, axis=-1, keepdims=True)
            result = inverse[rows, :1] * (lifted - left - hat * right)
            grad_out[rows, :] = result
            glow[rows, :] = result.astype(BF16)
            return (
                carry[0] + jnp.sum(grad * hat, axis=0, keepdims=True),
                carry[1] + jnp.sum(grad, axis=0, keepdims=True),
                carry[2] + jnp.sum(result, axis=0, keepdims=True),
            )

        nil = jnp.zeros((1, width), F32)
        sums = lax.fori_loop(0, tokens // tile, step, (nil, nil, nil))
        dvec[base + first_row : base + first_row + 1, :] = sums[0]
        dvec[base + first_row + 1 : base + first_row + 2, :] = sums[1]
        dvec[base + bias_row : base + bias_row + 1, :] = sums[2]

    def tn(left, right):
        return lax.dot_general(left, right, (((0,), (0,)), ((), ())), preferred_element_type=F32)

    def nt(left, right):
        return lax.dot_general(left, right, (((1,), (1,)), ((), ())), preferred_element_type=F32)

    def task0(layer):
        need(layer, "xh2", "r2")
        if layer == LAYERS - 1:
            grad_ref[...] = cot_ref[...].astype(F32)
        norm_back(layer, 10, grad_ref, xh2, r2, gtwo, 9)
        release(layer, "xh2", "r2")

    def task1(layer):
        need(layer, "active")
        rows_f = ff // 8

        def step(owner, carry):
            part = tn(active[:, pl.ds(pl.multiple_of(owner * rows_f, LANES), rows_f)], glow[...])
            oc, ox, oy = lax.rem(owner, 2), lax.rem(lax.div(owner, 2), 2), lax.div(owner, 4)
            for j in range(rows_f // rows_per):
                ring[j, oc, oy, ox] = part[j * rows_per : (j + 1) * rows_per].astype(BF16)
            return carry

        lax.fori_loop(0, 8, step, 0)
        release(layer, "active")

    def task2(layer, at, of):
        if at == 0:
            need(layer, "wb", "slope")
        cols_at = 256
        count = ff // cols_at // of

        def step(n, carry):
            cols = pl.ds(pl.multiple_of(n * cols_at, cols_at), cols_at)
            sums = jnp.zeros((1, cols_at), F32)
            for h in range(2):
                rows = slice(h * half, (h + 1) * half)
                inner_grad = (nt(glow[rows, :], wb[cols, :]) * slope[rows, cols].astype(F32)).astype(BF16)
                slope[rows, cols] = inner_grad
                sums = sums + jnp.sum(inner_grad.astype(F32), axis=0, keepdims=True)
            dbin[:, cols] = sums
            return carry

        lax.fori_loop(at * count, (at + 1) * count, step, 0)
        if at == of - 1:
            release(layer, "wb")
            for j in range(ff // width):
                dvec[12 * layer + 5 + j : 12 * layer + 6 + j, :] = dbin[:, j * width : (j + 1) * width]

    def weight_chunk(at, left, right):
        quarter = width // 2

        for iy in range(2):
            part = tn(left[:, iy * quarter : (iy + 1) * quarter], right)
            for i in range(4):
                ring[at, i % 2, iy, i // 2] = part[i * rows_per : (i + 1) * rows_per].astype(BF16)

    def task3(layer, j):
        if j == 0:
            need(layer, "flow")
        weight_chunk(4 + j, flow, slope[:, j * width : (j + 1) * width])
        if j == 3:
            release(layer, "flow")

    def task4(layer):
        need(layer, "wi", "xh1", "r1")

        def step(n, carry):
            rows = pl.ds(pl.multiple_of(n * half, half), half)
            for j in range(width // 256):
                cols = slice(j * 256, (j + 1) * 256)
                gtwo[rows, cols] = gtwo[rows, cols] + nt(slope[rows, :], wi[cols, :])
            return carry

        lax.fori_loop(0, 2, step, 0)
        norm_back(layer, 3, gtwo, xh1, r1, gtwo, 2)
        release(layer, "slope", "wi", "xh1", "r1")

    def task5(layer):
        need(layer, "att")
        weight_chunk(8, att, glow[...])

    def task6(layer):
        need(layer, "wo")

        def step(n, carry):
            rows = pl.ds(pl.multiple_of(n * half, half), half)
            for j in range(width // 256):
                cols = slice(j * 256, (j + 1) * 256)
                att[rows, cols] = nt(glow[rows, :], wo[cols, :]).astype(BF16)
            return carry

        lax.fori_loop(0, 2, step, 0)
        release(layer, "wo")

    def task7(layer, at, of):
        if at == 0:
            need(layer, "joined")
        count = rows_here // of
        base = 12 * layer

        def step(r, carry):
            rows = pl.ds(pl.multiple_of(r * ROW, ROW), ROW)
            first_head = lax.broadcasted_iota(jnp.int32, (ROW, LANES), 1) < HEAD_DIM
            seen = mask[pl.ds(r, 1)][0]
            seen = jnp.concatenate([seen, seen], axis=0) > 0.5

            def stacked(value):
                nil = jnp.zeros_like(value)
                return jnp.concatenate(
                    [jnp.where(first_head, value, nil), jnp.where(first_head, nil, value)], axis=0
                )

            for j in range(HEADS // 2):
                lanes = [slice(p * width + j * LANES, p * width + (j + 1) * LANES) for p in range(3)]
                query, keys, value = (joined[rows, lane] for lane in lanes)
                out_grad = stacked(att[rows, lanes[0]])
                both = stacked(query)
                scores = nt(both, keys) * HEAD_DIM ** (-0.5)
                scores = jnp.where(seen, scores, NEGATIVE)
                grown = jnp.exp(scores - jnp.max(scores, axis=-1, keepdims=True))
                probs = grown * (1.0 / jnp.sum(grown, axis=-1, keepdims=True))
                grad_value = tn(probs.astype(BF16), out_grad).astype(BF16)
                grad_probs = nt(out_grad, value)
                centre = jnp.sum(probs * grad_probs, axis=-1, keepdims=True)
                grad_scores = (probs * (grad_probs - centre)).astype(BF16)
                wide = jnp.dot(grad_scores, keys, preferred_element_type=F32)
                grad_query = jnp.where(first_head, wide[:ROW], wide[ROW:]) * HEAD_DIM ** (-0.5)
                grad_query = grad_query.astype(BF16)
                grad_key = (tn(grad_scores, both) * HEAD_DIM ** (-0.5)).astype(BF16)
                joined[rows, lanes[0]] = grad_query
                joined[rows, lanes[1]] = grad_key
                joined[rows, lanes[2]] = grad_value
                dvec[base : base + 1, lanes[0]] += jnp.sum(
                    grad_query.astype(F32), axis=0, keepdims=True
                )
                dvec[base + 1 : base + 2, lanes[0]] += jnp.sum(
                    grad_value.astype(F32), axis=0, keepdims=True
                )
            return carry

        lax.fori_loop(at * count, (at + 1) * count, step, 0)
        if at == of - 1:
            release(layer, "att")

    def task8(layer, j):
        if j == 0:
            need(layer, "hin")
        weight_chunk(9 + j, hin, joined[:, j * width : (j + 1) * width])
        if j == 2:
            release(layer, "hin")

    def task9(layer):
        need(layer, "wq")

        def step(n, carry):
            rows = pl.ds(pl.multiple_of(n * half, half), half)
            for j in range(width // 256):
                cols = slice(j * 256, (j + 1) * 256)
                grad_ref[rows, cols] = gtwo[rows, cols] + nt(joined[rows, :], wq[cols, :])
            return carry

        lax.fori_loop(0, 2, step, 0)
        release(layer, "joined", "wq")

    plan = {}
    for layer in range(LAYERS):
        start = 12 * (LAYERS - 1 - layer)
        plan[start - 2] = [(task0, layer)]
        plan[start - 1] = [(task1, layer)]
        plan[start] = [(task2, layer, 0, 2)]
        plan[start + 1] = [(task2, layer, 1, 2)]
        plan[start + 2] = [(task3, layer, 0), (task3, layer, 1)]
        plan[start + 3] = [(task3, layer, 2), (task3, layer, 3)]
        plan[start + 4] = [(task4, layer)]
        plan[start + 5] = [(task5, layer), (task6, layer)]
        plan[start + 6] = [(task7, layer, 0, 2)]
        plan[start + 7] = [(task7, layer, 1, 2)]
        plan[start + 8] = [(task8, layer, 0), (task8, layer, 1), (task8, layer, 2)]
        plan[start + 9] = [(task9, layer)]
    vector_from = 20
    for slot in range(-2, last_chunk + len(stages)):
        for at, stage in enumerate(stages):
            n = slot - at
            if 0 <= n < last_chunk:
                stage(n)
        if 0 <= slot - vector_from - 1 < 6:
            vstage(slot - vector_from - 1)
        for task, *what in plan.get(slot, ()):
            task(*what)

    for n in range(last_chunk - DEPTH, last_chunk):
        @pl.when(inner)
        def _(n=n):
            copy_z(n, 2).wait_send()

    for n in range(last_chunk - Z_DEPTH, last_chunk):
        @pl.when(outer)
        def _(n=n):
            copy_z(n, 2).wait_recv()


def backward(cotangent, segment_ids, vec, tokens, hlow, weights, kept):
    count, width = tokens.shape
    ff = weights[2].shape[2]
    rows_per = width // 8
    hbm = pl.BlockSpec(memory_space=pltpu.HBM)
    vmem = pl.BlockSpec(memory_space=pltpu.VMEM)
    small = vec.shape[0]
    out_shape = (
        jax.ShapeDtypeStruct((count, width), F32),
        jax.ShapeDtypeStruct((LAYERS * CHUNKS, rows_per, width), BF16),
        jax.ShapeDtypeStruct((small, LANES), BF16),
    )
    dma = pltpu.SemaphoreType.DMA
    z_sems = Z_DEPTH + DEPTH + LAYERS * CHUNKS
    scratch = [
        pltpu.VMEM((width, 3 * width), BF16), pltpu.VMEM((width, width), BF16),
        pltpu.VMEM((width, ff), BF16), pltpu.VMEM((ff, width), BF16),
        pltpu.VMEM((count, 3 * width), BF16), pltpu.VMEM((count, width), BF16),
        pltpu.VMEM((count, width), F32), pltpu.VMEM((count, LANES), F32),
        pltpu.VMEM((count, width), BF16), pltpu.VMEM((count, ff), BF16), pltpu.VMEM((count, ff), BF16),
        pltpu.VMEM((count, width), F32), pltpu.VMEM((count, LANES), F32),
        pltpu.VMEM((count, width), BF16),
        pltpu.VMEM((CHUNKS, 2, 2, 2, rows_per, width), BF16),
        pltpu.VMEM((DEPTH, 2, 2, rows_per, width), BF16),
        pltpu.VMEM((DEPTH, 2, 2, rows_per, width // 2), BF16),
        pltpu.VMEM((DEPTH, 2, rows_per, width // 2), BF16),
        pltpu.VMEM((Z_DEPTH, rows_per, width), BF16),
        pltpu.VMEM((DEPTH, rows_per, width), BF16),
        pltpu.VMEM((DEPTH, rows_per, width), BF16),
        pltpu.VMEM((count, width), F32), pltpu.VMEM((count, width), BF16),
        pltpu.VMEM((small, width), F32), pltpu.VMEM((1, ff), F32),
        pltpu.VMEM((segment_ids.shape[0], ROW, ROW), F32),
        pltpu.VMEM((2, 2, 2, small, LANES), BF16), pltpu.VMEM((2, 2, small, LANES), BF16),
        pltpu.VMEM((2, small, LANES), BF16), pltpu.VMEM((small, LANES), BF16),
        pltpu.VMEM((small, LANES), BF16), pltpu.VMEM((small, LANES), BF16),
        dma((14,)), dma((DEPTH,)), dma((DEPTH,)), dma((DEPTH, 2)), dma((DEPTH, 2)),
        dma((DEPTH, 2)), dma((DEPTH, 2)), dma((z_sems,)), dma((z_sems,)), dma((6,)), dma((6,)),
    ]
    return pl.pallas_call(
        backward_kernel,
        name="backward",
        out_shape=out_shape,
        in_specs=[vmem, vmem, vmem] + [hbm] * 15,
        out_specs=[vmem, vmem, vmem],
        scratch_shapes=scratch,
        compiler_params=pltpu.CompilerParams(
            collective_id=1, has_side_effects=True, vmem_limit_bytes=62 << 20
        ),
    )(cotangent, segment_ids, vec, tokens, hlow, *weights, *kept)


def norm_forward(values, gain_row, shift_row):
    centered = values - jnp.mean(values, axis=-1, keepdims=True)
    inverse = lax.rsqrt(jnp.mean(centered * centered, axis=-1, keepdims=True) + EPSILON)
    scaled = centered * inverse
    return (scaled * gain_row + shift_row, scaled, inverse)


def norm_backward(grad_out, scaled, inverse, gain_row):
    grad_scaled = grad_out * gain_row
    grad_in = inverse * (
        grad_scaled
        - jnp.mean(grad_scaled, axis=-1, keepdims=True)
        - scaled * jnp.mean(grad_scaled * scaled, axis=-1, keepdims=True)
    )
    return (grad_in, jnp.sum(grad_out * scaled, axis=0), jnp.sum(grad_out, axis=0))


def score_block(queries, key_rows, same_segment):
    scores = jnp.einsum(
        "rqhe,rkhe->rhqk", queries, key_rows, preferred_element_type=jnp.float32
    ) * HEAD_DIM ** (-0.5)
    return jnp.where(same_segment, scores, NEGATIVE)


def layer_forward(hidden, same_segment, weights):
    qkv_used, out_used, in_used, back_used, vector_low = weights
    vector = vector_low.astype(jnp.float32)
    row_count = same_segment.shape[0]
    model_width = out_used.shape[0]
    hidden_low = hidden.astype(jnp.bfloat16)
    bias_qkv = jnp.concatenate([vector[0], jnp.zeros_like(vector[0]), vector[1]])
    joined = (jnp.dot(hidden_low, qkv_used, preferred_element_type=jnp.float32) + bias_qkv).astype(
        jnp.bfloat16
    )
    split_qkv = joined.reshape(row_count, -1, 3, HEADS, HEAD_DIM)
    scores = score_block(split_qkv[:, :, 0], split_qkv[:, :, 1], same_segment)
    row_top = jnp.max(scores, axis=-1, keepdims=True)
    log_total = row_top + jnp.log(jnp.sum(jnp.exp(scores - row_top), axis=-1, keepdims=True))
    prob_low = jnp.exp(scores - log_total).astype(jnp.bfloat16)
    attended = jnp.einsum(
        "rhqk,rkhe->rqhe", prob_low, split_qkv[:, :, 2], preferred_element_type=jnp.float32
    )
    attended_low = attended.reshape(-1, model_width).astype(jnp.bfloat16)
    branch = jnp.dot(attended_low, out_used, preferred_element_type=jnp.float32) + vector[2]
    first_norm, scaled_one, inverse_one = norm_forward(hidden + branch, vector[3], vector[4])
    first_low = first_norm.astype(jnp.bfloat16)
    inner_pre = jnp.dot(first_low, in_used, preferred_element_type=jnp.float32) + vector[
        5:9
    ].reshape(-1)
    active_low = jax.nn.gelu(inner_pre, approximate=False).astype(jnp.bfloat16)
    outer_out = jnp.dot(active_low, back_used, preferred_element_type=jnp.float32) + vector[9]
    output, scaled_two, inverse_two = norm_forward(first_norm + outer_out, vector[10], vector[11])
    kept_state = (
        hidden_low,
        joined,
        log_total,
        attended_low,
        scaled_one,
        inverse_one,
        first_low,
        inner_pre,
        active_low,
        scaled_two,
        inverse_two,
    )
    return (output, kept_state)


def layer_backward(grad_out, same_segment, weights, kept_state):
    qkv_used, out_used, in_used, back_used, vector_low = weights
    vector = vector_low.astype(jnp.float32)
    (
        hidden_low,
        joined,
        log_total,
        attended_low,
        scaled_one,
        inverse_one,
        first_low,
        inner_pre,
        active_low,
        scaled_two,
        inverse_two,
    ) = kept_state
    row_count = same_segment.shape[0]
    model_width = out_used.shape[0]
    grad_two, gain_two_grad, shift_two_grad = norm_backward(
        grad_out, scaled_two, inverse_two, vector[10]
    )
    grad_outer = grad_two.astype(jnp.bfloat16)
    back_bias_grad = jnp.sum(grad_two, axis=0)
    back_weight_grad = jnp.einsum(
        "tf,td->fd", active_low, grad_outer, preferred_element_type=jnp.float32
    )
    grad_active = jnp.einsum("td,fd->tf", grad_outer, back_used, preferred_element_type=jnp.float32)
    gelu_value, gelu_pull = jax.vjp(
        lambda values: jax.nn.gelu(values, approximate=False), inner_pre
    )
    grad_inner = gelu_pull(grad_active)[0].astype(jnp.bfloat16)
    in_bias_grad = jnp.sum(grad_inner, axis=0, dtype=jnp.float32)
    in_weight_grad = jnp.einsum(
        "td,tf->df", first_low, grad_inner, preferred_element_type=jnp.float32
    )
    grad_first = grad_two + jnp.einsum(
        "tf,df->td", grad_inner, in_used, preferred_element_type=jnp.float32
    )
    grad_one, gain_one_grad, shift_one_grad = norm_backward(
        grad_first, scaled_one, inverse_one, vector[3]
    )
    grad_branch = grad_one.astype(jnp.bfloat16)
    out_bias_grad = jnp.sum(grad_one, axis=0)
    out_weight_grad = jnp.einsum(
        "td,te->de", attended_low, grad_branch, preferred_element_type=jnp.float32
    )
    grad_mixed = jnp.einsum("te,de->td", grad_branch, out_used, preferred_element_type=jnp.float32)
    grad_mixed = grad_mixed.astype(jnp.bfloat16).reshape(row_count, -1, HEADS, HEAD_DIM)
    split_qkv = joined.reshape(row_count, -1, 3, HEADS, HEAD_DIM)
    queries = split_qkv[:, :, 0]
    key_rows = split_qkv[:, :, 1]
    value_rows = split_qkv[:, :, 2]
    prob_full = jnp.exp(score_block(queries, key_rows, same_segment) - log_total)
    prob_low = prob_full.astype(jnp.bfloat16)
    grad_values = jnp.einsum(
        "rhqk,rqhe->rkhe", prob_low, grad_mixed, preferred_element_type=jnp.float32
    )
    grad_probs = jnp.einsum(
        "rqhe,rkhe->rhqk", grad_mixed, value_rows, preferred_element_type=jnp.float32
    )
    centred = jnp.sum(prob_full * grad_probs, axis=-1, keepdims=True)
    grad_scores = (prob_full * (grad_probs - centred)).astype(jnp.bfloat16)
    grad_queries = jnp.einsum(
        "rhqk,rkhe->rqhe", grad_scores, key_rows, preferred_element_type=jnp.float32
    ) * HEAD_DIM ** (-0.5)
    grad_keys = jnp.einsum(
        "rhqk,rqhe->rkhe", grad_scores, queries, preferred_element_type=jnp.float32
    ) * HEAD_DIM ** (-0.5)
    grad_joined = (
        jnp.stack([grad_queries, grad_keys, grad_values], axis=2)
        .reshape(-1, 3 * model_width)
        .astype(jnp.bfloat16)
    )
    qkv_bias_grad = jnp.sum(grad_joined, axis=0, dtype=jnp.float32)
    qkv_weight_grad = jnp.einsum(
        "td,tc->dc", hidden_low, grad_joined, preferred_element_type=jnp.float32
    )
    grad_hidden = grad_one + jnp.einsum(
        "tc,dc->td", grad_joined, qkv_used, preferred_element_type=jnp.float32
    )
    vector_grad = jnp.concatenate(
        [
            qkv_bias_grad[:model_width][None],
            qkv_bias_grad[2 * model_width :][None],
            out_bias_grad[None],
            gain_one_grad[None],
            shift_one_grad[None],
            in_bias_grad.reshape(4, model_width),
            back_bias_grad[None],
            gain_two_grad[None],
            shift_two_grad[None],
        ],
        axis=0,
    )
    return (
        grad_hidden,
        (qkv_weight_grad, out_weight_grad, in_weight_grad, back_weight_grad, vector_grad),
    )


def adam_step(weight, gradient, moment_one, moment_two, step_rate):
    first_moment = BETA_FIRST * moment_one + (1.0 - BETA_FIRST) * gradient
    second_moment = BETA_SECOND * moment_two + (1.0 - BETA_SECOND) * gradient * gradient
    first_hat = first_moment / (1.0 - BETA_FIRST**STEP)
    second_hat = second_moment / (1.0 - BETA_SECOND**STEP)
    updated = weight - step_rate * (
        first_hat / (jnp.sqrt(second_hat) + ADAM_EPSILON) + WEIGHT_DECAY * weight
    )
    return gradient, updated, second_moment


def update_layer(summed, masters, moments, layer_at):
    outcome = []
    for kind_at in range(5):
        step_rate = RATE_VECTOR if kind_at == 4 else RATE_MATRIX
        outcome.append(
            adam_step(
                masters[kind_at][layer_at],
                summed[kind_at],
                moments[kind_at][0, layer_at],
                moments[kind_at][1, layer_at],
                step_rate,
            )
        )
    return outcome


def local_parts(masters, layer_at):
    return tuple((master[layer_at].astype(jnp.bfloat16) for master in masters))


def collect(results, kind_at, member):
    return jnp.stack([layer_result[kind_at][member] for layer_result in results])


def on_device_any(
    tokens,
    segment_ids,
    cotangent,
    qkv_weight,
    out_weight,
    in_weight,
    back_weight,
    vectors,
    qkv_moments,
    out_moments,
    in_moments,
    back_moments,
    vector_moments,
):
    masters = (qkv_weight, out_weight, in_weight, back_weight, vectors)
    moments = (qkv_moments, out_moments, in_moments, back_moments, vector_moments)
    same_segment = (segment_ids[:, :, None] == segment_ids[:, None, :])[:, None]
    hidden = tokens.astype(jnp.float32)
    saved_states = []
    for layer_at in range(LAYERS):
        parts_now = local_parts(masters, layer_at)
        weights = (
            lax.all_gather(parts_now[0], "fsdp", axis=0, tiled=True),
            lax.all_gather(parts_now[1], "fsdp", axis=0, tiled=True),
            lax.all_gather(parts_now[2], "fsdp", axis=0, tiled=True),
            lax.all_gather(parts_now[3], "fsdp", axis=0, tiled=True),
            lax.all_gather(parts_now[4], "fsdp", axis=1, tiled=True),
        )
        hidden, kept_state = layer_forward(hidden, same_segment, weights)
        saved_states.append(kept_state)
    activations = hidden.astype(jnp.bfloat16)
    grad_hidden = cotangent.astype(jnp.float32)
    results = [None] * LAYERS
    for layer_at in reversed(range(LAYERS)):
        parts_now = local_parts(masters, layer_at)
        weights = (
            lax.all_gather(parts_now[0], "fsdp", axis=0, tiled=True),
            lax.all_gather(parts_now[1], "fsdp", axis=0, tiled=True),
            lax.all_gather(parts_now[2], "fsdp", axis=0, tiled=True),
            lax.all_gather(parts_now[3], "fsdp", axis=0, tiled=True),
            lax.all_gather(parts_now[4], "fsdp", axis=1, tiled=True),
        )
        grad_hidden, weight_grads = layer_backward(
            grad_hidden, same_segment, weights, saved_states[layer_at]
        )
        shards = (
            lax.psum_scatter(
                weight_grads[0].astype(jnp.bfloat16), "fsdp", scatter_dimension=0, tiled=True
            ).astype(jnp.float32),
            lax.psum_scatter(
                weight_grads[1].astype(jnp.bfloat16), "fsdp", scatter_dimension=0, tiled=True
            ).astype(jnp.float32),
            lax.psum_scatter(
                weight_grads[2].astype(jnp.bfloat16), "fsdp", scatter_dimension=0, tiled=True
            ).astype(jnp.float32),
            lax.psum_scatter(
                weight_grads[3].astype(jnp.bfloat16), "fsdp", scatter_dimension=0, tiled=True
            ).astype(jnp.float32),
            lax.psum_scatter(
                weight_grads[4].astype(jnp.bfloat16), "fsdp", scatter_dimension=1, tiled=True
            ).astype(jnp.float32),
        )
        totals = (
            lax.psum(shards[0].astype(jnp.bfloat16), "dp").astype(jnp.float32),
            lax.psum(shards[1].astype(jnp.bfloat16), "dp").astype(jnp.float32),
            lax.psum(shards[2].astype(jnp.bfloat16), "dp").astype(jnp.float32),
            lax.psum(shards[3].astype(jnp.bfloat16), "dp").astype(jnp.float32),
            lax.psum(shards[4].astype(jnp.bfloat16), "dp").astype(jnp.float32),
        )
        results[layer_at] = update_layer(totals, masters, moments, layer_at)
    return (
        activations,
        grad_hidden,
        collect(results, 0, 0),
        collect(results, 1, 0),
        collect(results, 2, 0),
        collect(results, 3, 0),
        collect(results, 4, 0),
        collect(results, 0, 1),
        collect(results, 1, 1),
        collect(results, 2, 1),
        collect(results, 3, 1),
        collect(results, 4, 1),
        collect(results, 0, 2),
        collect(results, 1, 2),
        collect(results, 2, 2),
        collect(results, 3, 2),
        collect(results, 4, 2),
    )


def on_device(
    tokens,
    segment_ids,
    cotangent,
    qkv_weight,
    out_weight,
    in_weight,
    back_weight,
    vectors,
    qkv_moments,
    out_moments,
    in_moments,
    back_moments,
    vector_moments,
):
    masters = (qkv_weight, out_weight, in_weight, back_weight, vectors)
    moments = (qkv_moments, out_moments, in_moments, back_moments, vector_moments)
    share = vectors.shape[2]
    vec_low = jnp.pad(vectors.reshape(-1, share), ((0, 8), (0, LANES - share))).astype(BF16)
    activations, wq, wo, wi, wb, vec, *kept, hlow = forward(
        tokens, segment_ids, vec_low, qkv_weight.astype(BF16), out_weight.astype(BF16),
        in_weight.astype(BF16), back_weight.astype(BF16),
    )
    grad, total, vtotal = backward(
        cotangent, segment_ids, vec, tokens, hlow, (wq, wo, wi, wb), kept
    )
    rows, width = total.shape[1:]
    total = total.reshape(LAYERS, CHUNKS, rows, width)[::-1]

    def side_by_side(first, last):
        return total[:, first:last].transpose(0, 2, 1, 3).reshape(LAYERS, rows, -1)

    summed = (
        side_by_side(9, 12),
        total[:, 8],
        side_by_side(4, 8),
        total[:, :4].reshape(LAYERS, 4 * rows, width),
        vtotal[: 12 * LAYERS, :share].reshape(LAYERS, 12, share),
    )
    results = [
        adam_step(
            masters[kind], summed[kind].astype(F32), moments[kind][0], moments[kind][1],
            RATE_VECTOR if kind == 4 else RATE_MATRIX,
        )
        for kind in range(5)
    ]
    return (
        activations,
        grad,
        *(result[0] for result in results),
        *(result[1] for result in results),
        *(result[2] for result in results),
    )


def solution(mesh):
    in_specs = (
        P(("fsdp", "dp"), None),
        P(("fsdp", "dp"), None),
        P(("fsdp", "dp"), None),
        P(None, "fsdp", None),
        P(None, "fsdp", None),
        P(None, "fsdp", None),
        P(None, "fsdp", None),
        P(None, None, "fsdp"),
        P(None, None, "fsdp", None),
        P(None, None, "fsdp", None),
        P(None, None, "fsdp", None),
        P(None, None, "fsdp", None),
        P(None, None, None, "fsdp"),
    )
    out_specs = (
        P(("fsdp", "dp"), None),
        P(("fsdp", "dp"), None),
        P(None, "fsdp", None),
        P(None, "fsdp", None),
        P(None, "fsdp", None),
        P(None, "fsdp", None),
        P(None, None, "fsdp"),
        P(None, "fsdp", None),
        P(None, "fsdp", None),
        P(None, "fsdp", None),
        P(None, "fsdp", None),
        P(None, None, "fsdp"),
        P(None, "fsdp", None),
        P(None, "fsdp", None),
        P(None, "fsdp", None),
        P(None, "fsdp", None),
        P(None, None, "fsdp"),
    )
    body = on_device if dict(mesh.shape) == {"fsdp": 8, "dp": 4} else on_device_any
    return jax.shard_map(
        body, mesh=mesh, in_specs=in_specs, out_specs=out_specs, check_vma=False
    )
```

```python
import jax
import jax.numpy as jnp
from jax import lax
from jax.experimental import pallas as pl
from jax.experimental.pallas import tpu as pltpu
from jax.sharding import PartitionSpec as P

HEADS = 12
HEAD_DIM = 64
LAYERS = 2
STEP = 3
ROW = 128
LANES = 128

EPSILON = 1e-05
NEGATIVE = -1000000000.0
BETA_FIRST = 0.5
BETA_SECOND = 0.5
WEIGHT_DECAY = 0.01
ADAM_EPSILON = 1e-08
RATE_MATRIX = 0.06
RATE_VECTOR = 0.5
MESH_ID = pl.DeviceIdType.MESH
BF16 = jnp.bfloat16
F32 = jnp.float32


class Place:
    def __init__(self):
        f = lax.axis_index("fsdp")
        z = lax.axis_index("dp")
        core = lax.rem(f, 2)
        x = lax.rem(lax.div(f, 2), 2)
        y = lax.div(f, 4)
        self.f, self.z, self.core, self.x, self.y = f, z, core, x, y
        self.fc = f + 1 - 2 * core
        self.fx = f + 2 - 4 * x
        self.fy = f + 4 - 8 * y
        self.fd = self.fx + 4 - 8 * y
        self.q = lax.rem(z, 2)
        self.to_c = {"fsdp": self.fc}
        self.to_x = {"fsdp": self.fx}
        self.to_y = {"fsdp": self.fy}
        self.to_z = {"dp": z + 1 - 2 * self.q}


def greet(partners):
    barrier = pltpu.get_barrier_semaphore()
    for partner in partners:
        pl.semaphore_signal(barrier, inc=1, device_id=partner, device_id_type=MESH_ID)
    pl.semaphore_wait(barrier, len(partners))


def norm_rows(values, gain_row, shift_row):
    centered = values - jnp.mean(values, axis=-1, keepdims=True)
    inverse = lax.rsqrt(jnp.mean(centered * centered, axis=-1, keepdims=True) + EPSILON)
    scaled = centered * inverse
    return scaled * gain_row + shift_row, scaled, inverse


def gelu_pair(value):
    cdf = 0.5 * (1.0 + lax.erf(value * 0.7071067811865476))
    slope = cdf + value * (0.3989422804014327 * jnp.exp(-0.5 * value * value))
    return value * cdf, slope


SPLITS = (3, 1, 2, 4)
COPY_KINDS = 14
VEC_KINDS = 7


def gather_pieces(shards):
    pieces = []
    for layer in range(LAYERS):
        for kind, (rows, cols) in enumerate(shards):
            count = SPLITS[kind]
            for i in range(count):
                if kind == 3:
                    pieces.append((layer, kind, i * rows // count, rows // count, 0, cols))
                else:
                    pieces.append((layer, kind, 0, rows, i * cols // count, cols // count))
    return pieces


ORDER = (
    ("own", 0), ("own", 1), ("own", 2), ("pre", 0), ("own", 3), ("pre", 1), ("own", 4), ("pre", 2),
    ("s1", 0), ("s1", 1), ("s1", 2), ("s1", 3), ("own", 5), ("s1", 4), ("s2", 0), ("s2", 1), ("s2", 2),
    ("own", 6), ("s2", 3), ("own", 7), ("s3", 0), ("own", 8), ("s3", 1), ("s1", 5), ("s4", 0),
    ("qkv", 0, 0), ("s3", 2), ("s4", 1), ("qkv", 0, 1), ("s2", 4), ("s3", 3), ("s4", 2), ("qkv", 0, 2),
    ("att", 0, 0), ("own", 9), ("s1", 6), ("att", 0, 1), ("s1", 7), ("att", 0, 2), ("own", 10),
    ("att", 0, 3), ("s1", 8), ("s3", 4), ("s4", 3), ("out", 0, 0), ("s2", 5), ("out", 0, 1),
    ("own", 11), ("s4", 4), ("in", 0, 0), ("own", 12), ("s1", 9), ("s2", 6), ("s2", 7), ("in", 0, 1),
    ("own", 13), ("s1", 10), ("s3", 5), ("s2", 8), ("s4", 5), ("in", 0, 2), ("own", 14), ("s1", 11),
    ("s3", 6), ("s3", 7), ("in", 0, 3), ("s1", 12), ("s2", 9), ("s3", 8), ("s4", 6), ("s4", 7),
    ("s1", 13), ("s4", 8), ("s2", 10), ("own", 15), ("s3", 9), ("s1", 14), ("s4", 9), ("back", 0, 0),
    ("s2", 11), ("back", 0, 1), ("own", 16), ("s2", 12), ("s2", 13), ("s3", 10), ("own", 17),
    ("s4", 10), ("qkv", 1, 0), ("own", 18), ("s3", 11), ("s1", 15), ("s3", 12), ("s4", 11),
    ("qkv", 1, 1), ("s2", 14), ("s3", 13), ("s4", 12), ("qkv", 1, 2), ("att", 1, 0), ("own", 19),
    ("s1", 16), ("att", 1, 1), ("att", 1, 2), ("s1", 17), ("att", 1, 3), ("s1", 18), ("s3", 14),
    ("s4", 13), ("out", 1, 0), ("out", 1, 1), ("s2", 15), ("s4", 14), ("in", 1, 0), ("s1", 19),
    ("s2", 16), ("in", 1, 1), ("s2", 17), ("s2", 18), ("s3", 15), ("s2", 19), ("s4", 15), ("in", 1, 2),
    ("s3", 16), ("in", 1, 3), ("s3", 17), ("s3", 18), ("s4", 16), ("s3", 19), ("s4", 17), ("s4", 18),
    ("s4", 19), ("back", 1, 0), ("back", 1, 1),
)


def forward_kernel(
    tok_ref, seg_ref, vec_ref, q_w, o_w, i_w, b_w,
    act_out, wq_out, wo_out, wi_out, wb_out, vec_out,
    joined_out, att_out, xh1_out, r1_out, flow_out, active_out, slope_out, xh2_out, r2_out, hlow_out,
    wq0, wo0, wi0, wb0, wq1, wo1, wi1, wb1, st_q, st_o, st_i, st_b, vslots, vec,
    hid, hlow, joined, att, first, xh1, r1, flow, active, slope, xh2, r2, mask,
    send_sem, recv_sem, own_sem, wout_sem, save_sem,
):
    here = Place()
    masters = (q_w, o_w, i_w, b_w)
    stages = (st_q, st_o, st_i, st_b)
    bufs = ((wq0, wo0, wi0, wb0), (wq1, wo1, wi1, wb1))
    wouts = (wq_out, wo_out, wi_out, wb_out)
    f, fx, fy, fd = here.f, here.fx, here.fy, here.fd
    pieces = gather_pieces([m.shape[1:] for m in masters])
    tokens, width = hid.shape
    half = tokens // 2

    def stage_copy(layer, kind):
        return pltpu.make_async_copy(
            masters[kind].at[layer], stages[kind].at[layer], own_sem.at[4 * layer + kind]
        )

    for layer in range(LAYERS):
        for kind in range(4):
            stage_copy(layer, kind).start()
    mine = jnp.zeros((1,) + vslots.shape[1:], BF16)
    vslots[pl.ds(f, 1)] = mine
    share = vec_ref.shape[2]
    for layer in range(LAYERS):
        vslots[pl.ds(f, 1), 16 * layer : 16 * layer + 12, :share] = vec_ref[:, layer, :].astype(BF16)[None]
    greet((here.to_c, here.to_x, here.to_y, here.to_z))

    started = []
    copies = {}

    def make(p, kind):
        layer, matrix, row_at, rows, col_at, cols = pieces[p]
        buf = bufs[layer][matrix]
        shard_rows = masters[matrix].shape[1]
        third = cols // 3
        two = 2 * third
        c_xy = pl.multiple_of(col_at + here.q * third, LANES)
        c_b = pl.multiple_of(c_xy + third, LANES)
        c_z = pl.multiple_of(col_at + here.q * two, LANES)
        c_w = pl.multiple_of(col_at + (1 - here.q) * two, LANES)

        def win(owner, col, wide):
            at = pl.multiple_of(owner * shard_rows + row_at, 32)
            return buf.at[pl.ds(at, rows), pl.ds(col, wide)]

        owner, col, wide, device = (
            (f, col_at, cols, here.to_c), (f, c_xy, two, here.to_x), (f, c_xy, two, here.to_y),
            (fx, c_xy, two, here.to_c), (fx, c_xy, third, here.to_y), (fx, c_z, third, here.to_z),
            (fy, c_xy, two, here.to_c), (fy, c_b, third, here.to_x), (fy, c_z, third, here.to_z),
            (fd, c_xy, two, here.to_c), (fd, c_z, third, here.to_z),
            (fx, c_w, third, here.to_c), (fy, c_w, third, here.to_c), (fd, c_w, third, here.to_c),
        )[kind]
        window = win(owner, col, wide)
        slot = p * COPY_KINDS + kind
        return pltpu.make_async_remote_copy(
            src_ref=window, dst_ref=window, send_sem=send_sem.at[slot], recv_sem=recv_sem.at[slot],
            device_id=device, device_id_type=MESH_ID,
        )

    def start(p, *kinds):
        for kind in kinds:
            copy = make(p, kind)
            copy.start()
            copies[p, kind] = copy
            started.append(copy)

    def arrived(p, *kinds):
        for kind in kinds:
            copies[p, kind].wait_recv()

    def send_own(p):
        layer, matrix, row_at, rows, col_at, cols = pieces[p]
        if row_at == 0 and col_at == 0:
            stage_copy(layer, matrix).wait()
        stage, buf = stages[matrix], bufs[layer][matrix]
        shard_rows = stage.shape[1]
        tile = 32

        def step(n, carry):
            at = pl.multiple_of(row_at + n * tile, tile)
            to = pl.multiple_of(f * shard_rows + row_at + n * tile, tile)
            buf[pl.ds(to, tile), col_at : col_at + cols] = stage[
                layer, pl.ds(at, tile), col_at : col_at + cols
            ].astype(BF16)
            return carry

        lax.fori_loop(0, rows // tile, step, 0)
        start(p, 1, 2, 0)

    wcopies = []

    def comm(what, p):
        if what == "own":
            send_own(p)
        elif what == "s1":
            arrived(p, 1, 2)
            start(p, 4, 7, 5, 8, 3, 6)
        elif what == "s2":
            arrived(p, 4, 7)
            start(p, 10, 9)
        elif what == "s3":
            arrived(p, 5, 8, 10)
            start(p, 11, 12, 13)
        else:
            arrived(p, 0, 3, 6, 9, 11, 12, 13)
            layer, matrix = pieces[p][:2]
            if p + 1 == len(pieces) or pieces[p + 1][1] != matrix:
                copy = pltpu.make_async_copy(
                    bufs[layer][matrix], wouts[matrix].at[layer], wout_sem.at[4 * layer + matrix]
                )
                copy.start()
                wcopies.append(copy)

    def vcopy(kind):
        owner, dev = (
            (f, here.to_x), (f, here.to_y), (f, here.to_c),
            (fx, here.to_y), (fx, here.to_c), (fy, here.to_c), (fd, here.to_c),
        )[kind]
        slot = len(pieces) * COPY_KINDS + kind
        return pltpu.make_async_remote_copy(
            src_ref=vslots.at[owner], dst_ref=vslots.at[owner], send_sem=send_sem.at[slot],
            recv_sem=recv_sem.at[slot], device_id=dev, device_id_type=MESH_ID,
        )

    vc = [vcopy(kind) for kind in range(VEC_KINDS)]
    started.extend(vc)
    for kind in (0, 1, 2):
        vc[kind].start()
    rows_here = seg_ref.shape[0]

    def prepare(step):
        if step == 0:
            for r in range(rows_here):
                wide = jnp.broadcast_to(seg_ref[r : r + 1, :].astype(F32), (ROW, ROW))
                mask[r] = jnp.where(wide == wide.T, 1.0, 0.0)
            vc[0].wait_recv()
            vc[1].wait_recv()
            for kind in (3, 4, 5):
                vc[kind].start()
        elif step == 1:
            vc[3].wait_recv()
            vc[6].start()
        else:
            for kind in (2, 4, 5, 6):
                vc[kind].wait_recv()
            lane = lax.broadcasted_iota(jnp.int32, (LANES, width), 0)
            column = lax.broadcasted_iota(jnp.int32, (LANES, width), 1)
            whole = jnp.zeros(vec.shape, F32)
            for owner in range(8):
                pick = (column == lane + owner * share) & (lane < share)
                whole = whole + jnp.dot(
                    vslots[owner], jnp.where(pick, 1.0, 0.0).astype(BF16),
                    preferred_element_type=F32,
                )
            vec[...] = whole

    saves = {}

    def save(layer, at, src, dst):
        copy = pltpu.make_async_copy(src, dst, save_sem.at[layer, at])
        copy.start()
        saves[layer, at] = copy

    def saved(layer, *ats):
        if layer >= 0:
            for at in ats:
                saves[layer, at].wait()

    def row(layer, at):
        return vec[16 * layer + at : 16 * layer + at + 1, :]

    def qkv(layer, part):
        low_ref, wq = (tok_ref if layer == 0 else hlow), bufs[layer][0]
        if part == 0:
            saved(layer - 1, 0)
        cols = slice(part * width, (part + 1) * width)

        def step(n, carry):
            rows = pl.ds(pl.multiple_of(n * half, half), half)
            acc = jnp.dot(low_ref[rows, :], wq[:, cols], preferred_element_type=F32)
            if part != 1:
                acc = acc + row(layer, part // 2)
            joined[rows, cols] = acc.astype(BF16)
            return carry

        lax.fori_loop(0, 2, step, 0)
        if part == 2:
            save(layer, 0, joined, joined_out.at[layer])

    def attend(layer, r):
        if r == 0:
            saved(layer - 1, 1)
        rows = slice(r * ROW, (r + 1) * ROW)
        first_head = lax.broadcasted_iota(jnp.int32, (ROW, LANES), 1) < HEAD_DIM
        seen = mask[r]
        seen = jnp.concatenate([seen, seen], axis=0) > 0.5
        for j in range(HEADS // 2):
            query, keys, value = (
                joined[rows, part * width + j * LANES : part * width + (j + 1) * LANES]
                for part in range(3)
            )
            nil = jnp.zeros_like(query)
            both = jnp.concatenate(
                [jnp.where(first_head, query, nil), jnp.where(first_head, nil, query)], axis=0
            )
            scores = lax.dot_general(
                both, keys, (((1,), (1,)), ((), ())), preferred_element_type=F32
            ) * HEAD_DIM ** (-0.5)
            scores = jnp.where(seen, scores, NEGATIVE)
            grown = jnp.exp(scores - jnp.max(scores, axis=-1, keepdims=True))
            probs = grown * (1.0 / jnp.sum(grown, axis=-1, keepdims=True))
            mixed = jnp.dot(probs.astype(BF16), value, preferred_element_type=F32)
            att[rows, j * LANES : (j + 1) * LANES] = jnp.where(
                first_head, mixed[:ROW], mixed[ROW:]
            ).astype(BF16)
        if r == rows_here - 1:
            save(layer, 1, att, att_out.at[layer])

    norm_tile = 64

    def out_half(layer, h):
        wo = bufs[layer][1]
        if h == 0:
            saved(layer - 1, 2, 3, 4)
        top = slice(h * half, (h + 1) * half)
        first[top, :] = jnp.dot(att[top, :], wo[...], preferred_element_type=F32)

        def step(n, carry):
            rows = pl.ds(pl.multiple_of(h * half + n * norm_tile, norm_tile), norm_tile)
            before = tok_ref[rows, :].astype(F32) if layer == 0 else hid[rows, :]
            normed, scaled, inverse = norm_rows(
                before + first[rows, :] + row(layer, 2), row(layer, 3), row(layer, 4)
            )
            first[rows, :] = normed
            flow[rows, :] = normed.astype(BF16)
            xh1[rows, :] = scaled
            r1[rows, :] = jnp.broadcast_to(inverse, (norm_tile, LANES))
            return carry

        lax.fori_loop(0, half // norm_tile, step, 0)
        if h == 1:
            save(layer, 2, xh1, xh1_out.at[layer])
            save(layer, 3, r1, r1_out.at[layer])
            save(layer, 4, flow, flow_out.at[layer])

    def in_part(layer, part):
        wi = bufs[layer][2]
        if part == 0:
            saved(layer - 1, 5, 6)
        bias_row = row(layer, 5 + part)
        tile = 256
        for sub in range(width // tile):
            bias = bias_row[:, sub * tile : (sub + 1) * tile]
            cols = slice(part * width + sub * tile, part * width + (sub + 1) * tile)

            def step(n, carry, cols=cols, bias=bias):
                rows = pl.ds(pl.multiple_of(n * half, half), half)
                inner = jnp.dot(flow[rows, :], wi[:, cols], preferred_element_type=F32) + bias
                value, change = gelu_pair(inner)
                active[rows, cols] = value.astype(BF16)
                slope[rows, cols] = change.astype(BF16)
                return carry

            lax.fori_loop(0, 2, step, 0)
        if part == 3:
            save(layer, 5, active, active_out.at[layer])
            save(layer, 6, slope, slope_out.at[layer])

    def back_half(layer, h):
        wb = bufs[layer][3]
        if h == 0:
            saved(layer - 1, 7, 8)
        top = slice(h * half, (h + 1) * half)
        first[top, :] = first[top, :] + jnp.dot(
            active[top, :], wb[...], preferred_element_type=F32
        )

        def step(n, carry):
            rows = pl.ds(pl.multiple_of(h * half + n * norm_tile, norm_tile), norm_tile)
            normed, scaled, inverse = norm_rows(
                first[rows, :] + row(layer, 9), row(layer, 10), row(layer, 11)
            )
            xh2[rows, :] = scaled
            r2[rows, :] = jnp.broadcast_to(inverse, (norm_tile, LANES))
            if layer == LAYERS - 1:
                act_out[rows, :] = normed.astype(BF16)
            else:
                hid[rows, :] = normed
                hlow[rows, :] = normed.astype(BF16)
            return carry

        lax.fori_loop(0, half // norm_tile, step, 0)
        if h == 1:
            save(layer, 7, xh2, xh2_out.at[layer])
            save(layer, 8, r2, r2_out.at[layer])
            if layer == 0:
                save(layer, 9, hlow, hlow_out)

    compute = {"qkv": qkv, "att": attend, "out": out_half, "in": in_part, "back": back_half}
    for what, *at in ORDER:
        if what in compute:
            compute[what](*at)
        elif what == "pre":
            prepare(*at)
        else:
            comm(what, *at)
    vec_save = pltpu.make_async_copy(vec, vec_out, save_sem.at[1, 9])
    vec_save.start()
    for copy in started:
        copy.wait_send()
    for copy in wcopies:
        copy.wait()
    saved(0, 9)
    saved(1, *range(9))
    vec_save.wait()


def forward(tokens, segment_ids, vectors, *masters):
    count, width = tokens.shape
    ff = masters[2].shape[2]
    copies = len(gather_pieces([m.shape[1:] for m in masters])) * COPY_KINDS + VEC_KINDS
    any_spec = pl.BlockSpec(memory_space=pltpu.HBM)
    vmem = pl.BlockSpec(memory_space=pltpu.VMEM)

    def shape(dims, kind):
        return jax.ShapeDtypeStruct(dims, kind)

    out_shape = (
        shape((count, width), BF16),
        shape((LAYERS, width, 3 * width), BF16),
        shape((LAYERS, width, width), BF16),
        shape((LAYERS, width, ff), BF16),
        shape((LAYERS, ff, width), BF16),
        shape((16 * LAYERS, width), F32),
        shape((LAYERS, count, 3 * width), BF16),
        shape((LAYERS, count, width), BF16),
        shape((LAYERS, count, width), F32),
        shape((LAYERS, count, LANES), F32),
        shape((LAYERS, count, width), BF16),
        shape((LAYERS, count, ff), BF16),
        shape((LAYERS, count, ff), BF16),
        shape((LAYERS, count, width), F32),
        shape((LAYERS, count, LANES), F32),
        shape((count, width), BF16),
    )
    weights = [
        pltpu.VMEM((width, 3 * width), BF16), pltpu.VMEM((width, width), BF16),
        pltpu.VMEM((width, ff), BF16), pltpu.VMEM((ff, width), BF16),
    ]
    scratch = weights * LAYERS + [pltpu.VMEM(m.shape, F32) for m in masters] + [
        pltpu.VMEM((8, 16 * LAYERS, LANES), BF16),
        pltpu.VMEM((16 * LAYERS, width), F32),
        pltpu.VMEM((count, width), F32),
        pltpu.VMEM((count, width), BF16),
        pltpu.VMEM((count, 3 * width), BF16),
        pltpu.VMEM((count, width), BF16),
        pltpu.VMEM((count, width), F32),
        pltpu.VMEM((count, width), F32),
        pltpu.VMEM((count, LANES), F32),
        pltpu.VMEM((count, width), BF16),
        pltpu.VMEM((count, ff), BF16),
        pltpu.VMEM((count, ff), BF16),
        pltpu.VMEM((count, width), F32),
        pltpu.VMEM((count, LANES), F32),
        pltpu.VMEM((segment_ids.shape[0], ROW, ROW), F32),
        pltpu.SemaphoreType.DMA((copies,)),
        pltpu.SemaphoreType.DMA((copies,)),
        pltpu.SemaphoreType.DMA((8,)),
        pltpu.SemaphoreType.DMA((8,)),
        pltpu.SemaphoreType.DMA((LAYERS, 10)),
    ]
    return pl.pallas_call(
        forward_kernel,
        name="forward",
        out_shape=out_shape,
        in_specs=[vmem, vmem, vmem] + [any_spec] * 4,
        out_specs=[vmem] + [any_spec] * (len(out_shape) - 1),
        scratch_shapes=scratch,
        compiler_params=pltpu.CompilerParams(
            collective_id=0, has_side_effects=True, vmem_limit_bytes=62 << 20
        ),
    )(tokens, segment_ids, vectors, *masters)


DEPTH = 4
Z_DEPTH = 6
CHUNKS = 12


def backward_kernel(
    cot_ref, seg_ref, vec_ref, tok_in, hlow_in, wq_in, wo_in, wi_in, wb_in,
    joined_in, att_in, xh1_in, r1_in, flow_in, active_in, slope_in, xh2_in, r2_in,
    grad_ref, total_ref, vtotal_ref,
    wq, wo, wi, wb, joined, att, xh1, r1, flow, active, slope, xh2, r2, hin,
    ring, got_d, got_a, got_b, got_z1, got_z2, part_sum, gtwo, glow, dvec, dbin, mask,
    vsend, vgot_d, vgot_a, vgot_b, vgot_z1, vgot_z2,
    load_sem, d_send, d_recv, a_send, a_recv, b_send, b_recv, z_send, z_recv, v_send, v_recv,
):
    here = Place()
    tokens, width = gtwo.shape
    ff = active.shape[1]
    rows_per, half_cols = ring.shape[4], width // 2
    core, x, y = here.core, here.x, here.y
    other_core, other_x, other_y = 1 - core, 1 - x, 1 - y
    to_mid = {"dp": 3 - here.z}
    inner = lax.rem(here.z + 1, 4) >= 2
    outer = jnp.logical_not(inner)
    last_chunk = LAYERS * CHUNKS
    greet((here.to_c, here.to_x, here.to_y, here.to_z, to_mid))

    sources = {
        "xh2": (xh2_in, xh2), "r2": (r2_in, r2), "active": (active_in, active), "wb": (wb_in, wb),
        "slope": (slope_in, slope), "flow": (flow_in, flow), "wi": (wi_in, wi),
        "xh1": (xh1_in, xh1), "r1": (r1_in, r1), "att": (att_in, att), "wo": (wo_in, wo),
        "joined": (joined_in, joined), "hin": (None, hin), "wq": (wq_in, wq),
    }
    order = list(sources)

    def load(layer, name):
        src, dst = sources[name]
        if name == "hin":
            src = tok_in if layer == 0 else hlow_in
        else:
            src = src.at[layer]
        return pltpu.make_async_copy(src, dst, load_sem.at[order.index(name)])

    for name in order:
        load(LAYERS - 1, name).start()

    def need(layer, *names):
        for name in names:
            load(layer, name).wait()

    def release(layer, *names):
        if layer > 0:
            for name in names:
                load(layer - 1, name).start()

    rows_here = seg_ref.shape[0]
    for r in range(rows_here):
        wide = jnp.broadcast_to(seg_ref[r : r + 1, :].astype(F32), (ROW, ROW))
        mask[r] = jnp.where(wide == wide.T, 1.0, 0.0)
    dvec[...] = jnp.zeros_like(dvec)

    def remote(src, dst, send, recv, device):
        return pltpu.make_async_remote_copy(
            src_ref=src, dst_ref=dst, send_sem=send, recv_sem=recv, device_id=device,
            device_id_type=MESH_ID,
        )

    low_cols, high_cols = pl.ds(0, half_cols), pl.ds(half_cols, half_cols)

    def copy_d(n):
        b, s = n % DEPTH, n % CHUNKS
        return remote(ring.at[s, other_core], got_d.at[b], d_send.at[b], d_recv.at[b], here.to_c)

    def copy_a(n, side):
        b, s = n % DEPTH, n % CHUNKS
        if side == 0:
            src, dev = ring.at[s, core, :, other_x, :, low_cols], here.to_x
        else:
            src, dev = ring.at[s, core, other_y, :, :, high_cols], here.to_y
        return remote(src, got_a.at[b, side], a_send.at[b, side], a_recv.at[b, side], dev)

    def copy_b(n, side):
        b, s = n % DEPTH, n % CHUNKS
        if side == 0:
            src, dev = ring.at[s, core, other_y, x, :, low_cols], here.to_y
        else:
            src, dev = ring.at[s, core, y, other_x, :, high_cols], here.to_x
        return remote(src, got_b.at[b, side], b_send.at[b, side], b_recv.at[b, side], dev)

    def copy_z(n, hop):
        b, far = n % DEPTH, n % Z_DEPTH
        if hop == 0:
            src, dst, dev, sem = part_sum.at[b], got_z1.at[far], here.to_z, far
        elif hop == 1:
            src, dst, dev, sem = part_sum.at[b], got_z2.at[b], to_mid, Z_DEPTH + b
        else:
            src, dst, dev, sem = total_ref.at[n], total_ref.at[n], here.to_z, Z_DEPTH + DEPTH + n
        return remote(src, dst, z_send.at[sem], z_recv.at[sem], dev)

    def added(a, b):
        return (a.astype(F32) + b.astype(F32)).astype(BF16)

    def stage0(n):
        copy_d(n).start()

    def stage1(n):
        b, s = n % DEPTH, n % CHUNKS
        copy_d(n).wait_recv()

        def add_shard(i, carry):
            iy, ix = lax.div(i, 2), lax.rem(i, 2)
            ring[s, core, iy, ix] = added(ring[s, core, iy, ix], got_d[b, iy, ix])
            return carry

        lax.fori_loop(0, 4, add_shard, 0)
        copy_a(n, 0).start()
        copy_a(n, 1).start()

    def stage2(n):
        b, s = n % DEPTH, n % CHUNKS
        copy_d(n).wait_send()
        copy_a(n, 0).wait_recv()
        for i in range(2):
            ring[s, core, i, x, :, low_cols] = added(
                ring[s, core, i, x, :, low_cols], got_a[b, 0, i]
            )
        copy_b(n, 0).start()
        copy_a(n, 1).wait_recv()
        for i in range(2):
            ring[s, core, y, i, :, high_cols] = added(
                ring[s, core, y, i, :, high_cols], got_a[b, 1, i]
            )
        copy_b(n, 1).start()

    def stage3(n):
        b, s = n % DEPTH, n % CHUNKS
        if n >= Z_DEPTH:
            @pl.when(outer)
            def _():
                copy_z(n - Z_DEPTH, 2).wait_recv()

        copy_a(n, 0).wait_send()
        copy_a(n, 1).wait_send()
        copy_b(n, 0).wait_recv()
        part_sum[b, :, low_cols] = added(ring[s, core, y, x, :, low_cols], got_b[b, 0])
        copy_b(n, 1).wait_recv()
        part_sum[b, :, high_cols] = added(ring[s, core, y, x, :, high_cols], got_b[b, 1])

        @pl.when(outer)
        def _():
            copy_z(n, 0).start()

    def stage4(n):
        b = n % DEPTH
        copy_b(n, 0).wait_send()
        copy_b(n, 1).wait_send()

        @pl.when(outer)
        def _():
            copy_z(n, 0).wait_send()

        @pl.when(inner)
        def _():
            copy_z(n, 0).wait_recv()
            part_sum[b] = added(part_sum[b], got_z1[n % Z_DEPTH])
            copy_z(n, 1).start()

    def stage5(n):
        b = n % DEPTH

        @pl.when(inner)
        def _():
            if n >= DEPTH:
                copy_z(n - DEPTH, 2).wait_send()
            copy_z(n, 1).wait_recv()
            copy_z(n, 1).wait_send()
            total_ref[n] = added(part_sum[b], got_z2[b])
            copy_z(n, 2).start()

    stages = (stage0, stage1, stage2, stage3, stage4, stage5)

    def vcopy(at):
        src, dst, dev = (
            (vsend.at[other_core], vgot_d, here.to_c),
            (vsend.at[core, :, other_x], vgot_a, here.to_x),
            (vsend.at[core, other_y, x], vgot_b, here.to_y),
            (vsend.at[core, y, x], vgot_z1, here.to_z),
            (vsend.at[core, y, x], vgot_z2, to_mid),
            (vtotal_ref, vtotal_ref, here.to_z),
        )[at]
        return remote(src, dst, v_send.at[at], v_recv.at[at], dev)

    def vstage(at):
        if at == 0:
            share = width // 8
            lane = lax.broadcasted_iota(jnp.int32, (width, LANES), 1)
            column = lax.broadcasted_iota(jnp.int32, (width, LANES), 0)
            low = dvec[...].astype(BF16)
            for owner in range(8):
                pick = (column == lane + owner * share) & (lane < share)
                vsend[owner % 2, owner // 4, (owner // 2) % 2] = jnp.dot(
                    low, jnp.where(pick, 1.0, 0.0).astype(BF16), preferred_element_type=F32
                ).astype(BF16)
            vcopy(0).start()
        elif at == 1:
            vcopy(0).wait_recv()
            for i in range(4):
                vsend[core, i // 2, i % 2] = added(vsend[core, i // 2, i % 2], vgot_d[i // 2, i % 2])
            vcopy(1).start()
        elif at == 2:
            vcopy(1).wait_recv()
            for i in range(2):
                vsend[core, i, x] = added(vsend[core, i, x], vgot_a[i])
            vcopy(2).start()
        elif at == 3:
            vcopy(2).wait_recv()
            vsend[core, y, x] = added(vsend[core, y, x], vgot_b[...])

            @pl.when(outer)
            def _():
                vcopy(3).start()
        elif at == 4:
            @pl.when(inner)
            def _():
                vcopy(3).wait_recv()
                vsend[core, y, x] = added(vsend[core, y, x], vgot_z1[...])
                vcopy(4).start()
        elif at == 5:
            @pl.when(inner)
            def _():
                vcopy(4).wait_recv()
                vcopy(4).wait_send()
                vtotal_ref[...] = added(vsend[core, y, x], vgot_z2[...])
                vcopy(5).start()
                vcopy(5).wait_send()

            @pl.when(outer)
            def _():
                vcopy(3).wait_send()
                vcopy(5).wait_recv()

            for early in range(3):
                vcopy(early).wait_send()

    tile = 64
    half = tokens // 2

    def norm_back(layer, first_row, grad_in, scaled, inverse, grad_out, bias_row):
        base = 16 * layer
        gain = vec_ref[base + first_row : base + first_row + 1, :]

        def step(n, carry):
            rows = pl.ds(pl.multiple_of(n * tile, tile), tile)
            grad = grad_in[rows, :]
            hat = scaled[rows, :]
            lifted = grad * gain
            left = jnp.mean(lifted, axis=-1, keepdims=True)
            right = jnp.mean(lifted * hat, axis=-1, keepdims=True)
            result = inverse[rows, :1] * (lifted - left - hat * right)
            grad_out[rows, :] = result
            glow[rows, :] = result.astype(BF16)
            return (
                carry[0] + jnp.sum(grad * hat, axis=0, keepdims=True),
                carry[1] + jnp.sum(grad, axis=0, keepdims=True),
                carry[2] + jnp.sum(result, axis=0, keepdims=True),
            )

        nil = jnp.zeros((1, width), F32)
        sums = lax.fori_loop(0, tokens // tile, step, (nil, nil, nil))
        dvec[base + first_row : base + first_row + 1, :] = sums[0]
        dvec[base + first_row + 1 : base + first_row + 2, :] = sums[1]
        dvec[base + bias_row : base + bias_row + 1, :] = sums[2]

    def tn(left, right):
        return lax.dot_general(left, right, (((0,), (0,)), ((), ())), preferred_element_type=F32)

    def nt(left, right):
        return lax.dot_general(left, right, (((1,), (1,)), ((), ())), preferred_element_type=F32)

    def task0(layer):
        need(layer, "xh2", "r2")
        if layer == LAYERS - 1:
            grad_ref[...] = cot_ref[...].astype(F32)
        norm_back(layer, 10, grad_ref, xh2, r2, gtwo, 9)
        release(layer, "xh2", "r2")

    def task1(layer):
        need(layer, "active")
        rows_f = ff // 8

        def step(owner, carry):
            part = tn(active[:, pl.ds(pl.multiple_of(owner * rows_f, LANES), rows_f)], glow[...])
            oc, ox, oy = lax.rem(owner, 2), lax.rem(lax.div(owner, 2), 2), lax.div(owner, 4)
            for j in range(rows_f // rows_per):
                ring[j, oc, oy, ox] = part[j * rows_per : (j + 1) * rows_per].astype(BF16)
            return carry

        lax.fori_loop(0, 8, step, 0)
        release(layer, "active")

    def task2(layer, at, of):
        if at == 0:
            need(layer, "wb", "slope")
        cols_at = 256
        count = ff // cols_at // of

        def step(n, carry):
            cols = pl.ds(pl.multiple_of(n * cols_at, cols_at), cols_at)
            sums = jnp.zeros((1, cols_at), F32)
            for h in range(2):
                rows = slice(h * half, (h + 1) * half)
                inner_grad = (nt(glow[rows, :], wb[cols, :]) * slope[rows, cols].astype(F32)).astype(BF16)
                slope[rows, cols] = inner_grad
                sums = sums + jnp.sum(inner_grad.astype(F32), axis=0, keepdims=True)
            dbin[:, cols] = sums
            return carry

        lax.fori_loop(at * count, (at + 1) * count, step, 0)
        if at == of - 1:
            release(layer, "wb")
            for j in range(ff // width):
                dvec[16 * layer + 5 + j : 16 * layer + 6 + j, :] = dbin[:, j * width : (j + 1) * width]

    def weight_chunk(at, left, right):
        quarter = width // 2

        for iy in range(2):
            part = tn(left[:, iy * quarter : (iy + 1) * quarter], right)
            for i in range(4):
                ring[at, i % 2, iy, i // 2] = part[i * rows_per : (i + 1) * rows_per].astype(BF16)

    def task3(layer, j):
        if j == 0:
            need(layer, "flow")
        weight_chunk(4 + j, flow, slope[:, j * width : (j + 1) * width])
        if j == 3:
            release(layer, "flow")

    def task4(layer):
        need(layer, "wi", "xh1", "r1")

        def step(n, carry):
            rows = pl.ds(pl.multiple_of(n * half, half), half)
            for j in range(width // 256):
                cols = slice(j * 256, (j + 1) * 256)
                gtwo[rows, cols] = gtwo[rows, cols] + nt(slope[rows, :], wi[cols, :])
            return carry

        lax.fori_loop(0, 2, step, 0)
        norm_back(layer, 3, gtwo, xh1, r1, gtwo, 2)
        release(layer, "slope", "wi", "xh1", "r1")

    def task5(layer):
        need(layer, "att")
        weight_chunk(8, att, glow[...])

    def task6(layer):
        need(layer, "wo")

        def step(n, carry):
            rows = pl.ds(pl.multiple_of(n * half, half), half)
            for j in range(width // 256):
                cols = slice(j * 256, (j + 1) * 256)
                att[rows, cols] = nt(glow[rows, :], wo[cols, :]).astype(BF16)
            return carry

        lax.fori_loop(0, 2, step, 0)
        release(layer, "wo")

    def task7(layer, at, of):
        if at == 0:
            need(layer, "joined")
        count = rows_here // of
        base = 16 * layer

        def step(r, carry):
            rows = pl.ds(pl.multiple_of(r * ROW, ROW), ROW)
            first_head = lax.broadcasted_iota(jnp.int32, (ROW, LANES), 1) < HEAD_DIM
            seen = mask[pl.ds(r, 1)][0]
            seen = jnp.concatenate([seen, seen], axis=0) > 0.5

            def stacked(value):
                nil = jnp.zeros_like(value)
                return jnp.concatenate(
                    [jnp.where(first_head, value, nil), jnp.where(first_head, nil, value)], axis=0
                )

            for j in range(HEADS // 2):
                lanes = [slice(p * width + j * LANES, p * width + (j + 1) * LANES) for p in range(3)]
                query, keys, value = (joined[rows, lane] for lane in lanes)
                out_grad = stacked(att[rows, lanes[0]])
                both = stacked(query)
                scores = nt(both, keys) * HEAD_DIM ** (-0.5)
                scores = jnp.where(seen, scores, NEGATIVE)
                grown = jnp.exp(scores - jnp.max(scores, axis=-1, keepdims=True))
                probs = grown * (1.0 / jnp.sum(grown, axis=-1, keepdims=True))
                grad_value = tn(probs.astype(BF16), out_grad).astype(BF16)
                grad_probs = nt(out_grad, value)
                centre = jnp.sum(probs * grad_probs, axis=-1, keepdims=True)
                grad_scores = (probs * (grad_probs - centre)).astype(BF16)
                wide = jnp.dot(grad_scores, keys, preferred_element_type=F32)
                grad_query = jnp.where(first_head, wide[:ROW], wide[ROW:]) * HEAD_DIM ** (-0.5)
                grad_query = grad_query.astype(BF16)
                grad_key = (tn(grad_scores, both) * HEAD_DIM ** (-0.5)).astype(BF16)
                joined[rows, lanes[0]] = grad_query
                joined[rows, lanes[1]] = grad_key
                joined[rows, lanes[2]] = grad_value
                dvec[base : base + 1, lanes[0]] += jnp.sum(
                    grad_query.astype(F32), axis=0, keepdims=True
                )
                dvec[base + 1 : base + 2, lanes[0]] += jnp.sum(
                    grad_value.astype(F32), axis=0, keepdims=True
                )
            return carry

        lax.fori_loop(at * count, (at + 1) * count, step, 0)
        if at == of - 1:
            release(layer, "att")

    def task8(layer, j):
        if j == 0:
            need(layer, "hin")
        weight_chunk(9 + j, hin, joined[:, j * width : (j + 1) * width])
        if j == 2:
            release(layer, "hin")

    def task9(layer):
        need(layer, "wq")

        def step(n, carry):
            rows = pl.ds(pl.multiple_of(n * half, half), half)
            for j in range(width // 256):
                cols = slice(j * 256, (j + 1) * 256)
                grad_ref[rows, cols] = gtwo[rows, cols] + nt(joined[rows, :], wq[cols, :])
            return carry

        lax.fori_loop(0, 2, step, 0)
        release(layer, "joined", "wq")

    plan = {}
    for layer in range(LAYERS):
        start = 12 * (LAYERS - 1 - layer)
        plan[start - 2] = [(task0, layer)]
        plan[start - 1] = [(task1, layer)]
        plan[start] = [(task2, layer, 0, 2)]
        plan[start + 1] = [(task2, layer, 1, 2)]
        plan[start + 2] = [(task3, layer, 0), (task3, layer, 1)]
        plan[start + 3] = [(task3, layer, 2), (task3, layer, 3)]
        plan[start + 4] = [(task4, layer)]
        plan[start + 5] = [(task5, layer), (task6, layer)]
        plan[start + 6] = [(task7, layer, 0, 2)]
        plan[start + 7] = [(task7, layer, 1, 2)]
        plan[start + 8] = [(task8, layer, 0), (task8, layer, 1), (task8, layer, 2)]
        plan[start + 9] = [(task9, layer)]
    vector_from = 20
    for slot in range(-2, last_chunk + len(stages)):
        for at, stage in enumerate(stages):
            n = slot - at
            if 0 <= n < last_chunk:
                stage(n)
        if 0 <= slot - vector_from - 1 < 6:
            vstage(slot - vector_from - 1)
        for task, *what in plan.get(slot, ()):
            task(*what)

    for n in range(last_chunk - DEPTH, last_chunk):
        @pl.when(inner)
        def _(n=n):
            copy_z(n, 2).wait_send()

    for n in range(last_chunk - Z_DEPTH, last_chunk):
        @pl.when(outer)
        def _(n=n):
            copy_z(n, 2).wait_recv()


def backward(cotangent, segment_ids, vec, tokens, hlow, weights, kept):
    count, width = tokens.shape
    ff = weights[2].shape[2]
    rows_per = width // 8
    hbm = pl.BlockSpec(memory_space=pltpu.HBM)
    vmem = pl.BlockSpec(memory_space=pltpu.VMEM)
    small = vec.shape[0]
    out_shape = (
        jax.ShapeDtypeStruct((count, width), F32),
        jax.ShapeDtypeStruct((LAYERS * CHUNKS, rows_per, width), BF16),
        jax.ShapeDtypeStruct((small, LANES), BF16),
    )
    dma = pltpu.SemaphoreType.DMA
    z_sems = Z_DEPTH + DEPTH + LAYERS * CHUNKS
    scratch = [
        pltpu.VMEM((width, 3 * width), BF16), pltpu.VMEM((width, width), BF16),
        pltpu.VMEM((width, ff), BF16), pltpu.VMEM((ff, width), BF16),
        pltpu.VMEM((count, 3 * width), BF16), pltpu.VMEM((count, width), BF16),
        pltpu.VMEM((count, width), F32), pltpu.VMEM((count, LANES), F32),
        pltpu.VMEM((count, width), BF16), pltpu.VMEM((count, ff), BF16), pltpu.VMEM((count, ff), BF16),
        pltpu.VMEM((count, width), F32), pltpu.VMEM((count, LANES), F32),
        pltpu.VMEM((count, width), BF16),
        pltpu.VMEM((CHUNKS, 2, 2, 2, rows_per, width), BF16),
        pltpu.VMEM((DEPTH, 2, 2, rows_per, width), BF16),
        pltpu.VMEM((DEPTH, 2, 2, rows_per, width // 2), BF16),
        pltpu.VMEM((DEPTH, 2, rows_per, width // 2), BF16),
        pltpu.VMEM((Z_DEPTH, rows_per, width), BF16),
        pltpu.VMEM((DEPTH, rows_per, width), BF16),
        pltpu.VMEM((DEPTH, rows_per, width), BF16),
        pltpu.VMEM((count, width), F32), pltpu.VMEM((count, width), BF16),
        pltpu.VMEM((small, width), F32), pltpu.VMEM((1, ff), F32),
        pltpu.VMEM((segment_ids.shape[0], ROW, ROW), F32),
        pltpu.VMEM((2, 2, 2, small, LANES), BF16), pltpu.VMEM((2, 2, small, LANES), BF16),
        pltpu.VMEM((2, small, LANES), BF16), pltpu.VMEM((small, LANES), BF16),
        pltpu.VMEM((small, LANES), BF16), pltpu.VMEM((small, LANES), BF16),
        dma((14,)), dma((DEPTH,)), dma((DEPTH,)), dma((DEPTH, 2)), dma((DEPTH, 2)),
        dma((DEPTH, 2)), dma((DEPTH, 2)), dma((z_sems,)), dma((z_sems,)), dma((6,)), dma((6,)),
    ]
    return pl.pallas_call(
        backward_kernel,
        name="backward",
        out_shape=out_shape,
        in_specs=[vmem, vmem, vmem] + [hbm] * 15,
        out_specs=[vmem, vmem, vmem],
        scratch_shapes=scratch,
        compiler_params=pltpu.CompilerParams(
            collective_id=1, has_side_effects=True, vmem_limit_bytes=62 << 20
        ),
    )(cotangent, segment_ids, vec, tokens, hlow, *weights, *kept)


SLOTS = 4


def adam_rule(weight, gradient, moment_one, moment_two, step_rate):
    first_moment = BETA_FIRST * moment_one + (1.0 - BETA_FIRST) * gradient
    second_moment = BETA_SECOND * moment_two + (1.0 - BETA_SECOND) * gradient * gradient
    first_hat = first_moment / (1.0 - BETA_FIRST**STEP)
    second_hat = second_moment / (1.0 - BETA_SECOND**STEP)
    updated = weight - step_rate * (
        first_hat / (jnp.sqrt(second_hat) + ADAM_EPSILON) + WEIGHT_DECAY * weight
    )
    return updated, second_moment


def adam_kernel(
    total_ref, vtotal_ref, vectors_ref, vector_moments_ref, act_in, grad_in,
    q_w, o_w, i_w, b_w, q_m, o_m, i_m, b_m,
    act_out, grad_out, q_g, o_g, i_g, b_g, q_n, o_n, i_n, b_n, q_s, o_s, i_s, b_s, v_g, v_n, v_s,
    held, made, act_held, grad_held, in_sem, out_sem, pass_sem,
):
    rows, width = held.shape[2:]
    kinds = {
        "q": (q_w, q_m, (q_g, q_n, q_s)), "o": (o_w, o_m, (o_g, o_n, o_s)),
        "i": (i_w, i_m, (i_g, i_n, i_s)), "b": (b_w, b_m, (b_g, b_n, b_s)),
    }
    chunks = []
    for n in range(LAYERS * CHUNKS):
        layer, at = LAYERS - 1 - n // CHUNKS, n % CHUNKS
        if at < 4:
            place = ("b", layer, slice(at * rows, (at + 1) * rows), slice(0, width))
        elif at < 8:
            place = ("i", layer, slice(0, rows), slice((at - 4) * width, (at - 3) * width))
        elif at == 8:
            place = ("o", layer, slice(0, rows), slice(0, width))
        else:
            place = ("q", layer, slice(0, rows), slice((at - 9) * width, (at - 8) * width))
        chunks.append(place)

    def reads(n):
        kind, layer, r, c = chunks[n]
        weight, moments, _ = kinds[kind]
        b = n % SLOTS
        sources = (weight.at[layer, r, c], moments.at[0, layer, r, c], moments.at[1, layer, r, c])
        return [
            pltpu.make_async_copy(source, held.at[b, k], in_sem.at[b, k])
            for k, source in enumerate(sources)
        ]

    def writes(n):
        kind, layer, r, c = chunks[n]
        b = n % SLOTS
        return [
            pltpu.make_async_copy(made.at[b, k], target.at[layer, r, c], out_sem.at[b, k])
            for k, target in enumerate(kinds[kind][2])
        ]

    for n in range(SLOTS - 1):
        for copy in reads(n):
            copy.start()
    passing = (
        pltpu.make_async_copy(act_in, act_held, pass_sem.at[0]),
        pltpu.make_async_copy(grad_in, grad_held, pass_sem.at[1]),
    )
    passed = (
        pltpu.make_async_copy(act_held, act_out, pass_sem.at[2]),
        pltpu.make_async_copy(grad_held, grad_out, pass_sem.at[3]),
    )
    for copy in passing:
        copy.start()
    share = vectors_ref.shape[2]
    for layer in range(LAYERS):
        gradient = vtotal_ref[16 * layer : 16 * layer + 12, :share].astype(F32)
        updated, second = adam_rule(
            vectors_ref[:, layer, :], gradient, vector_moments_ref[0, :, layer, :],
            vector_moments_ref[1, :, layer, :], RATE_VECTOR,
        )
        v_g[:, layer, :] = gradient
        v_n[:, layer, :] = updated
        v_s[:, layer, :] = second
    tile = 32
    for n in range(LAYERS * CHUNKS):
        b = n % SLOTS
        if n == SLOTS:
            for early, late in zip(passing, passed):
                early.wait()
                late.start()
        if n + SLOTS - 1 < LAYERS * CHUNKS:
            for copy in reads(n + SLOTS - 1):
                copy.start()
        for copy in reads(n):
            copy.wait()
        if n >= SLOTS:
            for copy in writes(n - SLOTS):
                copy.wait()

        def step(t, carry, n=n, b=b):
            r = pl.ds(pl.multiple_of(t * tile, tile), tile)
            gradient = total_ref[n, r, :].astype(F32)
            updated, second = adam_rule(
                held[b, 0, r, :], gradient, held[b, 1, r, :], held[b, 2, r, :], RATE_MATRIX
            )
            made[b, 0, r, :] = gradient
            made[b, 1, r, :] = updated
            made[b, 2, r, :] = second
            return carry

        lax.fori_loop(0, rows // tile, step, 0)
        for copy in writes(n):
            copy.start()
    for n in range(LAYERS * CHUNKS - SLOTS, LAYERS * CHUNKS):
        for copy in writes(n):
            copy.wait()
    for copy in passed:
        copy.wait()


def adam(activations, grad, total, vtotal, masters, moments):
    rows, width = total.shape[1:]
    hbm = pl.BlockSpec(memory_space=pltpu.HBM)
    vmem = pl.BlockSpec(memory_space=pltpu.VMEM)
    matrices, vectors = masters[:4], masters[4].transpose(1, 0, 2)
    passed = [jax.ShapeDtypeStruct(p.shape, p.dtype) for p in (activations, grad)]
    matrix_shapes = [jax.ShapeDtypeStruct(m.shape, F32) for m in matrices]
    vector_shape = jax.ShapeDtypeStruct(vectors.shape, F32)
    out = pl.pallas_call(
        adam_kernel,
        name="adam",
        out_shape=passed + matrix_shapes * 3 + [vector_shape] * 3,
        in_specs=[vmem] * 4 + [hbm] * 10,
        out_specs=[hbm] * 14 + [vmem] * 3,
        scratch_shapes=[
            pltpu.VMEM((SLOTS, 3, rows, width), F32), pltpu.VMEM((SLOTS, 3, rows, width), F32),
            pltpu.VMEM(activations.shape, BF16), pltpu.VMEM(grad.shape, F32),
            pltpu.SemaphoreType.DMA((SLOTS, 3)), pltpu.SemaphoreType.DMA((SLOTS, 3)),
            pltpu.SemaphoreType.DMA((4,)),
        ],
        compiler_params=pltpu.CompilerParams(vmem_limit_bytes=62 << 20),
    )(
        total, vtotal, vectors, moments[4].transpose(0, 2, 1, 3), activations, grad, *matrices,
        *moments[:4],
    )
    gradients, updates, states = out[2:6], out[6:10], out[10:14]
    vector_outs = [v.transpose(1, 0, 2) for v in out[14:]]
    return (
        out[0], out[1], *gradients, vector_outs[0], *updates, vector_outs[1], *states, vector_outs[2]
    )


def norm_forward(values, gain_row, shift_row):
    centered = values - jnp.mean(values, axis=-1, keepdims=True)
    inverse = lax.rsqrt(jnp.mean(centered * centered, axis=-1, keepdims=True) + EPSILON)
    scaled = centered * inverse
    return (scaled * gain_row + shift_row, scaled, inverse)


def norm_backward(grad_out, scaled, inverse, gain_row):
    grad_scaled = grad_out * gain_row
    grad_in = inverse * (
        grad_scaled
        - jnp.mean(grad_scaled, axis=-1, keepdims=True)
        - scaled * jnp.mean(grad_scaled * scaled, axis=-1, keepdims=True)
    )
    return (grad_in, jnp.sum(grad_out * scaled, axis=0), jnp.sum(grad_out, axis=0))


def score_block(queries, key_rows, same_segment):
    scores = jnp.einsum(
        "rqhe,rkhe->rhqk", queries, key_rows, preferred_element_type=jnp.float32
    ) * HEAD_DIM ** (-0.5)
    return jnp.where(same_segment, scores, NEGATIVE)


def layer_forward(hidden, same_segment, weights):
    qkv_used, out_used, in_used, back_used, vector_low = weights
    vector = vector_low.astype(jnp.float32)
    row_count = same_segment.shape[0]
    model_width = out_used.shape[0]
    hidden_low = hidden.astype(jnp.bfloat16)
    bias_qkv = jnp.concatenate([vector[0], jnp.zeros_like(vector[0]), vector[1]])
    joined = (jnp.dot(hidden_low, qkv_used, preferred_element_type=jnp.float32) + bias_qkv).astype(
        jnp.bfloat16
    )
    split_qkv = joined.reshape(row_count, -1, 3, HEADS, HEAD_DIM)
    scores = score_block(split_qkv[:, :, 0], split_qkv[:, :, 1], same_segment)
    row_top = jnp.max(scores, axis=-1, keepdims=True)
    log_total = row_top + jnp.log(jnp.sum(jnp.exp(scores - row_top), axis=-1, keepdims=True))
    prob_low = jnp.exp(scores - log_total).astype(jnp.bfloat16)
    attended = jnp.einsum(
        "rhqk,rkhe->rqhe", prob_low, split_qkv[:, :, 2], preferred_element_type=jnp.float32
    )
    attended_low = attended.reshape(-1, model_width).astype(jnp.bfloat16)
    branch = jnp.dot(attended_low, out_used, preferred_element_type=jnp.float32) + vector[2]
    first_norm, scaled_one, inverse_one = norm_forward(hidden + branch, vector[3], vector[4])
    first_low = first_norm.astype(jnp.bfloat16)
    inner_pre = jnp.dot(first_low, in_used, preferred_element_type=jnp.float32) + vector[
        5:9
    ].reshape(-1)
    active_low = jax.nn.gelu(inner_pre, approximate=False).astype(jnp.bfloat16)
    outer_out = jnp.dot(active_low, back_used, preferred_element_type=jnp.float32) + vector[9]
    output, scaled_two, inverse_two = norm_forward(first_norm + outer_out, vector[10], vector[11])
    kept_state = (
        hidden_low,
        joined,
        log_total,
        attended_low,
        scaled_one,
        inverse_one,
        first_low,
        inner_pre,
        active_low,
        scaled_two,
        inverse_two,
    )
    return (output, kept_state)


def layer_backward(grad_out, same_segment, weights, kept_state):
    qkv_used, out_used, in_used, back_used, vector_low = weights
    vector = vector_low.astype(jnp.float32)
    (
        hidden_low,
        joined,
        log_total,
        attended_low,
        scaled_one,
        inverse_one,
        first_low,
        inner_pre,
        active_low,
        scaled_two,
        inverse_two,
    ) = kept_state
    row_count = same_segment.shape[0]
    model_width = out_used.shape[0]
    grad_two, gain_two_grad, shift_two_grad = norm_backward(
        grad_out, scaled_two, inverse_two, vector[10]
    )
    grad_outer = grad_two.astype(jnp.bfloat16)
    back_bias_grad = jnp.sum(grad_two, axis=0)
    back_weight_grad = jnp.einsum(
        "tf,td->fd", active_low, grad_outer, preferred_element_type=jnp.float32
    )
    grad_active = jnp.einsum("td,fd->tf", grad_outer, back_used, preferred_element_type=jnp.float32)
    gelu_value, gelu_pull = jax.vjp(
        lambda values: jax.nn.gelu(values, approximate=False), inner_pre
    )
    grad_inner = gelu_pull(grad_active)[0].astype(jnp.bfloat16)
    in_bias_grad = jnp.sum(grad_inner, axis=0, dtype=jnp.float32)
    in_weight_grad = jnp.einsum(
        "td,tf->df", first_low, grad_inner, preferred_element_type=jnp.float32
    )
    grad_first = grad_two + jnp.einsum(
        "tf,df->td", grad_inner, in_used, preferred_element_type=jnp.float32
    )
    grad_one, gain_one_grad, shift_one_grad = norm_backward(
        grad_first, scaled_one, inverse_one, vector[3]
    )
    grad_branch = grad_one.astype(jnp.bfloat16)
    out_bias_grad = jnp.sum(grad_one, axis=0)
    out_weight_grad = jnp.einsum(
        "td,te->de", attended_low, grad_branch, preferred_element_type=jnp.float32
    )
    grad_mixed = jnp.einsum("te,de->td", grad_branch, out_used, preferred_element_type=jnp.float32)
    grad_mixed = grad_mixed.astype(jnp.bfloat16).reshape(row_count, -1, HEADS, HEAD_DIM)
    split_qkv = joined.reshape(row_count, -1, 3, HEADS, HEAD_DIM)
    queries = split_qkv[:, :, 0]
    key_rows = split_qkv[:, :, 1]
    value_rows = split_qkv[:, :, 2]
    prob_full = jnp.exp(score_block(queries, key_rows, same_segment) - log_total)
    prob_low = prob_full.astype(jnp.bfloat16)
    grad_values = jnp.einsum(
        "rhqk,rqhe->rkhe", prob_low, grad_mixed, preferred_element_type=jnp.float32
    )
    grad_probs = jnp.einsum(
        "rqhe,rkhe->rhqk", grad_mixed, value_rows, preferred_element_type=jnp.float32
    )
    centred = jnp.sum(prob_full * grad_probs, axis=-1, keepdims=True)
    grad_scores = (prob_full * (grad_probs - centred)).astype(jnp.bfloat16)
    grad_queries = jnp.einsum(
        "rhqk,rkhe->rqhe", grad_scores, key_rows, preferred_element_type=jnp.float32
    ) * HEAD_DIM ** (-0.5)
    grad_keys = jnp.einsum(
        "rhqk,rqhe->rkhe", grad_scores, queries, preferred_element_type=jnp.float32
    ) * HEAD_DIM ** (-0.5)
    grad_joined = (
        jnp.stack([grad_queries, grad_keys, grad_values], axis=2)
        .reshape(-1, 3 * model_width)
        .astype(jnp.bfloat16)
    )
    qkv_bias_grad = jnp.sum(grad_joined, axis=0, dtype=jnp.float32)
    qkv_weight_grad = jnp.einsum(
        "td,tc->dc", hidden_low, grad_joined, preferred_element_type=jnp.float32
    )
    grad_hidden = grad_one + jnp.einsum(
        "tc,dc->td", grad_joined, qkv_used, preferred_element_type=jnp.float32
    )
    vector_grad = jnp.concatenate(
        [
            qkv_bias_grad[:model_width][None],
            qkv_bias_grad[2 * model_width :][None],
            out_bias_grad[None],
            gain_one_grad[None],
            shift_one_grad[None],
            in_bias_grad.reshape(4, model_width),
            back_bias_grad[None],
            gain_two_grad[None],
            shift_two_grad[None],
        ],
        axis=0,
    )
    return (
        grad_hidden,
        (qkv_weight_grad, out_weight_grad, in_weight_grad, back_weight_grad, vector_grad),
    )


def adam_step(weight, gradient, moment_one, moment_two, step_rate):
    first_moment = BETA_FIRST * moment_one + (1.0 - BETA_FIRST) * gradient
    second_moment = BETA_SECOND * moment_two + (1.0 - BETA_SECOND) * gradient * gradient
    first_hat = first_moment / (1.0 - BETA_FIRST**STEP)
    second_hat = second_moment / (1.0 - BETA_SECOND**STEP)
    updated = weight - step_rate * (
        first_hat / (jnp.sqrt(second_hat) + ADAM_EPSILON) + WEIGHT_DECAY * weight
    )
    return gradient, updated, second_moment


def update_layer(summed, masters, moments, layer_at):
    outcome = []
    for kind_at in range(5):
        step_rate = RATE_VECTOR if kind_at == 4 else RATE_MATRIX
        outcome.append(
            adam_step(
                masters[kind_at][layer_at],
                summed[kind_at],
                moments[kind_at][0, layer_at],
                moments[kind_at][1, layer_at],
                step_rate,
            )
        )
    return outcome


def local_parts(masters, layer_at):
    return tuple((master[layer_at].astype(jnp.bfloat16) for master in masters))


def collect(results, kind_at, member):
    return jnp.stack([layer_result[kind_at][member] for layer_result in results])


def on_device_any(
    tokens,
    segment_ids,
    cotangent,
    qkv_weight,
    out_weight,
    in_weight,
    back_weight,
    vectors,
    qkv_moments,
    out_moments,
    in_moments,
    back_moments,
    vector_moments,
):
    masters = (qkv_weight, out_weight, in_weight, back_weight, vectors)
    moments = (qkv_moments, out_moments, in_moments, back_moments, vector_moments)
    same_segment = (segment_ids[:, :, None] == segment_ids[:, None, :])[:, None]
    hidden = tokens.astype(jnp.float32)
    saved_states = []
    for layer_at in range(LAYERS):
        parts_now = local_parts(masters, layer_at)
        weights = (
            lax.all_gather(parts_now[0], "fsdp", axis=0, tiled=True),
            lax.all_gather(parts_now[1], "fsdp", axis=0, tiled=True),
            lax.all_gather(parts_now[2], "fsdp", axis=0, tiled=True),
            lax.all_gather(parts_now[3], "fsdp", axis=0, tiled=True),
            lax.all_gather(parts_now[4], "fsdp", axis=1, tiled=True),
        )
        hidden, kept_state = layer_forward(hidden, same_segment, weights)
        saved_states.append(kept_state)
    activations = hidden.astype(jnp.bfloat16)
    grad_hidden = cotangent.astype(jnp.float32)
    results = [None] * LAYERS
    for layer_at in reversed(range(LAYERS)):
        parts_now = local_parts(masters, layer_at)
        weights = (
            lax.all_gather(parts_now[0], "fsdp", axis=0, tiled=True),
            lax.all_gather(parts_now[1], "fsdp", axis=0, tiled=True),
            lax.all_gather(parts_now[2], "fsdp", axis=0, tiled=True),
            lax.all_gather(parts_now[3], "fsdp", axis=0, tiled=True),
            lax.all_gather(parts_now[4], "fsdp", axis=1, tiled=True),
        )
        grad_hidden, weight_grads = layer_backward(
            grad_hidden, same_segment, weights, saved_states[layer_at]
        )
        shards = (
            lax.psum_scatter(
                weight_grads[0].astype(jnp.bfloat16), "fsdp", scatter_dimension=0, tiled=True
            ).astype(jnp.float32),
            lax.psum_scatter(
                weight_grads[1].astype(jnp.bfloat16), "fsdp", scatter_dimension=0, tiled=True
            ).astype(jnp.float32),
            lax.psum_scatter(
                weight_grads[2].astype(jnp.bfloat16), "fsdp", scatter_dimension=0, tiled=True
            ).astype(jnp.float32),
            lax.psum_scatter(
                weight_grads[3].astype(jnp.bfloat16), "fsdp", scatter_dimension=0, tiled=True
            ).astype(jnp.float32),
            lax.psum_scatter(
                weight_grads[4].astype(jnp.bfloat16), "fsdp", scatter_dimension=1, tiled=True
            ).astype(jnp.float32),
        )
        totals = (
            lax.psum(shards[0].astype(jnp.bfloat16), "dp").astype(jnp.float32),
            lax.psum(shards[1].astype(jnp.bfloat16), "dp").astype(jnp.float32),
            lax.psum(shards[2].astype(jnp.bfloat16), "dp").astype(jnp.float32),
            lax.psum(shards[3].astype(jnp.bfloat16), "dp").astype(jnp.float32),
            lax.psum(shards[4].astype(jnp.bfloat16), "dp").astype(jnp.float32),
        )
        results[layer_at] = update_layer(totals, masters, moments, layer_at)
    return (
        activations,
        grad_hidden,
        collect(results, 0, 0),
        collect(results, 1, 0),
        collect(results, 2, 0),
        collect(results, 3, 0),
        collect(results, 4, 0),
        collect(results, 0, 1),
        collect(results, 1, 1),
        collect(results, 2, 1),
        collect(results, 3, 1),
        collect(results, 4, 1),
        collect(results, 0, 2),
        collect(results, 1, 2),
        collect(results, 2, 2),
        collect(results, 3, 2),
        collect(results, 4, 2),
    )


def on_device(
    tokens,
    segment_ids,
    cotangent,
    qkv_weight,
    out_weight,
    in_weight,
    back_weight,
    vectors,
    qkv_moments,
    out_moments,
    in_moments,
    back_moments,
    vector_moments,
):
    masters = (qkv_weight, out_weight, in_weight, back_weight, vectors)
    moments = (qkv_moments, out_moments, in_moments, back_moments, vector_moments)
    activations, wq, wo, wi, wb, vec, *kept, hlow = forward(
        tokens, segment_ids, vectors.transpose(1, 0, 2), *masters[:4]
    )
    grad, total, vtotal = backward(
        cotangent, segment_ids, vec, tokens, hlow, (wq, wo, wi, wb), kept
    )
    return adam(activations, grad, total, vtotal, masters, moments)


def solution(mesh):
    in_specs = (
        P(("fsdp", "dp"), None),
        P(("fsdp", "dp"), None),
        P(("fsdp", "dp"), None),
        P(None, "fsdp", None),
        P(None, "fsdp", None),
        P(None, "fsdp", None),
        P(None, "fsdp", None),
        P(None, None, "fsdp"),
        P(None, None, "fsdp", None),
        P(None, None, "fsdp", None),
        P(None, None, "fsdp", None),
        P(None, None, "fsdp", None),
        P(None, None, None, "fsdp"),
    )
    out_specs = (
        P(("fsdp", "dp"), None),
        P(("fsdp", "dp"), None),
        P(None, "fsdp", None),
        P(None, "fsdp", None),
        P(None, "fsdp", None),
        P(None, "fsdp", None),
        P(None, None, "fsdp"),
        P(None, "fsdp", None),
        P(None, "fsdp", None),
        P(None, "fsdp", None),
        P(None, "fsdp", None),
        P(None, None, "fsdp"),
        P(None, "fsdp", None),
        P(None, "fsdp", None),
        P(None, "fsdp", None),
        P(None, "fsdp", None),
        P(None, None, "fsdp"),
    )
    body = on_device if dict(mesh.shape) == {"fsdp": 8, "dp": 4} else on_device_any
    return jax.shard_map(
        body, mesh=mesh, in_specs=in_specs, out_specs=out_specs, check_vma=False
    )
```

```python
import jax
import jax.numpy as jnp
from jax import lax
from jax.experimental import pallas as pl
from jax.experimental.pallas import tpu as pltpu
from jax.sharding import PartitionSpec as P

HEADS = 12
HEAD_DIM = 64
LAYERS = 2
STEP = 3
ROW = 128
LANES = 128

EPSILON = 1e-05
NEGATIVE = -1000000000.0
BETA_FIRST = 0.5
BETA_SECOND = 0.5
WEIGHT_DECAY = 0.01
ADAM_EPSILON = 1e-08
RATE_MATRIX = 0.06
RATE_VECTOR = 0.5
MESH_ID = pl.DeviceIdType.MESH
BF16 = jnp.bfloat16
F32 = jnp.float32


class Place:
    def __init__(self):
        f = lax.axis_index("fsdp")
        z = lax.axis_index("dp")
        core = lax.rem(f, 2)
        x = lax.rem(lax.div(f, 2), 2)
        y = lax.div(f, 4)
        self.f, self.z, self.core, self.x, self.y = f, z, core, x, y
        self.fc = f + 1 - 2 * core
        self.fx = f + 2 - 4 * x
        self.fy = f + 4 - 8 * y
        self.fd = self.fx + 4 - 8 * y
        self.q = lax.rem(z, 2)
        self.to_c = {"fsdp": self.fc}
        self.to_x = {"fsdp": self.fx}
        self.to_y = {"fsdp": self.fy}
        self.to_z = {"dp": z + 1 - 2 * self.q}


def greet(partners):
    barrier = pltpu.get_barrier_semaphore()
    for partner in partners:
        pl.semaphore_signal(barrier, inc=1, device_id=partner, device_id_type=MESH_ID)
    pl.semaphore_wait(barrier, len(partners))


def norm_rows(values, gain_row, shift_row):
    centered = values - jnp.mean(values, axis=-1, keepdims=True)
    inverse = lax.rsqrt(jnp.mean(centered * centered, axis=-1, keepdims=True) + EPSILON)
    scaled = centered * inverse
    return scaled * gain_row + shift_row, scaled, inverse


def gelu_pair(value):
    cdf = 0.5 * (1.0 + lax.erf(value * 0.7071067811865476))
    slope = cdf + value * (0.3989422804014327 * jnp.exp(-0.5 * value * value))
    return value * cdf, slope


SPLITS = (3, 1, 2, 4)
COPY_KINDS = 14
VEC_KINDS = 7


def gather_pieces(shards):
    pieces = []
    for layer in range(LAYERS):
        for kind, (rows, cols) in enumerate(shards):
            count = SPLITS[kind]
            for i in range(count):
                if kind == 3:
                    pieces.append((layer, kind, i * rows // count, rows // count, 0, cols))
                else:
                    pieces.append((layer, kind, 0, rows, i * cols // count, cols // count))
    return pieces


ORDER = (
    ("own", 0), ("own", 1), ("own", 2), ("pre", 0), ("own", 3), ("pre", 1), ("own", 4), ("pre", 2),
    ("s1", 0), ("s1", 1), ("s1", 2), ("s1", 3), ("own", 5), ("s1", 4), ("s2", 0), ("s2", 1), ("s2", 2),
    ("own", 6), ("s2", 3), ("own", 7), ("s3", 0), ("own", 8), ("s3", 1), ("s1", 5), ("s4", 0),
    ("qkv", 0, 0), ("s3", 2), ("s4", 1), ("qkv", 0, 1), ("s2", 4), ("s3", 3), ("s4", 2), ("qkv", 0, 2),
    ("att", 0, 0), ("own", 9), ("s1", 6), ("att", 0, 1), ("s1", 7), ("att", 0, 2), ("own", 10),
    ("att", 0, 3), ("s1", 8), ("s3", 4), ("s4", 3), ("out", 0, 0), ("s2", 5), ("out", 0, 1),
    ("own", 11), ("s4", 4), ("in", 0, 0), ("own", 12), ("s1", 9), ("s2", 6), ("s2", 7), ("in", 0, 1),
    ("own", 13), ("s1", 10), ("s3", 5), ("s2", 8), ("s4", 5), ("in", 0, 2), ("own", 14), ("s1", 11),
    ("s3", 6), ("s3", 7), ("in", 0, 3), ("s1", 12), ("s2", 9), ("s3", 8), ("s4", 6), ("s4", 7),
    ("s1", 13), ("s4", 8), ("s2", 10), ("own", 15), ("s3", 9), ("s1", 14), ("s4", 9), ("back", 0, 0),
    ("s2", 11), ("back", 0, 1), ("own", 16), ("s2", 12), ("s2", 13), ("s3", 10), ("own", 17),
    ("s4", 10), ("qkv", 1, 0), ("own", 18), ("s3", 11), ("s1", 15), ("s3", 12), ("s4", 11),
    ("qkv", 1, 1), ("s2", 14), ("s3", 13), ("s4", 12), ("qkv", 1, 2), ("att", 1, 0), ("own", 19),
    ("s1", 16), ("att", 1, 1), ("att", 1, 2), ("s1", 17), ("att", 1, 3), ("s1", 18), ("s3", 14),
    ("s4", 13), ("out", 1, 0), ("out", 1, 1), ("s2", 15), ("s4", 14), ("in", 1, 0), ("s1", 19),
    ("s2", 16), ("in", 1, 1), ("s2", 17), ("s2", 18), ("s3", 15), ("s2", 19), ("s4", 15), ("in", 1, 2),
    ("s3", 16), ("in", 1, 3), ("s3", 17), ("s3", 18), ("s4", 16), ("s3", 19), ("s4", 17), ("s4", 18),
    ("s4", 19), ("back", 1, 0), ("back", 1, 1),
)


def forward_kernel(
    tok_ref, seg_ref, vec_ref, q_w, o_w, i_w, b_w,
    act_out, wq_out, wo_out, wi_out, wb_out, vec_out,
    joined_out, att_out, xh1_out, r1_out, flow_out, active_out, slope_out, xh2_out, r2_out, hlow_out,
    wq0, wo0, wi0, wb0, wq1, wo1, wi1, wb1, st_q, st_o, st_i, st_b, vslots, vec,
    hid, hlow, joined, att, first, xh1, r1, flow, active, slope, xh2, r2, mask,
    send_sem, recv_sem, own_sem, wout_sem, save_sem,
):
    here = Place()
    masters = (q_w, o_w, i_w, b_w)
    stages = (st_q, st_o, st_i, st_b)
    bufs = ((wq0, wo0, wi0, wb0), (wq1, wo1, wi1, wb1))
    wouts = (wq_out, wo_out, wi_out, wb_out)
    f, fx, fy, fd = here.f, here.fx, here.fy, here.fd
    pieces = gather_pieces([m.shape[1:] for m in masters])
    tokens, width = hid.shape
    half = tokens // 2

    def stage_copy(layer, kind):
        return pltpu.make_async_copy(
            masters[kind].at[layer], stages[kind].at[layer], own_sem.at[4 * layer + kind]
        )

    for layer in range(LAYERS):
        for kind in range(4):
            stage_copy(layer, kind).start()
    mine = jnp.zeros((1,) + vslots.shape[1:], BF16)
    vslots[pl.ds(f, 1)] = mine
    share = vec_ref.shape[2]
    for layer in range(LAYERS):
        vslots[pl.ds(f, 1), 16 * layer : 16 * layer + 12, :share] = vec_ref[:, layer, :].astype(BF16)[None]
    greet((here.to_c, here.to_x, here.to_y, here.to_z))

    started = []
    copies = {}

    def make(p, kind):
        layer, matrix, row_at, rows, col_at, cols = pieces[p]
        buf = bufs[layer][matrix]
        shard_rows = masters[matrix].shape[1]
        third = cols // 3
        two = 2 * third
        c_xy = pl.multiple_of(col_at + here.q * third, LANES)
        c_b = pl.multiple_of(c_xy + third, LANES)
        c_z = pl.multiple_of(col_at + here.q * two, LANES)
        c_w = pl.multiple_of(col_at + (1 - here.q) * two, LANES)

        def win(owner, col, wide):
            at = pl.multiple_of(owner * shard_rows + row_at, 32)
            return buf.at[pl.ds(at, rows), pl.ds(col, wide)]

        owner, col, wide, device = (
            (f, col_at, cols, here.to_c), (f, c_xy, two, here.to_x), (f, c_xy, two, here.to_y),
            (fx, c_xy, two, here.to_c), (fx, c_xy, third, here.to_y), (fx, c_z, third, here.to_z),
            (fy, c_xy, two, here.to_c), (fy, c_b, third, here.to_x), (fy, c_z, third, here.to_z),
            (fd, c_xy, two, here.to_c), (fd, c_z, third, here.to_z),
            (fx, c_w, third, here.to_c), (fy, c_w, third, here.to_c), (fd, c_w, third, here.to_c),
        )[kind]
        window = win(owner, col, wide)
        slot = p * COPY_KINDS + kind
        return pltpu.make_async_remote_copy(
            src_ref=window, dst_ref=window, send_sem=send_sem.at[slot], recv_sem=recv_sem.at[slot],
            device_id=device, device_id_type=MESH_ID,
        )

    def start(p, *kinds):
        for kind in kinds:
            copy = make(p, kind)
            copy.start()
            copies[p, kind] = copy
            started.append(copy)

    def arrived(p, *kinds):
        for kind in kinds:
            copies[p, kind].wait_recv()

    def send_own(p):
        layer, matrix, row_at, rows, col_at, cols = pieces[p]
        if row_at == 0 and col_at == 0:
            stage_copy(layer, matrix).wait()
        stage, buf = stages[matrix], bufs[layer][matrix]
        shard_rows = stage.shape[1]
        tile = 32

        def step(n, carry):
            at = pl.multiple_of(row_at + n * tile, tile)
            to = pl.multiple_of(f * shard_rows + row_at + n * tile, tile)
            buf[pl.ds(to, tile), col_at : col_at + cols] = stage[
                layer, pl.ds(at, tile), col_at : col_at + cols
            ].astype(BF16)
            return carry

        lax.fori_loop(0, rows // tile, step, 0)
        start(p, 1, 2, 0)

    wcopies = []

    def comm(what, p):
        if what == "own":
            send_own(p)
        elif what == "s1":
            arrived(p, 1, 2)
            start(p, 4, 7, 5, 8, 3, 6)
        elif what == "s2":
            arrived(p, 4, 7)
            start(p, 10, 9)
        elif what == "s3":
            arrived(p, 5, 8, 10)
            start(p, 11, 12, 13)
        else:
            arrived(p, 0, 3, 6, 9, 11, 12, 13)
            layer, matrix = pieces[p][:2]
            if p + 1 == len(pieces) or pieces[p + 1][1] != matrix:
                copy = pltpu.make_async_copy(
                    bufs[layer][matrix], wouts[matrix].at[layer], wout_sem.at[4 * layer + matrix]
                )
                copy.start()
                wcopies.append(copy)

    def vcopy(kind):
        owner, dev = (
            (f, here.to_x), (f, here.to_y), (f, here.to_c),
            (fx, here.to_y), (fx, here.to_c), (fy, here.to_c), (fd, here.to_c),
        )[kind]
        slot = len(pieces) * COPY_KINDS + kind
        return pltpu.make_async_remote_copy(
            src_ref=vslots.at[owner], dst_ref=vslots.at[owner], send_sem=send_sem.at[slot],
            recv_sem=recv_sem.at[slot], device_id=dev, device_id_type=MESH_ID,
        )

    vc = [vcopy(kind) for kind in range(VEC_KINDS)]
    started.extend(vc)
    for kind in (0, 1, 2):
        vc[kind].start()
    rows_here = seg_ref.shape[0]

    def prepare(step):
        if step == 0:
            for r in range(rows_here):
                wide = jnp.broadcast_to(seg_ref[r : r + 1, :].astype(F32), (ROW, ROW))
                mask[r] = jnp.where(wide == wide.T, 1.0, 0.0)
            vc[0].wait_recv()
            vc[1].wait_recv()
            for kind in (3, 4, 5):
                vc[kind].start()
        elif step == 1:
            vc[3].wait_recv()
            vc[6].start()
        else:
            for kind in (2, 4, 5, 6):
                vc[kind].wait_recv()
            lane = lax.broadcasted_iota(jnp.int32, (LANES, width), 0)
            column = lax.broadcasted_iota(jnp.int32, (LANES, width), 1)
            whole = jnp.zeros(vec.shape, F32)
            for owner in range(8):
                pick = (column == lane + owner * share) & (lane < share)
                whole = whole + jnp.dot(
                    vslots[owner], jnp.where(pick, 1.0, 0.0).astype(BF16),
                    preferred_element_type=F32,
                )
            vec[...] = whole

    saves = {}

    def save(layer, at, src, dst):
        copy = pltpu.make_async_copy(src, dst, save_sem.at[layer, at])
        copy.start()
        saves[layer, at] = copy

    def saved(layer, *ats):
        if layer >= 0:
            for at in ats:
                saves[layer, at].wait()

    def row(layer, at):
        return vec[16 * layer + at : 16 * layer + at + 1, :]

    def qkv(layer, part):
        low_ref, wq = (tok_ref if layer == 0 else hlow), bufs[layer][0]
        if part == 0:
            saved(layer - 1, 0)
        cols = slice(part * width, (part + 1) * width)

        def step(n, carry):
            rows = pl.ds(pl.multiple_of(n * half, half), half)
            acc = jnp.dot(low_ref[rows, :], wq[:, cols], preferred_element_type=F32)
            if part != 1:
                acc = acc + row(layer, part // 2)
            joined[rows, cols] = acc.astype(BF16)
            return carry

        lax.fori_loop(0, 2, step, 0)
        if part == 2:
            save(layer, 0, joined, joined_out.at[layer])

    def attend(layer, r):
        if r == 0:
            saved(layer - 1, 1)
        rows = slice(r * ROW, (r + 1) * ROW)
        first_head = lax.broadcasted_iota(jnp.int32, (ROW, LANES), 1) < HEAD_DIM
        seen = mask[r]
        seen = jnp.concatenate([seen, seen], axis=1) > 0.5
        group = 3
        for at in range(0, HEADS // 2, group):
            lanes = [
                [slice(p * width + j * LANES, p * width + (j + 1) * LANES) for p in range(3)]
                for j in range(at, at + group)
            ]
            query, keys, value = ([joined[rows, lane[p]] for lane in lanes] for p in range(3))
            both = [
                jnp.concatenate(
                    [jnp.where(first_head, q, jnp.zeros_like(q)), jnp.where(first_head, jnp.zeros_like(q), q)],
                    axis=0,
                )
                for q in query
            ]
            scores = [
                lax.dot_general(k, q, (((1,), (1,)), ((), ())), preferred_element_type=F32)
                for k, q in zip(keys, both)
            ]
            scores = [jnp.where(seen, s * HEAD_DIM ** (-0.5), NEGATIVE) for s in scores]
            grown = [jnp.exp(s - jnp.max(s, axis=0, keepdims=True)) for s in scores]
            probs = [
                (e * (1.0 / jnp.sum(e, axis=0, keepdims=True))).astype(BF16) for e in grown
            ]
            mixed = [
                lax.dot_general(p, v, (((0,), (0,)), ((), ())), preferred_element_type=F32)
                for p, v in zip(probs, value)
            ]
            for m, lane in zip(mixed, lanes):
                att[rows, lane[0]] = jnp.where(first_head, m[:ROW], m[ROW:]).astype(BF16)
        if r == rows_here - 1:
            save(layer, 1, att, att_out.at[layer])

    norm_tile = 64

    def out_half(layer, h):
        wo = bufs[layer][1]
        if h == 0:
            saved(layer - 1, 2, 3, 4)
        top = slice(h * half, (h + 1) * half)
        first[top, :] = jnp.dot(att[top, :], wo[...], preferred_element_type=F32)

        def step(n, carry):
            rows = pl.ds(pl.multiple_of(h * half + n * norm_tile, norm_tile), norm_tile)
            before = tok_ref[rows, :].astype(F32) if layer == 0 else hid[rows, :]
            normed, scaled, inverse = norm_rows(
                before + first[rows, :] + row(layer, 2), row(layer, 3), row(layer, 4)
            )
            first[rows, :] = normed
            flow[rows, :] = normed.astype(BF16)
            xh1[rows, :] = scaled
            r1[rows, :] = jnp.broadcast_to(inverse, (norm_tile, LANES))
            return carry

        lax.fori_loop(0, half // norm_tile, step, 0)
        if h == 1:
            save(layer, 2, xh1, xh1_out.at[layer])
            save(layer, 3, r1, r1_out.at[layer])
            save(layer, 4, flow, flow_out.at[layer])

    def in_part(layer, part):
        wi = bufs[layer][2]
        if part == 0:
            saved(layer - 1, 5, 6)
        bias_row = row(layer, 5 + part)
        tile = 256
        for sub in range(width // tile):
            bias = bias_row[:, sub * tile : (sub + 1) * tile]
            cols = slice(part * width + sub * tile, part * width + (sub + 1) * tile)

            def step(n, carry, cols=cols, bias=bias):
                rows = pl.ds(pl.multiple_of(n * half, half), half)
                inner = jnp.dot(flow[rows, :], wi[:, cols], preferred_element_type=F32) + bias
                value, change = gelu_pair(inner)
                active[rows, cols] = value.astype(BF16)
                slope[rows, cols] = change.astype(BF16)
                return carry

            lax.fori_loop(0, 2, step, 0)
        if part == 3:
            save(layer, 5, active, active_out.at[layer])
            save(layer, 6, slope, slope_out.at[layer])

    def back_half(layer, h):
        wb = bufs[layer][3]
        if h == 0:
            saved(layer - 1, 7, 8)
        top = slice(h * half, (h + 1) * half)
        first[top, :] = first[top, :] + jnp.dot(
            active[top, :], wb[...], preferred_element_type=F32
        )

        def step(n, carry):
            rows = pl.ds(pl.multiple_of(h * half + n * norm_tile, norm_tile), norm_tile)
            normed, scaled, inverse = norm_rows(
                first[rows, :] + row(layer, 9), row(layer, 10), row(layer, 11)
            )
            xh2[rows, :] = scaled
            r2[rows, :] = jnp.broadcast_to(inverse, (norm_tile, LANES))
            if layer == LAYERS - 1:
                act_out[rows, :] = normed.astype(BF16)
            else:
                hid[rows, :] = normed
                hlow[rows, :] = normed.astype(BF16)
            return carry

        lax.fori_loop(0, half // norm_tile, step, 0)
        if h == 1:
            save(layer, 7, xh2, xh2_out.at[layer])
            save(layer, 8, r2, r2_out.at[layer])
            if layer == 0:
                save(layer, 9, hlow, hlow_out)

    compute = {"qkv": qkv, "att": attend, "out": out_half, "in": in_part, "back": back_half}
    for what, *at in ORDER:
        if what in compute:
            compute[what](*at)
        elif what == "pre":
            prepare(*at)
        else:
            comm(what, *at)
    vec_save = pltpu.make_async_copy(vec, vec_out, save_sem.at[1, 9])
    vec_save.start()
    for copy in started:
        copy.wait_send()
    for copy in wcopies:
        copy.wait()
    saved(0, 9)
    saved(1, *range(9))
    vec_save.wait()


def forward(tokens, segment_ids, vectors, *masters):
    count, width = tokens.shape
    ff = masters[2].shape[2]
    copies = len(gather_pieces([m.shape[1:] for m in masters])) * COPY_KINDS + VEC_KINDS
    any_spec = pl.BlockSpec(memory_space=pltpu.HBM)
    vmem = pl.BlockSpec(memory_space=pltpu.VMEM)

    def shape(dims, kind):
        return jax.ShapeDtypeStruct(dims, kind)

    out_shape = (
        shape((count, width), BF16),
        shape((LAYERS, width, 3 * width), BF16),
        shape((LAYERS, width, width), BF16),
        shape((LAYERS, width, ff), BF16),
        shape((LAYERS, ff, width), BF16),
        shape((16 * LAYERS, width), F32),
        shape((LAYERS, count, 3 * width), BF16),
        shape((LAYERS, count, width), BF16),
        shape((LAYERS, count, width), F32),
        shape((LAYERS, count, LANES), F32),
        shape((LAYERS, count, width), BF16),
        shape((LAYERS, count, ff), BF16),
        shape((LAYERS, count, ff), BF16),
        shape((LAYERS, count, width), F32),
        shape((LAYERS, count, LANES), F32),
        shape((count, width), BF16),
    )
    weights = [
        pltpu.VMEM((width, 3 * width), BF16), pltpu.VMEM((width, width), BF16),
        pltpu.VMEM((width, ff), BF16), pltpu.VMEM((ff, width), BF16),
    ]
    scratch = weights * LAYERS + [pltpu.VMEM(m.shape, F32) for m in masters] + [
        pltpu.VMEM((8, 16 * LAYERS, LANES), BF16),
        pltpu.VMEM((16 * LAYERS, width), F32),
        pltpu.VMEM((count, width), F32),
        pltpu.VMEM((count, width), BF16),
        pltpu.VMEM((count, 3 * width), BF16),
        pltpu.VMEM((count, width), BF16),
        pltpu.VMEM((count, width), F32),
        pltpu.VMEM((count, width), F32),
        pltpu.VMEM((count, LANES), F32),
        pltpu.VMEM((count, width), BF16),
        pltpu.VMEM((count, ff), BF16),
        pltpu.VMEM((count, ff), BF16),
        pltpu.VMEM((count, width), F32),
        pltpu.VMEM((count, LANES), F32),
        pltpu.VMEM((segment_ids.shape[0], ROW, ROW), F32),
        pltpu.SemaphoreType.DMA((copies,)),
        pltpu.SemaphoreType.DMA((copies,)),
        pltpu.SemaphoreType.DMA((8,)),
        pltpu.SemaphoreType.DMA((8,)),
        pltpu.SemaphoreType.DMA((LAYERS, 10)),
    ]
    return pl.pallas_call(
        forward_kernel,
        name="forward",
        out_shape=out_shape,
        in_specs=[vmem, vmem, vmem] + [any_spec] * 4,
        out_specs=[vmem] + [any_spec] * (len(out_shape) - 1),
        scratch_shapes=scratch,
        compiler_params=pltpu.CompilerParams(
            collective_id=0, has_side_effects=True, vmem_limit_bytes=62 << 20
        ),
    )(tokens, segment_ids, vectors, *masters)


DEPTH = 6
Z_DEPTH = 12
CHUNKS = 12
TAIL = {21: (512, 256), 22: (256, 256, 256), 23: (256, 256, 256)}
BACK_ORDER = (
    ("t0", 1), ("t1", 1, 0), ("t1", 1, 1), (0, 0), (0, 1), (0, 2), (0, 3), ("t2", 1, 0), ("t2", 1, 1),
    (1, 0), (1, 1), ("t2", 1, 2), (1, 2), (1, 3), ("t2", 1, 3), ("t3", 1, 0), (0, 4), ("t3", 1, 1),
    (2, 0), (0, 5), ("t3", 1, 2), ("t3", 1, 3), (1, 4), (0, 6), (0, 7), ("t4", 1, 0), (2, 1), (1, 5),
    ("t4", 1, 1), (2, 2), ("t5", 1), (0, 8), ("t6", 1), (2, 3), ("t7", 1, 0), (3, 0), ("t7", 1, 1),
    ("t7", 1, 2), ("t7", 1, 3), (2, 4), (1, 6), (3, 1), ("t8", 1, 0), (0, 9), (4, 0), ("t8", 1, 1),
    (0, 10), ("t8", 1, 2), ("t9", 1, 0), (2, 5), (1, 7), (3, 2), ("t9", 1, 1), (4, 1), ("t0", 0),
    (3, 3), (5, 0), (3, 4), (4, 2), (2, 6), (1, 8), (1, 9), (3, 5), (1, 10), (0, 11), (4, 3), (5, 1),
    ("t1", 0, 0), (2, 7), (1, 11), (4, 4), (5, 2), (3, 6), ("t1", 0, 1), (0, 12), (0, 13), (0, 14),
    (0, 15), (4, 5), (5, 3), ("t2", 0, 0), (2, 8), (1, 12), (5, 4), ("t2", 0, 1), (2, 9), (4, 6),
    ("t2", 0, 2), (5, 5), ("t2", 0, 3), (2, 10), ("t3", 0, 0), (3, 7), (0, 16), ("t3", 0, 1), (0, 17),
    ("t3", 0, 2), (5, 6), (2, 11), (1, 13), (3, 8), (4, 7), ("t3", 0, 3), ("t4", 0, 0), ("t4", 0, 1),
    (2, 12), (3, 9), (1, 14), (3, 10), (4, 8), (5, 7), ("t5", 0), (3, 11), ("t6", 0), ("t7", 0, 0),
    ("t7", 0, 1), (2, 13), (1, 15), (3, 12), (1, 16), (1, 17), (0, 18), (4, 9), (4, 10), (5, 8),
    ("t7", 0, 2), (2, 14), (1, 18), (0, 19), (3, 13), (0, 20), (4, 11), ("t7", 0, 3), ("v", 0), (5, 9),
    ("t8", 0, 0), (2, 15), (1, 19), (0, 21), (0, 22), (4, 12), ("v", 1), ("t8", 0, 1), (0, 23),
    (0, 24), (5, 10), ("t8", 0, 2), (2, 16), (4, 13), ("t9", 0, 0), ("t9", 0, 1), (5, 11), (2, 17),
    (3, 14), (5, 12), (2, 18), (1, 20), (5, 13), (3, 15), (4, 14), (2, 19), (1, 21), (0, 25), ("v", 2),
    (3, 16), (4, 15), (5, 14), (3, 17), (3, 18), (4, 16), (5, 15), (2, 20), (1, 22), (1, 23), (1, 24),
    (3, 19), (4, 17), ("v", 3), (2, 21), (1, 25), (0, 26), (0, 27), (5, 16), (3, 20), (4, 18), (2, 22),
    (1, 26), (0, 28), (2, 23), (5, 17), (2, 24), (4, 19), ("v", 4), (3, 21), (2, 25), (1, 27), (5, 18),
    (3, 22), (4, 20), (2, 26), (1, 28), (3, 23), (3, 24), (4, 21), (5, 19), (3, 25), ("v", 5), (2, 27),
    (4, 22), (4, 23), (5, 20), (3, 26), (2, 28), (4, 24), (5, 21), (3, 27), (5, 22), (3, 28), (4, 25),
    (5, 23), (5, 24), (4, 26), (5, 25), (4, 27), (4, 28), (5, 26), (5, 27), (5, 28),
)


def reduce_items(width):
    items = []
    for chunk in range(LAYERS * CHUNKS):
        at = 0
        for cols in TAIL.get(chunk, (width,)):
            items.append((chunk, at, cols))
            at += cols
    return items


def backward_kernel(
    cot_ref, seg_ref, vec_ref, tok_in, hlow_in, wq_in, wo_in, wi_in, wb_in,
    joined_in, att_in, xh1_in, r1_in, flow_in, active_in, slope_in, xh2_in, r2_in,
    grad_ref, total_ref, vtotal_ref,
    wq, wo, wi, wb, joined, att, xh1, r1, flow, active, slope, xh2, r2, hin,
    ring, got_d, got_a, got_b, got_z1, got_z2, part_sum, gtwo, glow, dvec, dbin, mask,
    vsend, vgot_d, vgot_a, vgot_b, vgot_z1, vgot_z2,
    load_sem, d_send, d_recv, a_send, a_recv, b_send, b_recv, z_send, z_recv, v_send, v_recv,
):
    here = Place()
    tokens, width = gtwo.shape
    ff = active.shape[1]
    rows_per = ring.shape[4]
    core, x, y = here.core, here.x, here.y
    other_core, other_x, other_y = 1 - core, 1 - x, 1 - y
    to_mid = {"dp": 3 - here.z}
    inner = lax.rem(here.z + 1, 4) >= 2
    outer = jnp.logical_not(inner)
    greet((here.to_c, here.to_x, here.to_y, here.to_z, to_mid))

    sources = {
        "xh2": (xh2_in, xh2), "r2": (r2_in, r2), "active": (active_in, active), "wb": (wb_in, wb),
        "slope": (slope_in, slope), "flow": (flow_in, flow), "wi": (wi_in, wi),
        "xh1": (xh1_in, xh1), "r1": (r1_in, r1), "att": (att_in, att), "wo": (wo_in, wo),
        "joined": (joined_in, joined), "hin": (None, hin), "wq": (wq_in, wq),
    }
    order = list(sources)

    def load(layer, name):
        src, dst = sources[name]
        if name == "hin":
            src = tok_in if layer == 0 else hlow_in
        else:
            src = src.at[layer]
        return pltpu.make_async_copy(src, dst, load_sem.at[order.index(name)])

    early = 3
    for name in order[:early]:
        load(LAYERS - 1, name).start()

    def need(layer, *names):
        for name in names:
            load(layer, name).wait()

    def release(layer, *names):
        if layer > 0:
            for name in names:
                load(layer - 1, name).start()

    rows_here = seg_ref.shape[0]
    for r in range(rows_here):
        wide = jnp.broadcast_to(seg_ref[r : r + 1, :].astype(F32), (ROW, ROW))
        mask[r] = jnp.where(wide == wide.T, 1.0, 0.0)
    dvec[...] = jnp.zeros_like(dvec)

    def remote(src, dst, send, recv, device):
        return pltpu.make_async_remote_copy(
            src_ref=src, dst_ref=dst, send_sem=send, recv_sem=recv, device_id=device,
            device_id_type=MESH_ID,
        )

    items = reduce_items(width)

    def place(n):
        chunk, at, cols = items[n]
        return n % DEPTH, chunk % CHUNKS, cols // 2, slice(at, at + cols // 2), slice(at + cols // 2, at + cols)

    def copy_d(n):
        _, at, cols = items[n]
        b, s = place(n)[:2]
        src = ring.at[s, other_core, :, :, :, at : at + cols]
        return remote(src, got_d.at[b, :, :, :, :cols], d_send.at[b], d_recv.at[b], here.to_c)

    def copy_a(n, side):
        b, s, part, low, high = place(n)
        if side == 0:
            src, dev = ring.at[s, core, :, other_x, :, low], here.to_x
        else:
            src, dev = ring.at[s, core, other_y, :, :, high], here.to_y
        dst = got_a.at[b, side, :, :, :part]
        return remote(src, dst, a_send.at[b, side], a_recv.at[b, side], dev)

    def copy_b(n, side):
        b, s, part, low, high = place(n)
        if side == 0:
            src, dev = ring.at[s, core, other_y, x, :, low], here.to_y
        else:
            src, dev = ring.at[s, core, y, other_x, :, high], here.to_x
        dst = got_b.at[b, side, :, :part]
        return remote(src, dst, b_send.at[b, side], b_recv.at[b, side], dev)

    def copy_z(n, hop):
        chunk, at, cols = items[n]
        b, far = n % DEPTH, n % Z_DEPTH
        if hop == 0:
            src, dst, dev, sem = part_sum.at[b, :, :cols], got_z1.at[far, :, :cols], here.to_z, far
        elif hop == 1:
            src, dst, dev, sem = part_sum.at[b, :, :cols], got_z2.at[b, :, :cols], to_mid, Z_DEPTH + b
        else:
            src = total_ref.at[chunk, :, at : at + cols]
            dst, dev, sem = src, here.to_z, Z_DEPTH + DEPTH + n
        return remote(src, dst, z_send.at[sem], z_recv.at[sem], dev)

    def added(a, b):
        return (a.astype(F32) + b.astype(F32)).astype(BF16)

    def stage0(n):
        copy_d(n).start()

    def stage1(n):
        _, at, cols = items[n]
        b, s = place(n)[:2]
        cols_here = slice(at, at + cols)
        copy_d(n).wait_recv()

        def add_shard(i, carry):
            iy, ix = lax.div(i, 2), lax.rem(i, 2)
            ring[s, core, iy, ix, :, cols_here] = added(
                ring[s, core, iy, ix, :, cols_here], got_d[b, iy, ix, :, :cols]
            )
            return carry

        lax.fori_loop(0, 4, add_shard, 0)
        copy_a(n, 0).start()
        copy_a(n, 1).start()
        copy_d(n).wait_send()

    def stage2(n):
        b, s, part, low, high = place(n)
        copy_a(n, 0).wait_recv()
        for i in range(2):
            ring[s, core, i, x, :, low] = added(ring[s, core, i, x, :, low], got_a[b, 0, i, :, :part])
        copy_b(n, 0).start()
        copy_a(n, 1).wait_recv()
        for i in range(2):
            ring[s, core, y, i, :, high] = added(ring[s, core, y, i, :, high], got_a[b, 1, i, :, :part])
        copy_b(n, 1).start()
        copy_a(n, 0).wait_send()
        copy_a(n, 1).wait_send()

    def stage3(n):
        b, s, part, low, high = place(n)
        if n >= Z_DEPTH:
            @pl.when(outer)
            def _():
                copy_z(n - Z_DEPTH, 2).wait_recv()

        copy_b(n, 0).wait_recv()
        part_sum[b, :, :part] = added(ring[s, core, y, x, :, low], got_b[b, 0, :, :part])
        copy_b(n, 1).wait_recv()
        part_sum[b, :, part : 2 * part] = added(ring[s, core, y, x, :, high], got_b[b, 1, :, :part])

        @pl.when(outer)
        def _():
            copy_z(n, 0).start()

        copy_b(n, 0).wait_send()
        copy_b(n, 1).wait_send()

    def stage4(n):
        b, cols = n % DEPTH, items[n][2]

        @pl.when(outer)
        def _():
            copy_z(n, 0).wait_send()

        @pl.when(inner)
        def _():
            copy_z(n, 0).wait_recv()
            part_sum[b, :, :cols] = added(part_sum[b, :, :cols], got_z1[n % Z_DEPTH, :, :cols])
            copy_z(n, 1).start()

    def stage5(n):
        chunk, at, cols = items[n]
        b = n % DEPTH

        @pl.when(inner)
        def _():
            copy_z(n, 1).wait_recv()
            copy_z(n, 1).wait_send()
            total_ref[chunk, :, at : at + cols] = added(part_sum[b, :, :cols], got_z2[b, :, :cols])
            copy_z(n, 2).start()

    stages = (stage0, stage1, stage2, stage3, stage4, stage5)

    def vcopy(at):
        src, dst, dev = (
            (vsend.at[other_core], vgot_d, here.to_c),
            (vsend.at[core, :, other_x], vgot_a, here.to_x),
            (vsend.at[core, other_y, x], vgot_b, here.to_y),
            (vsend.at[core, y, x], vgot_z1, here.to_z),
            (vsend.at[core, y, x], vgot_z2, to_mid),
            (vtotal_ref, vtotal_ref, here.to_z),
        )[at]
        return remote(src, dst, v_send.at[at], v_recv.at[at], dev)

    def vstage(at):
        if at == 0:
            share = width // 8
            lane = lax.broadcasted_iota(jnp.int32, (width, LANES), 1)
            column = lax.broadcasted_iota(jnp.int32, (width, LANES), 0)
            low = dvec[...].astype(BF16)
            for owner in range(8):
                pick = (column == lane + owner * share) & (lane < share)
                vsend[owner % 2, owner // 4, (owner // 2) % 2] = jnp.dot(
                    low, jnp.where(pick, 1.0, 0.0).astype(BF16), preferred_element_type=F32
                ).astype(BF16)
            vcopy(0).start()
        elif at == 1:
            vcopy(0).wait_recv()
            for i in range(4):
                vsend[core, i // 2, i % 2] = added(vsend[core, i // 2, i % 2], vgot_d[i // 2, i % 2])
            vcopy(1).start()
        elif at == 2:
            vcopy(1).wait_recv()
            for i in range(2):
                vsend[core, i, x] = added(vsend[core, i, x], vgot_a[i])
            vcopy(2).start()
        elif at == 3:
            vcopy(2).wait_recv()
            vsend[core, y, x] = added(vsend[core, y, x], vgot_b[...])

            @pl.when(outer)
            def _():
                vcopy(3).start()
        elif at == 4:
            @pl.when(inner)
            def _():
                vcopy(3).wait_recv()
                vsend[core, y, x] = added(vsend[core, y, x], vgot_z1[...])
                vcopy(4).start()
        elif at == 5:
            @pl.when(inner)
            def _():
                vcopy(4).wait_recv()
                vcopy(4).wait_send()
                vtotal_ref[...] = added(vsend[core, y, x], vgot_z2[...])
                vcopy(5).start()
                vcopy(5).wait_send()

            @pl.when(outer)
            def _():
                vcopy(3).wait_send()
                vcopy(5).wait_recv()

            for early in range(3):
                vcopy(early).wait_send()

    tile = 64
    half = tokens // 2

    def norm_back(layer, first_row, grad_in, scaled, inverse, grad_out, bias_row):
        base = 16 * layer
        gain = vec_ref[base + first_row : base + first_row + 1, :]

        def step(n, carry):
            rows = pl.ds(pl.multiple_of(n * tile, tile), tile)
            grad = grad_in[rows, :]
            hat = scaled[rows, :]
            lifted = grad * gain
            left = jnp.mean(lifted, axis=-1, keepdims=True)
            right = jnp.mean(lifted * hat, axis=-1, keepdims=True)
            result = inverse[rows, :1] * (lifted - left - hat * right)
            grad_out[rows, :] = result
            glow[rows, :] = result.astype(BF16)
            return (
                carry[0] + jnp.sum(grad * hat, axis=0, keepdims=True),
                carry[1] + jnp.sum(grad, axis=0, keepdims=True),
                carry[2] + jnp.sum(result, axis=0, keepdims=True),
            )

        nil = jnp.zeros((1, width), F32)
        sums = lax.fori_loop(0, tokens // tile, step, (nil, nil, nil))
        dvec[base + first_row : base + first_row + 1, :] = sums[0]
        dvec[base + first_row + 1 : base + first_row + 2, :] = sums[1]
        dvec[base + bias_row : base + bias_row + 1, :] = sums[2]

    def tn(left, right):
        return lax.dot_general(left, right, (((0,), (0,)), ((), ())), preferred_element_type=F32)

    def nt(left, right):
        return lax.dot_general(left, right, (((1,), (1,)), ((), ())), preferred_element_type=F32)

    def task0(layer):
        need(layer, "xh2", "r2")
        if layer == LAYERS - 1:
            for name in order[early:]:
                load(layer, name).start()
            grad_ref[...] = cot_ref[...].astype(F32)
        norm_back(layer, 10, grad_ref, xh2, r2, gtwo, 9)
        release(layer, "xh2", "r2")

    def task1(layer, at):
        if at == 0:
            need(layer, "active")
        rows_f = ff // 8

        def step(owner, carry):
            part = tn(active[:, pl.ds(pl.multiple_of(owner * rows_f, LANES), rows_f)], glow[...])
            oc, ox, oy = lax.rem(owner, 2), lax.rem(lax.div(owner, 2), 2), lax.div(owner, 4)
            for j in range(rows_f // rows_per):
                ring[j, oc, oy, ox] = part[j * rows_per : (j + 1) * rows_per].astype(BF16)
            return carry

        lax.fori_loop(4 * at, 4 * at + 4, step, 0)
        if at == 1:
            release(layer, "active")

    def task2(layer, at, of=4):
        if at == 0:
            need(layer, "wb", "slope")
        cols_at = 256
        count = ff // cols_at // of

        def step(n, carry):
            cols = pl.ds(pl.multiple_of(n * cols_at, cols_at), cols_at)
            sums = jnp.zeros((1, cols_at), F32)
            for h in range(2):
                rows = slice(h * half, (h + 1) * half)
                inner_grad = (nt(glow[rows, :], wb[cols, :]) * slope[rows, cols].astype(F32)).astype(BF16)
                slope[rows, cols] = inner_grad
                sums = sums + jnp.sum(inner_grad.astype(F32), axis=0, keepdims=True)
            dbin[:, cols] = sums
            return carry

        lax.fori_loop(at * count, (at + 1) * count, step, 0)
        if at == of - 1:
            release(layer, "wb")
            for j in range(ff // width):
                dvec[16 * layer + 5 + j : 16 * layer + 6 + j, :] = dbin[:, j * width : (j + 1) * width]

    def weight_chunk(at, left, right):
        quarter = width // 2

        for iy in range(2):
            part = tn(left[:, iy * quarter : (iy + 1) * quarter], right)
            for i in range(4):
                ring[at, i % 2, iy, i // 2] = part[i * rows_per : (i + 1) * rows_per].astype(BF16)

    def task3(layer, j):
        if j == 0:
            need(layer, "flow")
        weight_chunk(4 + j, flow, slope[:, j * width : (j + 1) * width])
        if j == 3:
            release(layer, "flow")

    def add_product(target, base, left, right, h):
        rows = slice(h * half, (h + 1) * half)
        block = 256

        for j in range(width // block):
            cols = slice(j * block, (j + 1) * block)
            product = nt(left[rows, :], right[cols, :])
            if base is not None:
                product = base[rows, cols] + product
            target[rows, cols] = product.astype(target.dtype)

    def task4(layer, h):
        if h == 0:
            need(layer, "wi", "xh1", "r1")
        add_product(gtwo, gtwo, slope, wi, h)
        if h == 1:
            norm_back(layer, 3, gtwo, xh1, r1, gtwo, 2)
            release(layer, "slope", "wi", "xh1", "r1")

    def task5(layer):
        need(layer, "att")
        weight_chunk(8, att, glow[...])

    def task6(layer):
        need(layer, "wo")
        for h in range(2):
            add_product(att, None, glow, wo, h)
        release(layer, "wo")

    def task7(layer, r):
        if r == 0:
            need(layer, "joined")
        base = 16 * layer
        rows = slice(r * ROW, (r + 1) * ROW)
        first_head = lax.broadcasted_iota(jnp.int32, (ROW, LANES), 1) < HEAD_DIM
        seen = mask[r]
        seen = jnp.concatenate([seen, seen], axis=1) > 0.5

        def stacked(value):
            nil = jnp.zeros_like(value)
            return jnp.concatenate(
                [jnp.where(first_head, value, nil), jnp.where(first_head, nil, value)], axis=0
            )

        group = 3
        for first in range(0, HEADS // 2, group):
            lanes = [
                [slice(p * width + j * LANES, p * width + (j + 1) * LANES) for p in range(3)]
                for j in range(first, first + group)
            ]
            query, keys, value = ([joined[rows, lane[p]] for lane in lanes] for p in range(3))
            out_grad = [stacked(att[rows, lane[0]]) for lane in lanes]
            both = [stacked(q) for q in query]
            scores = [
                jnp.where(seen, nt(k, q) * HEAD_DIM ** (-0.5), NEGATIVE) for k, q in zip(keys, both)
            ]
            grad_probs = [nt(v, g) for v, g in zip(value, out_grad)]
            grown = [jnp.exp(s - jnp.max(s, axis=0, keepdims=True)) for s in scores]
            probs = [e * (1.0 / jnp.sum(e, axis=0, keepdims=True)) for e in grown]
            grad_value = [
                jnp.dot(p.astype(BF16), g, preferred_element_type=F32).astype(BF16)
                for p, g in zip(probs, out_grad)
            ]
            centre = [jnp.sum(p * g, axis=0, keepdims=True) for p, g in zip(probs, grad_probs)]
            grad_scores = [(p * (g - c)).astype(BF16) for p, g, c in zip(probs, grad_probs, centre)]
            wide = [tn(g, k) for g, k in zip(grad_scores, keys)]
            grad_key = [
                jnp.dot(g, q, preferred_element_type=F32) * HEAD_DIM ** (-0.5)
                for g, q in zip(grad_scores, both)
            ]
            grad_query = [
                (jnp.where(first_head, w[:ROW], w[ROW:]) * HEAD_DIM ** (-0.5)).astype(BF16) for w in wide
            ]
            for at, lane in enumerate(lanes):
                joined[rows, lane[0]] = grad_query[at]
                joined[rows, lane[1]] = grad_key[at].astype(BF16)
                joined[rows, lane[2]] = grad_value[at]
                dvec[base : base + 1, lane[0]] += jnp.sum(
                    grad_query[at].astype(F32), axis=0, keepdims=True
                )
                dvec[base + 1 : base + 2, lane[0]] += jnp.sum(
                    grad_value[at].astype(F32), axis=0, keepdims=True
                )
        if r == rows_here - 1:
            release(layer, "att")

    def task8(layer, j):
        if j == 0:
            need(layer, "hin")
        weight_chunk(9 + j, hin, joined[:, j * width : (j + 1) * width])
        if j == 2:
            release(layer, "hin")

    def task9(layer, h):
        if h == 0:
            need(layer, "wq")
        add_product(grad_ref, gtwo, joined, wq, h)
        if h == 1:
            release(layer, "joined", "wq")

    tasks = {
        "t0": task0, "t1": task1, "t2": task2, "t3": task3, "t4": task4,
        "t5": task5, "t6": task6, "t7": task7, "t8": task8, "t9": task9,
    }
    for what, *at in BACK_ORDER:
        if what == "v":
            vstage(*at)
        elif what in tasks:
            tasks[what](*at)
        else:
            stages[what](*at)

    @pl.when(inner)
    def _():
        for n in range(len(items)):
            copy_z(n, 2).wait_send()

    @pl.when(outer)
    def _():
        for n in range(len(items) - Z_DEPTH, len(items)):
            copy_z(n, 2).wait_recv()


def backward(cotangent, segment_ids, vec, tokens, hlow, weights, kept):
    count, width = tokens.shape
    ff = weights[2].shape[2]
    rows_per = width // 8
    hbm = pl.BlockSpec(memory_space=pltpu.HBM)
    vmem = pl.BlockSpec(memory_space=pltpu.VMEM)
    small = vec.shape[0]
    out_shape = (
        jax.ShapeDtypeStruct((count, width), F32),
        jax.ShapeDtypeStruct((LAYERS * CHUNKS, rows_per, width), BF16),
        jax.ShapeDtypeStruct((small, LANES), BF16),
    )
    dma = pltpu.SemaphoreType.DMA
    z_sems = Z_DEPTH + DEPTH + len(reduce_items(width))
    scratch = [
        pltpu.VMEM((width, 3 * width), BF16), pltpu.VMEM((width, width), BF16),
        pltpu.VMEM((width, ff), BF16), pltpu.VMEM((ff, width), BF16),
        pltpu.VMEM((count, 3 * width), BF16), pltpu.VMEM((count, width), BF16),
        pltpu.VMEM((count, width), F32), pltpu.VMEM((count, LANES), F32),
        pltpu.VMEM((count, width), BF16), pltpu.VMEM((count, ff), BF16), pltpu.VMEM((count, ff), BF16),
        pltpu.VMEM((count, width), F32), pltpu.VMEM((count, LANES), F32),
        pltpu.VMEM((count, width), BF16),
        pltpu.VMEM((CHUNKS, 2, 2, 2, rows_per, width), BF16),
        pltpu.VMEM((DEPTH, 2, 2, rows_per, width), BF16),
        pltpu.VMEM((DEPTH, 2, 2, rows_per, width // 2), BF16),
        pltpu.VMEM((DEPTH, 2, rows_per, width // 2), BF16),
        pltpu.VMEM((Z_DEPTH, rows_per, width), BF16),
        pltpu.VMEM((DEPTH, rows_per, width), BF16),
        pltpu.VMEM((DEPTH, rows_per, width), BF16),
        pltpu.VMEM((count, width), F32), pltpu.VMEM((count, width), BF16),
        pltpu.VMEM((small, width), F32), pltpu.VMEM((1, ff), F32),
        pltpu.VMEM((segment_ids.shape[0], ROW, ROW), F32),
        pltpu.VMEM((2, 2, 2, small, LANES), BF16), pltpu.VMEM((2, 2, small, LANES), BF16),
        pltpu.VMEM((2, small, LANES), BF16), pltpu.VMEM((small, LANES), BF16),
        pltpu.VMEM((small, LANES), BF16), pltpu.VMEM((small, LANES), BF16),
        dma((14,)), dma((DEPTH,)), dma((DEPTH,)), dma((DEPTH, 2)), dma((DEPTH, 2)),
        dma((DEPTH, 2)), dma((DEPTH, 2)), dma((z_sems,)), dma((z_sems,)), dma((6,)), dma((6,)),
    ]
    return pl.pallas_call(
        backward_kernel,
        name="backward",
        out_shape=out_shape,
        in_specs=[vmem, vmem, vmem] + [hbm] * 15,
        out_specs=[vmem, vmem, vmem],
        scratch_shapes=scratch,
        compiler_params=pltpu.CompilerParams(
            collective_id=1, has_side_effects=True, vmem_limit_bytes=62 << 20
        ),
    )(cotangent, segment_ids, vec, tokens, hlow, *weights, *kept)


SLOTS = 4


def adam_rule(weight, gradient, moment_one, moment_two, step_rate):
    first_moment = BETA_FIRST * moment_one + (1.0 - BETA_FIRST) * gradient
    second_moment = BETA_SECOND * moment_two + (1.0 - BETA_SECOND) * gradient * gradient
    first_hat = first_moment / (1.0 - BETA_FIRST**STEP)
    second_hat = second_moment / (1.0 - BETA_SECOND**STEP)
    updated = weight - step_rate * (
        first_hat / (jnp.sqrt(second_hat) + ADAM_EPSILON) + WEIGHT_DECAY * weight
    )
    return updated, second_moment


def adam_kernel(
    total_ref, vtotal_ref, vectors_ref, vector_moments_ref, act_in, grad_in,
    q_w, o_w, i_w, b_w, q_m, o_m, i_m, b_m,
    act_out, grad_out, q_g, o_g, i_g, b_g, q_n, o_n, i_n, b_n, q_s, o_s, i_s, b_s, v_g, v_n, v_s,
    held, made, act_held, grad_held, in_sem, out_sem, pass_sem,
):
    rows, width = held.shape[2:]
    kinds = {
        "q": (q_w, q_m, (q_g, q_n, q_s)), "o": (o_w, o_m, (o_g, o_n, o_s)),
        "i": (i_w, i_m, (i_g, i_n, i_s)), "b": (b_w, b_m, (b_g, b_n, b_s)),
    }
    chunks = []
    for n in range(LAYERS * CHUNKS):
        layer, at = LAYERS - 1 - n // CHUNKS, n % CHUNKS
        if at < 4:
            place = ("b", layer, slice(at * rows, (at + 1) * rows), slice(0, width))
        elif at < 8:
            place = ("i", layer, slice(0, rows), slice((at - 4) * width, (at - 3) * width))
        elif at == 8:
            place = ("o", layer, slice(0, rows), slice(0, width))
        else:
            place = ("q", layer, slice(0, rows), slice((at - 9) * width, (at - 8) * width))
        chunks.append(place)

    def reads(n):
        kind, layer, r, c = chunks[n]
        weight, moments, _ = kinds[kind]
        b = n % SLOTS
        sources = (weight.at[layer, r, c], moments.at[0, layer, r, c], moments.at[1, layer, r, c])
        return [
            pltpu.make_async_copy(source, held.at[b, k], in_sem.at[b, k])
            for k, source in enumerate(sources)
        ]

    def writes(n):
        kind, layer, r, c = chunks[n]
        b = n % SLOTS
        return [
            pltpu.make_async_copy(made.at[b, k], target.at[layer, r, c], out_sem.at[b, k])
            for k, target in enumerate(kinds[kind][2])
        ]

    for n in range(SLOTS - 1):
        for copy in reads(n):
            copy.start()
    passing = (
        pltpu.make_async_copy(act_in, act_held, pass_sem.at[0]),
        pltpu.make_async_copy(grad_in, grad_held, pass_sem.at[1]),
    )
    passed = (
        pltpu.make_async_copy(act_held, act_out, pass_sem.at[2]),
        pltpu.make_async_copy(grad_held, grad_out, pass_sem.at[3]),
    )
    for copy in passing:
        copy.start()
    share = vectors_ref.shape[2]
    for layer in range(LAYERS):
        gradient = vtotal_ref[16 * layer : 16 * layer + 12, :share].astype(F32)
        updated, second = adam_rule(
            vectors_ref[:, layer, :], gradient, vector_moments_ref[0, :, layer, :],
            vector_moments_ref[1, :, layer, :], RATE_VECTOR,
        )
        v_g[:, layer, :] = gradient
        v_n[:, layer, :] = updated
        v_s[:, layer, :] = second
    tile = 32
    for n in range(LAYERS * CHUNKS):
        b = n % SLOTS
        if n == SLOTS:
            for early, late in zip(passing, passed):
                early.wait()
                late.start()
        if n + SLOTS - 1 < LAYERS * CHUNKS:
            for copy in reads(n + SLOTS - 1):
                copy.start()
        for copy in reads(n):
            copy.wait()
        if n >= SLOTS:
            for copy in writes(n - SLOTS):
                copy.wait()

        def step(t, carry, n=n, b=b):
            r = pl.ds(pl.multiple_of(t * tile, tile), tile)
            gradient = total_ref[n, r, :].astype(F32)
            updated, second = adam_rule(
                held[b, 0, r, :], gradient, held[b, 1, r, :], held[b, 2, r, :], RATE_MATRIX
            )
            made[b, 0, r, :] = gradient
            made[b, 1, r, :] = updated
            made[b, 2, r, :] = second
            return carry

        lax.fori_loop(0, rows // tile, step, 0)
        for copy in writes(n):
            copy.start()
    for n in range(LAYERS * CHUNKS - SLOTS, LAYERS * CHUNKS):
        for copy in writes(n):
            copy.wait()
    for copy in passed:
        copy.wait()


def adam(activations, grad, total, vtotal, masters, moments):
    rows, width = total.shape[1:]
    hbm = pl.BlockSpec(memory_space=pltpu.HBM)
    vmem = pl.BlockSpec(memory_space=pltpu.VMEM)
    matrices, vectors = masters[:4], masters[4].transpose(1, 0, 2)
    passed = [jax.ShapeDtypeStruct(p.shape, p.dtype) for p in (activations, grad)]
    matrix_shapes = [jax.ShapeDtypeStruct(m.shape, F32) for m in matrices]
    vector_shape = jax.ShapeDtypeStruct(vectors.shape, F32)
    out = pl.pallas_call(
        adam_kernel,
        name="adam",
        out_shape=passed + matrix_shapes * 3 + [vector_shape] * 3,
        in_specs=[vmem] * 4 + [hbm] * 10,
        out_specs=[hbm] * 14 + [vmem] * 3,
        scratch_shapes=[
            pltpu.VMEM((SLOTS, 3, rows, width), F32), pltpu.VMEM((SLOTS, 3, rows, width), F32),
            pltpu.VMEM(activations.shape, BF16), pltpu.VMEM(grad.shape, F32),
            pltpu.SemaphoreType.DMA((SLOTS, 3)), pltpu.SemaphoreType.DMA((SLOTS, 3)),
            pltpu.SemaphoreType.DMA((4,)),
        ],
        compiler_params=pltpu.CompilerParams(vmem_limit_bytes=62 << 20),
    )(
        total, vtotal, vectors, moments[4].transpose(0, 2, 1, 3), activations, grad, *matrices,
        *moments[:4],
    )
    gradients, updates, states = out[2:6], out[6:10], out[10:14]
    vector_outs = [v.transpose(1, 0, 2) for v in out[14:]]
    return (
        out[0], out[1], *gradients, vector_outs[0], *updates, vector_outs[1], *states, vector_outs[2]
    )


def norm_forward(values, gain_row, shift_row):
    centered = values - jnp.mean(values, axis=-1, keepdims=True)
    inverse = lax.rsqrt(jnp.mean(centered * centered, axis=-1, keepdims=True) + EPSILON)
    scaled = centered * inverse
    return (scaled * gain_row + shift_row, scaled, inverse)


def norm_backward(grad_out, scaled, inverse, gain_row):
    grad_scaled = grad_out * gain_row
    grad_in = inverse * (
        grad_scaled
        - jnp.mean(grad_scaled, axis=-1, keepdims=True)
        - scaled * jnp.mean(grad_scaled * scaled, axis=-1, keepdims=True)
    )
    return (grad_in, jnp.sum(grad_out * scaled, axis=0), jnp.sum(grad_out, axis=0))


def score_block(queries, key_rows, same_segment):
    scores = jnp.einsum(
        "rqhe,rkhe->rhqk", queries, key_rows, preferred_element_type=jnp.float32
    ) * HEAD_DIM ** (-0.5)
    return jnp.where(same_segment, scores, NEGATIVE)


def layer_forward(hidden, same_segment, weights):
    qkv_used, out_used, in_used, back_used, vector_low = weights
    vector = vector_low.astype(jnp.float32)
    row_count = same_segment.shape[0]
    model_width = out_used.shape[0]
    hidden_low = hidden.astype(jnp.bfloat16)
    bias_qkv = jnp.concatenate([vector[0], jnp.zeros_like(vector[0]), vector[1]])
    joined = (jnp.dot(hidden_low, qkv_used, preferred_element_type=jnp.float32) + bias_qkv).astype(
        jnp.bfloat16
    )
    split_qkv = joined.reshape(row_count, -1, 3, HEADS, HEAD_DIM)
    scores = score_block(split_qkv[:, :, 0], split_qkv[:, :, 1], same_segment)
    row_top = jnp.max(scores, axis=-1, keepdims=True)
    log_total = row_top + jnp.log(jnp.sum(jnp.exp(scores - row_top), axis=-1, keepdims=True))
    prob_low = jnp.exp(scores - log_total).astype(jnp.bfloat16)
    attended = jnp.einsum(
        "rhqk,rkhe->rqhe", prob_low, split_qkv[:, :, 2], preferred_element_type=jnp.float32
    )
    attended_low = attended.reshape(-1, model_width).astype(jnp.bfloat16)
    branch = jnp.dot(attended_low, out_used, preferred_element_type=jnp.float32) + vector[2]
    first_norm, scaled_one, inverse_one = norm_forward(hidden + branch, vector[3], vector[4])
    first_low = first_norm.astype(jnp.bfloat16)
    inner_pre = jnp.dot(first_low, in_used, preferred_element_type=jnp.float32) + vector[
        5:9
    ].reshape(-1)
    active_low = jax.nn.gelu(inner_pre, approximate=False).astype(jnp.bfloat16)
    outer_out = jnp.dot(active_low, back_used, preferred_element_type=jnp.float32) + vector[9]
    output, scaled_two, inverse_two = norm_forward(first_norm + outer_out, vector[10], vector[11])
    kept_state = (
        hidden_low,
        joined,
        log_total,
        attended_low,
        scaled_one,
        inverse_one,
        first_low,
        inner_pre,
        active_low,
        scaled_two,
        inverse_two,
    )
    return (output, kept_state)


def layer_backward(grad_out, same_segment, weights, kept_state):
    qkv_used, out_used, in_used, back_used, vector_low = weights
    vector = vector_low.astype(jnp.float32)
    (
        hidden_low,
        joined,
        log_total,
        attended_low,
        scaled_one,
        inverse_one,
        first_low,
        inner_pre,
        active_low,
        scaled_two,
        inverse_two,
    ) = kept_state
    row_count = same_segment.shape[0]
    model_width = out_used.shape[0]
    grad_two, gain_two_grad, shift_two_grad = norm_backward(
        grad_out, scaled_two, inverse_two, vector[10]
    )
    grad_outer = grad_two.astype(jnp.bfloat16)
    back_bias_grad = jnp.sum(grad_two, axis=0)
    back_weight_grad = jnp.einsum(
        "tf,td->fd", active_low, grad_outer, preferred_element_type=jnp.float32
    )
    grad_active = jnp.einsum("td,fd->tf", grad_outer, back_used, preferred_element_type=jnp.float32)
    gelu_value, gelu_pull = jax.vjp(
        lambda values: jax.nn.gelu(values, approximate=False), inner_pre
    )
    grad_inner = gelu_pull(grad_active)[0].astype(jnp.bfloat16)
    in_bias_grad = jnp.sum(grad_inner, axis=0, dtype=jnp.float32)
    in_weight_grad = jnp.einsum(
        "td,tf->df", first_low, grad_inner, preferred_element_type=jnp.float32
    )
    grad_first = grad_two + jnp.einsum(
        "tf,df->td", grad_inner, in_used, preferred_element_type=jnp.float32
    )
    grad_one, gain_one_grad, shift_one_grad = norm_backward(
        grad_first, scaled_one, inverse_one, vector[3]
    )
    grad_branch = grad_one.astype(jnp.bfloat16)
    out_bias_grad = jnp.sum(grad_one, axis=0)
    out_weight_grad = jnp.einsum(
        "td,te->de", attended_low, grad_branch, preferred_element_type=jnp.float32
    )
    grad_mixed = jnp.einsum("te,de->td", grad_branch, out_used, preferred_element_type=jnp.float32)
    grad_mixed = grad_mixed.astype(jnp.bfloat16).reshape(row_count, -1, HEADS, HEAD_DIM)
    split_qkv = joined.reshape(row_count, -1, 3, HEADS, HEAD_DIM)
    queries = split_qkv[:, :, 0]
    key_rows = split_qkv[:, :, 1]
    value_rows = split_qkv[:, :, 2]
    prob_full = jnp.exp(score_block(queries, key_rows, same_segment) - log_total)
    prob_low = prob_full.astype(jnp.bfloat16)
    grad_values = jnp.einsum(
        "rhqk,rqhe->rkhe", prob_low, grad_mixed, preferred_element_type=jnp.float32
    )
    grad_probs = jnp.einsum(
        "rqhe,rkhe->rhqk", grad_mixed, value_rows, preferred_element_type=jnp.float32
    )
    centred = jnp.sum(prob_full * grad_probs, axis=-1, keepdims=True)
    grad_scores = (prob_full * (grad_probs - centred)).astype(jnp.bfloat16)
    grad_queries = jnp.einsum(
        "rhqk,rkhe->rqhe", grad_scores, key_rows, preferred_element_type=jnp.float32
    ) * HEAD_DIM ** (-0.5)
    grad_keys = jnp.einsum(
        "rhqk,rqhe->rkhe", grad_scores, queries, preferred_element_type=jnp.float32
    ) * HEAD_DIM ** (-0.5)
    grad_joined = (
        jnp.stack([grad_queries, grad_keys, grad_values], axis=2)
        .reshape(-1, 3 * model_width)
        .astype(jnp.bfloat16)
    )
    qkv_bias_grad = jnp.sum(grad_joined, axis=0, dtype=jnp.float32)
    qkv_weight_grad = jnp.einsum(
        "td,tc->dc", hidden_low, grad_joined, preferred_element_type=jnp.float32
    )
    grad_hidden = grad_one + jnp.einsum(
        "tc,dc->td", grad_joined, qkv_used, preferred_element_type=jnp.float32
    )
    vector_grad = jnp.concatenate(
        [
            qkv_bias_grad[:model_width][None],
            qkv_bias_grad[2 * model_width :][None],
            out_bias_grad[None],
            gain_one_grad[None],
            shift_one_grad[None],
            in_bias_grad.reshape(4, model_width),
            back_bias_grad[None],
            gain_two_grad[None],
            shift_two_grad[None],
        ],
        axis=0,
    )
    return (
        grad_hidden,
        (qkv_weight_grad, out_weight_grad, in_weight_grad, back_weight_grad, vector_grad),
    )


def adam_step(weight, gradient, moment_one, moment_two, step_rate):
    first_moment = BETA_FIRST * moment_one + (1.0 - BETA_FIRST) * gradient
    second_moment = BETA_SECOND * moment_two + (1.0 - BETA_SECOND) * gradient * gradient
    first_hat = first_moment / (1.0 - BETA_FIRST**STEP)
    second_hat = second_moment / (1.0 - BETA_SECOND**STEP)
    updated = weight - step_rate * (
        first_hat / (jnp.sqrt(second_hat) + ADAM_EPSILON) + WEIGHT_DECAY * weight
    )
    return gradient, updated, second_moment


def update_layer(summed, masters, moments, layer_at):
    outcome = []
    for kind_at in range(5):
        step_rate = RATE_VECTOR if kind_at == 4 else RATE_MATRIX
        outcome.append(
            adam_step(
                masters[kind_at][layer_at],
                summed[kind_at],
                moments[kind_at][0, layer_at],
                moments[kind_at][1, layer_at],
                step_rate,
            )
        )
    return outcome


def local_parts(masters, layer_at):
    return tuple((master[layer_at].astype(jnp.bfloat16) for master in masters))


def collect(results, kind_at, member):
    return jnp.stack([layer_result[kind_at][member] for layer_result in results])


def on_device_any(
    tokens,
    segment_ids,
    cotangent,
    qkv_weight,
    out_weight,
    in_weight,
    back_weight,
    vectors,
    qkv_moments,
    out_moments,
    in_moments,
    back_moments,
    vector_moments,
):
    masters = (qkv_weight, out_weight, in_weight, back_weight, vectors)
    moments = (qkv_moments, out_moments, in_moments, back_moments, vector_moments)
    same_segment = (segment_ids[:, :, None] == segment_ids[:, None, :])[:, None]
    hidden = tokens.astype(jnp.float32)
    saved_states = []
    for layer_at in range(LAYERS):
        parts_now = local_parts(masters, layer_at)
        weights = (
            lax.all_gather(parts_now[0], "fsdp", axis=0, tiled=True),
            lax.all_gather(parts_now[1], "fsdp", axis=0, tiled=True),
            lax.all_gather(parts_now[2], "fsdp", axis=0, tiled=True),
            lax.all_gather(parts_now[3], "fsdp", axis=0, tiled=True),
            lax.all_gather(parts_now[4], "fsdp", axis=1, tiled=True),
        )
        hidden, kept_state = layer_forward(hidden, same_segment, weights)
        saved_states.append(kept_state)
    activations = hidden.astype(jnp.bfloat16)
    grad_hidden = cotangent.astype(jnp.float32)
    results = [None] * LAYERS
    for layer_at in reversed(range(LAYERS)):
        parts_now = local_parts(masters, layer_at)
        weights = (
            lax.all_gather(parts_now[0], "fsdp", axis=0, tiled=True),
            lax.all_gather(parts_now[1], "fsdp", axis=0, tiled=True),
            lax.all_gather(parts_now[2], "fsdp", axis=0, tiled=True),
            lax.all_gather(parts_now[3], "fsdp", axis=0, tiled=True),
            lax.all_gather(parts_now[4], "fsdp", axis=1, tiled=True),
        )
        grad_hidden, weight_grads = layer_backward(
            grad_hidden, same_segment, weights, saved_states[layer_at]
        )
        shards = (
            lax.psum_scatter(
                weight_grads[0].astype(jnp.bfloat16), "fsdp", scatter_dimension=0, tiled=True
            ).astype(jnp.float32),
            lax.psum_scatter(
                weight_grads[1].astype(jnp.bfloat16), "fsdp", scatter_dimension=0, tiled=True
            ).astype(jnp.float32),
            lax.psum_scatter(
                weight_grads[2].astype(jnp.bfloat16), "fsdp", scatter_dimension=0, tiled=True
            ).astype(jnp.float32),
            lax.psum_scatter(
                weight_grads[3].astype(jnp.bfloat16), "fsdp", scatter_dimension=0, tiled=True
            ).astype(jnp.float32),
            lax.psum_scatter(
                weight_grads[4].astype(jnp.bfloat16), "fsdp", scatter_dimension=1, tiled=True
            ).astype(jnp.float32),
        )
        totals = (
            lax.psum(shards[0].astype(jnp.bfloat16), "dp").astype(jnp.float32),
            lax.psum(shards[1].astype(jnp.bfloat16), "dp").astype(jnp.float32),
            lax.psum(shards[2].astype(jnp.bfloat16), "dp").astype(jnp.float32),
            lax.psum(shards[3].astype(jnp.bfloat16), "dp").astype(jnp.float32),
            lax.psum(shards[4].astype(jnp.bfloat16), "dp").astype(jnp.float32),
        )
        results[layer_at] = update_layer(totals, masters, moments, layer_at)
    return (
        activations,
        grad_hidden,
        collect(results, 0, 0),
        collect(results, 1, 0),
        collect(results, 2, 0),
        collect(results, 3, 0),
        collect(results, 4, 0),
        collect(results, 0, 1),
        collect(results, 1, 1),
        collect(results, 2, 1),
        collect(results, 3, 1),
        collect(results, 4, 1),
        collect(results, 0, 2),
        collect(results, 1, 2),
        collect(results, 2, 2),
        collect(results, 3, 2),
        collect(results, 4, 2),
    )


def on_device(
    tokens,
    segment_ids,
    cotangent,
    qkv_weight,
    out_weight,
    in_weight,
    back_weight,
    vectors,
    qkv_moments,
    out_moments,
    in_moments,
    back_moments,
    vector_moments,
):
    masters = (qkv_weight, out_weight, in_weight, back_weight, vectors)
    moments = (qkv_moments, out_moments, in_moments, back_moments, vector_moments)
    activations, wq, wo, wi, wb, vec, *kept, hlow = forward(
        tokens, segment_ids, vectors.transpose(1, 0, 2), *masters[:4]
    )
    grad, total, vtotal = backward(
        cotangent, segment_ids, vec, tokens, hlow, (wq, wo, wi, wb), kept
    )
    return adam(activations, grad, total, vtotal, masters, moments)


def solution(mesh):
    in_specs = (
        P(("fsdp", "dp"), None),
        P(("fsdp", "dp"), None),
        P(("fsdp", "dp"), None),
        P(None, "fsdp", None),
        P(None, "fsdp", None),
        P(None, "fsdp", None),
        P(None, "fsdp", None),
        P(None, None, "fsdp"),
        P(None, None, "fsdp", None),
        P(None, None, "fsdp", None),
        P(None, None, "fsdp", None),
        P(None, None, "fsdp", None),
        P(None, None, None, "fsdp"),
    )
    out_specs = (
        P(("fsdp", "dp"), None),
        P(("fsdp", "dp"), None),
        P(None, "fsdp", None),
        P(None, "fsdp", None),
        P(None, "fsdp", None),
        P(None, "fsdp", None),
        P(None, None, "fsdp"),
        P(None, "fsdp", None),
        P(None, "fsdp", None),
        P(None, "fsdp", None),
        P(None, "fsdp", None),
        P(None, None, "fsdp"),
        P(None, "fsdp", None),
        P(None, "fsdp", None),
        P(None, "fsdp", None),
        P(None, "fsdp", None),
        P(None, None, "fsdp"),
    )
    body = on_device if dict(mesh.shape) == {"fsdp": 8, "dp": 4} else on_device_any
    return jax.shard_map(
        body, mesh=mesh, in_specs=in_specs, out_specs=out_specs, check_vma=False
    )
```

```python
import jax
import jax.numpy as jnp
from jax import lax
from jax.experimental import pallas as pl
from jax.experimental.pallas import tpu as pltpu
from jax.sharding import PartitionSpec as P

HEADS = 12
HEAD_DIM = 64
LAYERS = 2
STEP = 3
ROW = 128
LANES = 128

EPSILON = 1e-05
NEGATIVE = -1000000000.0
BETA_FIRST = 0.5
BETA_SECOND = 0.5
WEIGHT_DECAY = 0.01
ADAM_EPSILON = 1e-08
RATE_MATRIX = 0.06
RATE_VECTOR = 0.5
MESH_ID = pl.DeviceIdType.MESH
BF16 = jnp.bfloat16
F32 = jnp.float32


class Place:
    def __init__(self):
        f = lax.axis_index("fsdp")
        z = lax.axis_index("dp")
        core = lax.rem(f, 2)
        x = lax.rem(lax.div(f, 2), 2)
        y = lax.div(f, 4)
        self.f, self.z, self.core, self.x, self.y = f, z, core, x, y
        self.fc = f + 1 - 2 * core
        self.fx = f + 2 - 4 * x
        self.fy = f + 4 - 8 * y
        self.fd = self.fx + 4 - 8 * y
        self.q = lax.rem(z, 2)
        self.to_c = {"fsdp": self.fc}
        self.to_x = {"fsdp": self.fx}
        self.to_y = {"fsdp": self.fy}
        self.to_z = {"dp": z + 1 - 2 * self.q}


def greet(partners):
    barrier = pltpu.get_barrier_semaphore()
    for partner in partners:
        pl.semaphore_signal(barrier, inc=1, device_id=partner, device_id_type=MESH_ID)
    pl.semaphore_wait(barrier, len(partners))


def norm_rows(values, gain_row, shift_row):
    centered = values - jnp.mean(values, axis=-1, keepdims=True)
    inverse = lax.rsqrt(jnp.mean(centered * centered, axis=-1, keepdims=True) + EPSILON)
    scaled = centered * inverse
    return scaled * gain_row + shift_row, scaled, inverse


def gelu_pair(value):
    cdf = 0.5 * (1.0 + lax.erf(value * 0.7071067811865476))
    slope = cdf + value * (0.3989422804014327 * jnp.exp(-0.5 * value * value))
    return value * cdf, slope


SPLITS = (3, 1, 2, 2)
COPY_KINDS = 14
VEC_KINDS = 7


def gather_pieces(shards):
    pieces = []
    for layer in range(LAYERS):
        for kind, (rows, cols) in enumerate(shards):
            count = SPLITS[kind]
            for i in range(count):
                if kind == 3:
                    pieces.append((layer, kind, i * rows // count, rows // count, 0, cols))
                else:
                    pieces.append((layer, kind, 0, rows, i * cols // count, cols // count))
    return pieces


ORDER = (
    ("own", 0), ("pre", 0), ("own", 1), ("pre", 1), ("own", 2), ("pre", 2), ("own", 3), ("s1", 0),
    ("s1", 1), ("s1", 2), ("own", 4), ("s1", 3), ("s2", 0), ("s2", 1), ("s2", 2), ("own", 5),
    ("s1", 4), ("s3", 0), ("s2", 3), ("s3", 1), ("s4", 0), ("qkv", 0, 0), ("s3", 2), ("s4", 1),
    ("qkv", 0, 1), ("own", 6), ("s4", 2), ("qkv", 0, 2), ("s1", 5), ("att", 0, 0), ("att", 0, 1),
    ("s2", 4), ("s3", 3), ("att", 0, 2), ("att", 0, 3), ("own", 7), ("s4", 3), ("out", 0, 0),
    ("s1", 6), ("out", 0, 1), ("s2", 5), ("s3", 4), ("s4", 4), ("in", 0, 0), ("own", 8), ("s1", 7),
    ("in", 0, 1), ("own", 9), ("s2", 6), ("s3", 5), ("s1", 8), ("s4", 5), ("in", 0, 2), ("own", 10),
    ("s2", 7), ("own", 11), ("in", 0, 3), ("own", 12), ("s1", 9), ("s2", 8), ("s3", 6), ("s1", 10),
    ("s3", 7), ("s4", 6), ("s1", 11), ("s4", 7), ("back", 0, 0), ("back", 0, 1), ("own", 13),
    ("s1", 12), ("s3", 8), ("s2", 9), ("s2", 10), ("s4", 8), ("qkv", 1, 0), ("s2", 11), ("own", 14),
    ("s1", 13), ("s3", 9), ("s3", 10), ("s2", 12), ("s4", 9), ("qkv", 1, 1), ("s3", 11), ("s4", 10),
    ("qkv", 1, 2), ("att", 1, 0), ("own", 15), ("att", 1, 1), ("s1", 14), ("att", 1, 2), ("s2", 13),
    ("att", 1, 3), ("s3", 12), ("s4", 11), ("out", 1, 0), ("out", 1, 1), ("s4", 12), ("in", 1, 0),
    ("s1", 15), ("in", 1, 1), ("s2", 14), ("s3", 13), ("s2", 15), ("s4", 13), ("in", 1, 2),
    ("in", 1, 3), ("s3", 14), ("s4", 14), ("s3", 15), ("s4", 15), ("back", 1, 0), ("back", 1, 1),
)


def forward_kernel(
    tok_ref, seg_ref, vec_ref, q_w, o_w, i_w, b_w,
    act_out, wq_out, wo_out, wi_out, wb_out, vec_out,
    joined_out, att_out, xh1_out, r1_out, flow_out, active_out, slope_out, xh2_out, r2_out, hlow_out,
    wq0, wo0, wi0, wb0, wq1, wo1, wi1, wb1, st_q, st_o, st_i, st_b, vslots, vec,
    hid, hlow, joined, att, first, xh1, r1, flow, active, slope, xh2, r2, mask,
    send_sem, recv_sem, own_sem, wout_sem, save_sem,
):
    here = Place()
    masters = (q_w, o_w, i_w, b_w)
    stages = (st_q, st_o, st_i, st_b)
    bufs = ((wq0, wo0, wi0, wb0), (wq1, wo1, wi1, wb1))
    wouts = (wq_out, wo_out, wi_out, wb_out)
    f, fx, fy, fd = here.f, here.fx, here.fy, here.fd
    pieces = gather_pieces([m.shape[1:] for m in masters])
    tokens, width = hid.shape
    half = tokens // 2

    def stage_copy(layer, kind):
        return pltpu.make_async_copy(
            masters[kind].at[layer], stages[kind].at[layer], own_sem.at[4 * layer + kind]
        )

    stage_copy(0, 0).start()
    mine = jnp.zeros((1,) + vslots.shape[1:], BF16)
    vslots[pl.ds(f, 1)] = mine
    share = vec_ref.shape[2]
    for layer in range(LAYERS):
        vslots[pl.ds(f, 1), 16 * layer : 16 * layer + 12, :share] = vec_ref[:, layer, :].astype(BF16)[None]
    greet((here.to_c, here.to_x, here.to_y, here.to_z))

    started = []
    copies = {}

    def make(p, kind):
        layer, matrix, row_at, rows, col_at, cols = pieces[p]
        buf = bufs[layer][matrix]
        shard_rows = masters[matrix].shape[1]
        third = cols // 3
        two = 2 * third
        c_xy = pl.multiple_of(col_at + here.q * third, LANES)
        c_b = pl.multiple_of(c_xy + third, LANES)
        c_z = pl.multiple_of(col_at + here.q * two, LANES)
        c_w = pl.multiple_of(col_at + (1 - here.q) * two, LANES)

        def win(owner, col, wide):
            at = pl.multiple_of(owner * shard_rows + row_at, 32)
            return buf.at[pl.ds(at, rows), pl.ds(col, wide)]

        owner, col, wide, device = (
            (f, col_at, cols, here.to_c), (f, c_xy, two, here.to_x), (f, c_xy, two, here.to_y),
            (fx, c_xy, two, here.to_c), (fx, c_xy, third, here.to_y), (fx, c_z, third, here.to_z),
            (fy, c_xy, two, here.to_c), (fy, c_b, third, here.to_x), (fy, c_z, third, here.to_z),
            (fd, c_xy, two, here.to_c), (fd, c_z, third, here.to_z),
            (fx, c_w, third, here.to_c), (fy, c_w, third, here.to_c), (fd, c_w, third, here.to_c),
        )[kind]
        window = win(owner, col, wide)
        slot = p * COPY_KINDS + kind
        return pltpu.make_async_remote_copy(
            src_ref=window, dst_ref=window, send_sem=send_sem.at[slot], recv_sem=recv_sem.at[slot],
            device_id=device, device_id_type=MESH_ID,
        )

    def start(p, *kinds):
        for kind in kinds:
            copy = make(p, kind)
            copy.start()
            copies[p, kind] = copy
            started.append(copy)

    def arrived(p, *kinds):
        for kind in kinds:
            copies[p, kind].wait_recv()

    def send_own(p):
        layer, matrix, row_at, rows, col_at, cols = pieces[p]
        if row_at == 0 and col_at == 0:
            stage_copy(layer, matrix).wait()
        stage, buf = stages[matrix], bufs[layer][matrix]
        shard_rows = stage.shape[1]
        tile = 32

        def step(n, carry):
            at = pl.multiple_of(row_at + n * tile, tile)
            to = pl.multiple_of(f * shard_rows + row_at + n * tile, tile)
            buf[pl.ds(to, tile), col_at : col_at + cols] = stage[
                layer, pl.ds(at, tile), col_at : col_at + cols
            ].astype(BF16)
            return carry

        lax.fori_loop(0, rows // tile, step, 0)
        start(p, 1, 2, 0)
        if p == 0:
            for later in range(1, 4 * LAYERS):
                stage_copy(later // 4, later % 4).start()

    wcopies = []

    def comm(what, p):
        if what == "own":
            send_own(p)
        elif what == "s1":
            arrived(p, 1, 2)
            start(p, 4, 7, 5, 8, 3, 6)
        elif what == "s2":
            arrived(p, 4, 7)
            start(p, 10, 9)
        elif what == "s3":
            arrived(p, 5, 8, 10)
            start(p, 11, 12, 13)
        else:
            arrived(p, 0, 3, 6, 9, 11, 12, 13)
            layer, matrix = pieces[p][:2]
            if p + 1 == len(pieces) or pieces[p + 1][1] != matrix:
                copy = pltpu.make_async_copy(
                    bufs[layer][matrix], wouts[matrix].at[layer], wout_sem.at[4 * layer + matrix]
                )
                copy.start()
                wcopies.append(copy)

    def vcopy(kind):
        owner, dev = (
            (f, here.to_x), (f, here.to_y), (f, here.to_c),
            (fx, here.to_y), (fx, here.to_c), (fy, here.to_c), (fd, here.to_c),
        )[kind]
        slot = len(pieces) * COPY_KINDS + kind
        return pltpu.make_async_remote_copy(
            src_ref=vslots.at[owner], dst_ref=vslots.at[owner], send_sem=send_sem.at[slot],
            recv_sem=recv_sem.at[slot], device_id=dev, device_id_type=MESH_ID,
        )

    vc = [vcopy(kind) for kind in range(VEC_KINDS)]
    started.extend(vc)
    for kind in (0, 1, 2):
        vc[kind].start()
    rows_here = seg_ref.shape[0]

    def prepare(step):
        if step == 0:
            for r in range(rows_here):
                wide = jnp.broadcast_to(seg_ref[r : r + 1, :].astype(F32), (ROW, ROW))
                mask[r] = jnp.where(wide == wide.T, 1.0, 0.0)
            vc[0].wait_recv()
            vc[1].wait_recv()
            for kind in (3, 4, 5):
                vc[kind].start()
        elif step == 1:
            vc[3].wait_recv()
            vc[6].start()
        else:
            for kind in (2, 4, 5, 6):
                vc[kind].wait_recv()
            lane = lax.broadcasted_iota(jnp.int32, (LANES, width), 0)
            column = lax.broadcasted_iota(jnp.int32, (LANES, width), 1)
            whole = jnp.zeros(vec.shape, F32)
            for owner in range(8):
                pick = (column == lane + owner * share) & (lane < share)
                whole = whole + jnp.dot(
                    vslots[owner], jnp.where(pick, 1.0, 0.0).astype(BF16),
                    preferred_element_type=F32,
                )
            vec[...] = whole

    saves = {}

    def save(layer, at, src, dst):
        copy = pltpu.make_async_copy(src, dst, save_sem.at[layer, at])
        copy.start()
        saves[layer, at] = copy

    def saved(layer, *ats):
        if layer >= 0:
            for at in ats:
                saves[layer, at].wait()

    def row(layer, at):
        return vec[16 * layer + at : 16 * layer + at + 1, :]

    def qkv(layer, part):
        low_ref, wq = (tok_ref if layer == 0 else hlow), bufs[layer][0]
        if part == 0:
            saved(layer - 1, 0)
        cols = slice(part * width, (part + 1) * width)

        def step(n, carry):
            rows = pl.ds(pl.multiple_of(n * half, half), half)
            acc = jnp.dot(low_ref[rows, :], wq[:, cols], preferred_element_type=F32)
            if part != 1:
                acc = acc + row(layer, part // 2)
            joined[rows, cols] = acc.astype(BF16)
            return carry

        lax.fori_loop(0, 2, step, 0)
        if part == 2:
            save(layer, 0, joined, joined_out.at[layer])

    def attend(layer, r):
        if r == 0:
            saved(layer - 1, 1)
        rows = slice(r * ROW, (r + 1) * ROW)
        first_head = lax.broadcasted_iota(jnp.int32, (ROW, LANES), 1) < HEAD_DIM
        seen = mask[r]
        seen = jnp.concatenate([seen, seen], axis=1) > 0.5
        group = 3
        for at in range(0, HEADS // 2, group):
            lanes = [
                [slice(p * width + j * LANES, p * width + (j + 1) * LANES) for p in range(3)]
                for j in range(at, at + group)
            ]
            query, keys, value = ([joined[rows, lane[p]] for lane in lanes] for p in range(3))
            both = [
                jnp.concatenate(
                    [jnp.where(first_head, q, jnp.zeros_like(q)), jnp.where(first_head, jnp.zeros_like(q), q)],
                    axis=0,
                )
                for q in query
            ]
            scores = [
                lax.dot_general(k, q, (((1,), (1,)), ((), ())), preferred_element_type=F32)
                for k, q in zip(keys, both)
            ]
            scores = [jnp.where(seen, s * HEAD_DIM ** (-0.5), NEGATIVE) for s in scores]
            grown = [jnp.exp(s - jnp.max(s, axis=0, keepdims=True)) for s in scores]
            probs = [
                (e * (1.0 / jnp.sum(e, axis=0, keepdims=True))).astype(BF16) for e in grown
            ]
            mixed = [
                lax.dot_general(p, v, (((0,), (0,)), ((), ())), preferred_element_type=F32)
                for p, v in zip(probs, value)
            ]
            for m, lane in zip(mixed, lanes):
                att[rows, lane[0]] = jnp.where(first_head, m[:ROW], m[ROW:]).astype(BF16)
        if r == rows_here - 1:
            save(layer, 1, att, att_out.at[layer])

    norm_tile = 64

    def out_half(layer, h):
        wo = bufs[layer][1]
        if h == 0:
            saved(layer - 1, 2, 3, 4)
        top = slice(h * half, (h + 1) * half)
        first[top, :] = jnp.dot(att[top, :], wo[...], preferred_element_type=F32)

        def step(n):
            rows = slice(h * half + n * norm_tile, h * half + (n + 1) * norm_tile)
            before = tok_ref[rows, :].astype(F32) if layer == 0 else hid[rows, :]
            normed, scaled, inverse = norm_rows(
                before + first[rows, :] + row(layer, 2), row(layer, 3), row(layer, 4)
            )
            first[rows, :] = normed
            flow[rows, :] = normed.astype(BF16)
            xh1[rows, :] = scaled
            r1[rows, :] = jnp.broadcast_to(inverse, (norm_tile, LANES))

        for n in range(half // norm_tile):
            step(n)
        if h == 1:
            save(layer, 2, xh1, xh1_out.at[layer])
            save(layer, 3, r1, r1_out.at[layer])
            save(layer, 4, flow, flow_out.at[layer])

    def in_part(layer, part):
        wi = bufs[layer][2]
        if part == 0:
            saved(layer - 1, 5, 6)
        bias_row = row(layer, 5 + part)
        tile = 256
        for sub in range(width // tile):
            bias = bias_row[:, sub * tile : (sub + 1) * tile]
            cols = slice(part * width + sub * tile, part * width + (sub + 1) * tile)

            def step(n, carry, cols=cols, bias=bias):
                rows = pl.ds(pl.multiple_of(n * half, half), half)
                inner = jnp.dot(flow[rows, :], wi[:, cols], preferred_element_type=F32) + bias
                value, change = gelu_pair(inner)
                active[rows, cols] = value.astype(BF16)
                slope[rows, cols] = change.astype(BF16)
                return carry

            lax.fori_loop(0, 2, step, 0)
        if part == 3:
            save(layer, 5, active, active_out.at[layer])
            save(layer, 6, slope, slope_out.at[layer])

    def back_half(layer, h):
        wb = bufs[layer][3]
        if h == 0:
            saved(layer - 1, 7, 8)
        top = slice(h * half, (h + 1) * half)
        first[top, :] = first[top, :] + jnp.dot(
            active[top, :], wb[...], preferred_element_type=F32
        )

        def step(n):
            rows = slice(h * half + n * norm_tile, h * half + (n + 1) * norm_tile)
            normed, scaled, inverse = norm_rows(
                first[rows, :] + row(layer, 9), row(layer, 10), row(layer, 11)
            )
            xh2[rows, :] = scaled
            r2[rows, :] = jnp.broadcast_to(inverse, (norm_tile, LANES))
            if layer == LAYERS - 1:
                act_out[rows, :] = normed.astype(BF16)
            else:
                hid[rows, :] = normed
                hlow[rows, :] = normed.astype(BF16)

        for n in range(half // norm_tile):
            step(n)
        if h == 1:
            save(layer, 7, xh2, xh2_out.at[layer])
            save(layer, 8, r2, r2_out.at[layer])
            if layer == 0:
                save(layer, 9, hlow, hlow_out)

    compute = {"qkv": qkv, "att": attend, "out": out_half, "in": in_part, "back": back_half}
    for what, *at in ORDER:
        if what in compute:
            compute[what](*at)
        elif what == "pre":
            prepare(*at)
        else:
            comm(what, *at)
    vec_save = pltpu.make_async_copy(vec, vec_out, save_sem.at[1, 9])
    vec_save.start()
    for copy in started:
        copy.wait_send()
    for copy in wcopies:
        copy.wait()
    saved(0, 9)
    saved(1, *range(9))
    vec_save.wait()


def forward(tokens, segment_ids, vectors, *masters):
    count, width = tokens.shape
    ff = masters[2].shape[2]
    copies = len(gather_pieces([m.shape[1:] for m in masters])) * COPY_KINDS + VEC_KINDS
    any_spec = pl.BlockSpec(memory_space=pltpu.HBM)
    vmem = pl.BlockSpec(memory_space=pltpu.VMEM)

    def shape(dims, kind):
        return jax.ShapeDtypeStruct(dims, kind)

    out_shape = (
        shape((count, width), BF16),
        shape((LAYERS, width, 3 * width), BF16),
        shape((LAYERS, width, width), BF16),
        shape((LAYERS, width, ff), BF16),
        shape((LAYERS, ff, width), BF16),
        shape((16 * LAYERS, width), F32),
        shape((LAYERS, count, 3 * width), BF16),
        shape((LAYERS, count, width), BF16),
        shape((LAYERS, count, width), F32),
        shape((LAYERS, count, LANES), F32),
        shape((LAYERS, count, width), BF16),
        shape((LAYERS, count, ff), BF16),
        shape((LAYERS, count, ff), BF16),
        shape((LAYERS, count, width), F32),
        shape((LAYERS, count, LANES), F32),
        shape((count, width), BF16),
    )
    weights = [
        pltpu.VMEM((width, 3 * width), BF16), pltpu.VMEM((width, width), BF16),
        pltpu.VMEM((width, ff), BF16), pltpu.VMEM((ff, width), BF16),
    ]
    scratch = weights * LAYERS + [pltpu.VMEM(m.shape, F32) for m in masters] + [
        pltpu.VMEM((8, 16 * LAYERS, LANES), BF16),
        pltpu.VMEM((16 * LAYERS, width), F32),
        pltpu.VMEM((count, width), F32),
        pltpu.VMEM((count, width), BF16),
        pltpu.VMEM((count, 3 * width), BF16),
        pltpu.VMEM((count, width), BF16),
        pltpu.VMEM((count, width), F32),
        pltpu.VMEM((count, width), F32),
        pltpu.VMEM((count, LANES), F32),
        pltpu.VMEM((count, width), BF16),
        pltpu.VMEM((count, ff), BF16),
        pltpu.VMEM((count, ff), BF16),
        pltpu.VMEM((count, width), F32),
        pltpu.VMEM((count, LANES), F32),
        pltpu.VMEM((segment_ids.shape[0], ROW, ROW), F32),
        pltpu.SemaphoreType.DMA((copies,)),
        pltpu.SemaphoreType.DMA((copies,)),
        pltpu.SemaphoreType.DMA((8,)),
        pltpu.SemaphoreType.DMA((8,)),
        pltpu.SemaphoreType.DMA((LAYERS, 10)),
    ]
    return pl.pallas_call(
        forward_kernel,
        name="forward",
        out_shape=out_shape,
        in_specs=[vmem, vmem, vmem] + [any_spec] * 4,
        out_specs=[vmem] + [any_spec] * (len(out_shape) - 1),
        scratch_shapes=scratch,
        compiler_params=pltpu.CompilerParams(
            collective_id=0, has_side_effects=True, vmem_limit_bytes=62 << 20
        ),
    )(tokens, segment_ids, vectors, *masters)


DEPTH = 6
Z_DEPTH = 12
CHUNKS = 12
TAIL = {21: (512, 256), 22: (256, 256, 256), 23: (256, 256, 256)}
BACK_ORDER = (
    ("t0", 1), ("t1", 1, 0), ("t1", 1, 1), (0, 0), (0, 1), (0, 2), (0, 3), ("t2", 1, 0), ("t2", 1, 1),
    (1, 0), (1, 1), ("t2", 1, 2), (1, 2), (1, 3), ("t2", 1, 3), ("t3", 1, 0), (0, 4), ("t3", 1, 1),
    (2, 0), (0, 5), ("t3", 1, 2), ("t3", 1, 3), (1, 4), (0, 6), (0, 7), ("t4", 1, 0), (2, 1), (1, 5),
    ("t4", 1, 1), (2, 2), ("t5", 1), (0, 8), ("t6", 1), (2, 3), ("t7", 1, 0), (3, 0), ("t7", 1, 1),
    ("t7", 1, 2), ("t7", 1, 3), (2, 4), (1, 6), (3, 1), ("t8", 1, 0), (0, 9), (4, 0), ("t8", 1, 1),
    (0, 10), ("t8", 1, 2), ("t9", 1, 0), (2, 5), (1, 7), (3, 2), ("t9", 1, 1), (4, 1), ("t0", 0),
    (3, 3), (5, 0), (3, 4), (4, 2), (2, 6), (1, 8), (1, 9), (3, 5), (1, 10), (0, 11), (4, 3), (5, 1),
    ("t1", 0, 0), (2, 7), (1, 11), (4, 4), (5, 2), (3, 6), ("t1", 0, 1), (0, 12), (0, 13), (0, 14),
    (0, 15), (4, 5), (5, 3), ("t2", 0, 0), (2, 8), (1, 12), (5, 4), ("t2", 0, 1), (2, 9), (4, 6),
    ("t2", 0, 2), (5, 5), ("t2", 0, 3), (2, 10), ("t3", 0, 0), (3, 7), (0, 16), ("t3", 0, 1), (0, 17),
    ("t3", 0, 2), (5, 6), (2, 11), (1, 13), (3, 8), (4, 7), ("t3", 0, 3), ("t4", 0, 0), ("t4", 0, 1),
    (2, 12), (3, 9), (1, 14), (3, 10), (4, 8), (5, 7), ("t5", 0), (3, 11), ("t6", 0), ("t7", 0, 0),
    ("t7", 0, 1), (2, 13), (1, 15), (3, 12), (1, 16), (1, 17), (0, 18), (4, 9), (4, 10), (5, 8),
    ("t7", 0, 2), (2, 14), (1, 18), (0, 19), (3, 13), (0, 20), (4, 11), ("t7", 0, 3), ("v", 0), (5, 9),
    ("t8", 0, 0), (2, 15), (1, 19), (0, 21), (0, 22), (4, 12), ("v", 1), ("t8", 0, 1), (0, 23),
    (0, 24), (5, 10), ("t8", 0, 2), (2, 16), (4, 13), ("t9", 0, 0), ("t9", 0, 1), (5, 11), (2, 17),
    (3, 14), (5, 12), (2, 18), (1, 20), (5, 13), (3, 15), (4, 14), (2, 19), (1, 21), (0, 25), ("v", 2),
    (3, 16), (4, 15), (5, 14), (3, 17), (3, 18), (4, 16), (5, 15), (2, 20), (1, 22), (1, 23), (1, 24),
    (3, 19), (4, 17), ("v", 3), (2, 21), (1, 25), (0, 26), (0, 27), (5, 16), (3, 20), (4, 18), (2, 22),
    (1, 26), (0, 28), (2, 23), (5, 17), (2, 24), (4, 19), ("v", 4), (3, 21), (2, 25), (1, 27), (5, 18),
    (3, 22), (4, 20), (2, 26), (1, 28), (3, 23), (3, 24), (4, 21), (5, 19), (3, 25), ("v", 5), (2, 27),
    (4, 22), (4, 23), (5, 20), (3, 26), (2, 28), (4, 24), (5, 21), (3, 27), (5, 22), (3, 28), (4, 25),
    (5, 23), (5, 24), (4, 26), (5, 25), (4, 27), (4, 28), (5, 26), (5, 27), (5, 28),
)


def reduce_items(width):
    items = []
    for chunk in range(LAYERS * CHUNKS):
        at = 0
        for cols in TAIL.get(chunk, (width,)):
            items.append((chunk, at, cols))
            at += cols
    return items


def backward_kernel(
    cot_ref, seg_ref, vec_ref, tok_in, hlow_in, wq_in, wo_in, wi_in, wb_in,
    joined_in, att_in, xh1_in, r1_in, flow_in, active_in, slope_in, xh2_in, r2_in,
    grad_ref, total_ref, vtotal_ref,
    wq, wo, wi, wb, joined, att, xh1, r1, flow, active, slope, xh2, r2, hin,
    ring, got_d, got_a, got_b, got_z1, got_z2, part_sum, gtwo, glow, dvec, dbin, mask,
    vsend, vgot_d, vgot_a, vgot_b, vgot_z1, vgot_z2,
    load_sem, d_send, d_recv, a_send, a_recv, b_send, b_recv, z_send, z_recv, v_send, v_recv,
):
    here = Place()
    tokens, width = gtwo.shape
    ff = active.shape[1]
    rows_per = ring.shape[4]
    core, x, y = here.core, here.x, here.y
    other_core, other_x, other_y = 1 - core, 1 - x, 1 - y
    to_mid = {"dp": 3 - here.z}
    inner = lax.rem(here.z + 1, 4) >= 2
    outer = jnp.logical_not(inner)
    greet((here.to_c, here.to_x, here.to_y, here.to_z, to_mid))

    sources = {
        "xh2": (xh2_in, xh2), "r2": (r2_in, r2), "active": (active_in, active), "wb": (wb_in, wb),
        "slope": (slope_in, slope), "flow": (flow_in, flow), "wi": (wi_in, wi),
        "xh1": (xh1_in, xh1), "r1": (r1_in, r1), "att": (att_in, att), "wo": (wo_in, wo),
        "joined": (joined_in, joined), "hin": (None, hin), "wq": (wq_in, wq),
    }
    order = list(sources)

    def load(layer, name):
        src, dst = sources[name]
        if name == "hin":
            src = tok_in if layer == 0 else hlow_in
        else:
            src = src.at[layer]
        return pltpu.make_async_copy(src, dst, load_sem.at[order.index(name)])

    early = 3
    for name in order[:early]:
        load(LAYERS - 1, name).start()

    def need(layer, *names):
        for name in names:
            load(layer, name).wait()

    def release(layer, *names):
        if layer > 0:
            for name in names:
                load(layer - 1, name).start()

    rows_here = seg_ref.shape[0]
    for r in range(rows_here):
        wide = jnp.broadcast_to(seg_ref[r : r + 1, :].astype(F32), (ROW, ROW))
        mask[r] = jnp.where(wide == wide.T, 1.0, 0.0)
    dvec[...] = jnp.zeros_like(dvec)

    def remote(src, dst, send, recv, device):
        return pltpu.make_async_remote_copy(
            src_ref=src, dst_ref=dst, send_sem=send, recv_sem=recv, device_id=device,
            device_id_type=MESH_ID,
        )

    items = reduce_items(width)

    def place(n):
        chunk, at, cols = items[n]
        return n % DEPTH, chunk % CHUNKS, cols // 2, slice(at, at + cols // 2), slice(at + cols // 2, at + cols)

    def copy_d(n):
        _, at, cols = items[n]
        b, s = place(n)[:2]
        src = ring.at[s, other_core, :, :, :, at : at + cols]
        return remote(src, got_d.at[b, :, :, :, :cols], d_send.at[b], d_recv.at[b], here.to_c)

    def copy_a(n, side):
        b, s, part, low, high = place(n)
        if side == 0:
            src, dev = ring.at[s, core, :, other_x, :, low], here.to_x
        else:
            src, dev = ring.at[s, core, other_y, :, :, high], here.to_y
        dst = got_a.at[b, side, :, :, :part]
        return remote(src, dst, a_send.at[b, side], a_recv.at[b, side], dev)

    def copy_b(n, side):
        b, s, part, low, high = place(n)
        if side == 0:
            src, dev = ring.at[s, core, other_y, x, :, low], here.to_y
        else:
            src, dev = ring.at[s, core, y, other_x, :, high], here.to_x
        dst = got_b.at[b, side, :, :part]
        return remote(src, dst, b_send.at[b, side], b_recv.at[b, side], dev)

    def copy_z(n, hop):
        chunk, at, cols = items[n]
        b, far = n % DEPTH, n % Z_DEPTH
        if hop == 0:
            src, dst, dev, sem = part_sum.at[b, :, :cols], got_z1.at[far, :, :cols], here.to_z, far
        elif hop == 1:
            src, dst, dev, sem = part_sum.at[b, :, :cols], got_z2.at[b, :, :cols], to_mid, Z_DEPTH + b
        else:
            src = total_ref.at[chunk, :, at : at + cols]
            dst, dev, sem = src, here.to_z, Z_DEPTH + DEPTH + n
        return remote(src, dst, z_send.at[sem], z_recv.at[sem], dev)

    def added(a, b):
        return (a.astype(F32) + b.astype(F32)).astype(BF16)

    def stage0(n):
        copy_d(n).start()

    def stage1(n):
        _, at, cols = items[n]
        b, s = place(n)[:2]
        cols_here = slice(at, at + cols)
        copy_d(n).wait_recv()

        def add_shard(i, carry):
            iy, ix = lax.div(i, 2), lax.rem(i, 2)
            ring[s, core, iy, ix, :, cols_here] = added(
                ring[s, core, iy, ix, :, cols_here], got_d[b, iy, ix, :, :cols]
            )
            return carry

        lax.fori_loop(0, 4, add_shard, 0)
        copy_a(n, 0).start()
        copy_a(n, 1).start()
        copy_d(n).wait_send()

    def stage2(n):
        b, s, part, low, high = place(n)
        copy_a(n, 0).wait_recv()
        for i in range(2):
            ring[s, core, i, x, :, low] = added(ring[s, core, i, x, :, low], got_a[b, 0, i, :, :part])
        copy_b(n, 0).start()
        copy_a(n, 1).wait_recv()
        for i in range(2):
            ring[s, core, y, i, :, high] = added(ring[s, core, y, i, :, high], got_a[b, 1, i, :, :part])
        copy_b(n, 1).start()
        copy_a(n, 0).wait_send()
        copy_a(n, 1).wait_send()

    def stage3(n):
        b, s, part, low, high = place(n)
        if n >= Z_DEPTH:
            @pl.when(outer)
            def _():
                copy_z(n - Z_DEPTH, 2).wait_recv()

        copy_b(n, 0).wait_recv()
        part_sum[b, :, :part] = added(ring[s, core, y, x, :, low], got_b[b, 0, :, :part])
        copy_b(n, 1).wait_recv()
        part_sum[b, :, part : 2 * part] = added(ring[s, core, y, x, :, high], got_b[b, 1, :, :part])

        @pl.when(outer)
        def _():
            copy_z(n, 0).start()

        copy_b(n, 0).wait_send()
        copy_b(n, 1).wait_send()

    def stage4(n):
        b, cols = n % DEPTH, items[n][2]

        @pl.when(outer)
        def _():
            copy_z(n, 0).wait_send()

        @pl.when(inner)
        def _():
            copy_z(n, 0).wait_recv()
            part_sum[b, :, :cols] = added(part_sum[b, :, :cols], got_z1[n % Z_DEPTH, :, :cols])
            copy_z(n, 1).start()

    def stage5(n):
        chunk, at, cols = items[n]
        b = n % DEPTH

        @pl.when(inner)
        def _():
            copy_z(n, 1).wait_recv()
            copy_z(n, 1).wait_send()
            total_ref[chunk, :, at : at + cols] = added(part_sum[b, :, :cols], got_z2[b, :, :cols])
            copy_z(n, 2).start()

    stages = (stage0, stage1, stage2, stage3, stage4, stage5)

    def vcopy(at):
        src, dst, dev = (
            (vsend.at[other_core], vgot_d, here.to_c),
            (vsend.at[core, :, other_x], vgot_a, here.to_x),
            (vsend.at[core, other_y, x], vgot_b, here.to_y),
            (vsend.at[core, y, x], vgot_z1, here.to_z),
            (vsend.at[core, y, x], vgot_z2, to_mid),
            (vtotal_ref, vtotal_ref, here.to_z),
        )[at]
        return remote(src, dst, v_send.at[at], v_recv.at[at], dev)

    def vstage(at):
        if at == 0:
            share = width // 8
            lane = lax.broadcasted_iota(jnp.int32, (width, LANES), 1)
            column = lax.broadcasted_iota(jnp.int32, (width, LANES), 0)
            low = dvec[...].astype(BF16)
            for owner in range(8):
                pick = (column == lane + owner * share) & (lane < share)
                vsend[owner % 2, owner // 4, (owner // 2) % 2] = jnp.dot(
                    low, jnp.where(pick, 1.0, 0.0).astype(BF16), preferred_element_type=F32
                ).astype(BF16)
            vcopy(0).start()
        elif at == 1:
            vcopy(0).wait_recv()
            for i in range(4):
                vsend[core, i // 2, i % 2] = added(vsend[core, i // 2, i % 2], vgot_d[i // 2, i % 2])
            vcopy(1).start()
        elif at == 2:
            vcopy(1).wait_recv()
            for i in range(2):
                vsend[core, i, x] = added(vsend[core, i, x], vgot_a[i])
            vcopy(2).start()
        elif at == 3:
            vcopy(2).wait_recv()
            vsend[core, y, x] = added(vsend[core, y, x], vgot_b[...])

            @pl.when(outer)
            def _():
                vcopy(3).start()
        elif at == 4:
            @pl.when(inner)
            def _():
                vcopy(3).wait_recv()
                vsend[core, y, x] = added(vsend[core, y, x], vgot_z1[...])
                vcopy(4).start()
        elif at == 5:
            @pl.when(inner)
            def _():
                vcopy(4).wait_recv()
                vcopy(4).wait_send()
                vtotal_ref[...] = added(vsend[core, y, x], vgot_z2[...])
                vcopy(5).start()
                vcopy(5).wait_send()

            @pl.when(outer)
            def _():
                vcopy(3).wait_send()
                vcopy(5).wait_recv()

            for early in range(3):
                vcopy(early).wait_send()

    tile = 64
    half = tokens // 2

    def norm_back(layer, first_row, grad_in, scaled, inverse, grad_out, bias_row):
        base = 16 * layer
        gain = vec_ref[base + first_row : base + first_row + 1, :]

        def step(n, carry):
            rows = pl.ds(pl.multiple_of(n * tile, tile), tile)
            grad = grad_in[rows, :]
            hat = scaled[rows, :]
            lifted = grad * gain
            left = jnp.mean(lifted, axis=-1, keepdims=True)
            right = jnp.mean(lifted * hat, axis=-1, keepdims=True)
            result = inverse[rows, :1] * (lifted - left - hat * right)
            grad_out[rows, :] = result
            glow[rows, :] = result.astype(BF16)
            return (
                carry[0] + jnp.sum(grad * hat, axis=0, keepdims=True),
                carry[1] + jnp.sum(grad, axis=0, keepdims=True),
                carry[2] + jnp.sum(result, axis=0, keepdims=True),
            )

        nil = jnp.zeros((1, width), F32)
        sums = lax.fori_loop(0, tokens // tile, step, (nil, nil, nil))
        dvec[base + first_row : base + first_row + 1, :] = sums[0]
        dvec[base + first_row + 1 : base + first_row + 2, :] = sums[1]
        dvec[base + bias_row : base + bias_row + 1, :] = sums[2]

    def tn(left, right):
        return lax.dot_general(left, right, (((0,), (0,)), ((), ())), preferred_element_type=F32)

    def nt(left, right):
        return lax.dot_general(left, right, (((1,), (1,)), ((), ())), preferred_element_type=F32)

    def task0(layer):
        need(layer, "xh2", "r2")
        if layer == LAYERS - 1:
            for name in order[early:]:
                load(layer, name).start()
            grad_ref[...] = cot_ref[...].astype(F32)
        norm_back(layer, 10, grad_ref, xh2, r2, gtwo, 9)
        release(layer, "xh2", "r2")

    def task1(layer, at):
        if at == 0:
            need(layer, "active")
        rows_f = ff // 8

        def step(owner, carry):
            part = tn(active[:, pl.ds(pl.multiple_of(owner * rows_f, LANES), rows_f)], glow[...])
            oc, ox, oy = lax.rem(owner, 2), lax.rem(lax.div(owner, 2), 2), lax.div(owner, 4)
            for j in range(rows_f // rows_per):
                ring[j, oc, oy, ox] = part[j * rows_per : (j + 1) * rows_per].astype(BF16)
            return carry

        lax.fori_loop(4 * at, 4 * at + 4, step, 0)
        if at == 1:
            release(layer, "active")

    def task2(layer, at, of=4):
        if at == 0:
            need(layer, "wb", "slope")
        cols_at = 256
        count = ff // cols_at // of

        def step(n, carry):
            cols = pl.ds(pl.multiple_of(n * cols_at, cols_at), cols_at)
            sums = jnp.zeros((1, cols_at), F32)
            for h in range(2):
                rows = slice(h * half, (h + 1) * half)
                inner_grad = (nt(glow[rows, :], wb[cols, :]) * slope[rows, cols].astype(F32)).astype(BF16)
                slope[rows, cols] = inner_grad
                sums = sums + jnp.sum(inner_grad.astype(F32), axis=0, keepdims=True)
            dbin[:, cols] = sums
            return carry

        lax.fori_loop(at * count, (at + 1) * count, step, 0)
        if at == of - 1:
            release(layer, "wb")
            for j in range(ff // width):
                dvec[16 * layer + 5 + j : 16 * layer + 6 + j, :] = dbin[:, j * width : (j + 1) * width]

    def weight_chunk(at, left, right):
        quarter = width // 2

        for iy in range(2):
            part = tn(left[:, iy * quarter : (iy + 1) * quarter], right)
            for i in range(4):
                ring[at, i % 2, iy, i // 2] = part[i * rows_per : (i + 1) * rows_per].astype(BF16)

    def task3(layer, j):
        if j == 0:
            need(layer, "flow")
        weight_chunk(4 + j, flow, slope[:, j * width : (j + 1) * width])
        if j == 3:
            release(layer, "flow")

    def add_product(target, base, left, right, h):
        rows = slice(h * half, (h + 1) * half)
        block = 256

        for j in range(width // block):
            cols = slice(j * block, (j + 1) * block)
            product = nt(left[rows, :], right[cols, :])
            if base is not None:
                product = base[rows, cols] + product
            target[rows, cols] = product.astype(target.dtype)

    def task4(layer, h):
        if h == 0:
            need(layer, "wi", "xh1", "r1")
        add_product(gtwo, gtwo, slope, wi, h)
        if h == 1:
            norm_back(layer, 3, gtwo, xh1, r1, gtwo, 2)
            release(layer, "slope", "wi", "xh1", "r1")

    def task5(layer):
        need(layer, "att")
        weight_chunk(8, att, glow[...])

    def task6(layer):
        need(layer, "wo")
        for h in range(2):
            add_product(att, None, glow, wo, h)
        release(layer, "wo")

    def task7(layer, r):
        if r == 0:
            need(layer, "joined")
        base = 16 * layer
        rows = slice(r * ROW, (r + 1) * ROW)
        first_head = lax.broadcasted_iota(jnp.int32, (ROW, LANES), 1) < HEAD_DIM
        seen = mask[r]
        seen = jnp.concatenate([seen, seen], axis=1) > 0.5

        def stacked(value):
            nil = jnp.zeros_like(value)
            return jnp.concatenate(
                [jnp.where(first_head, value, nil), jnp.where(first_head, nil, value)], axis=0
            )

        group = 3
        for first in range(0, HEADS // 2, group):
            lanes = [
                [slice(p * width + j * LANES, p * width + (j + 1) * LANES) for p in range(3)]
                for j in range(first, first + group)
            ]
            query, keys, value = ([joined[rows, lane[p]] for lane in lanes] for p in range(3))
            out_grad = [stacked(att[rows, lane[0]]) for lane in lanes]
            both = [stacked(q) for q in query]
            scores = [
                jnp.where(seen, nt(k, q) * HEAD_DIM ** (-0.5), NEGATIVE) for k, q in zip(keys, both)
            ]
            grad_probs = [nt(v, g) for v, g in zip(value, out_grad)]
            grown = [jnp.exp(s - jnp.max(s, axis=0, keepdims=True)) for s in scores]
            probs = [e * (1.0 / jnp.sum(e, axis=0, keepdims=True)) for e in grown]
            grad_value = [
                jnp.dot(p.astype(BF16), g, preferred_element_type=F32).astype(BF16)
                for p, g in zip(probs, out_grad)
            ]
            centre = [jnp.sum(p * g, axis=0, keepdims=True) for p, g in zip(probs, grad_probs)]
            grad_scores = [(p * (g - c)).astype(BF16) for p, g, c in zip(probs, grad_probs, centre)]
            wide = [tn(g, k) for g, k in zip(grad_scores, keys)]
            grad_key = [
                jnp.dot(g, q, preferred_element_type=F32) * HEAD_DIM ** (-0.5)
                for g, q in zip(grad_scores, both)
            ]
            grad_query = [
                (jnp.where(first_head, w[:ROW], w[ROW:]) * HEAD_DIM ** (-0.5)).astype(BF16) for w in wide
            ]
            for at, lane in enumerate(lanes):
                joined[rows, lane[0]] = grad_query[at]
                joined[rows, lane[1]] = grad_key[at].astype(BF16)
                joined[rows, lane[2]] = grad_value[at]
                dvec[base : base + 1, lane[0]] += jnp.sum(
                    grad_query[at].astype(F32), axis=0, keepdims=True
                )
                dvec[base + 1 : base + 2, lane[0]] += jnp.sum(
                    grad_value[at].astype(F32), axis=0, keepdims=True
                )
        if r == rows_here - 1:
            release(layer, "att")

    def task8(layer, j):
        if j == 0:
            need(layer, "hin")
        weight_chunk(9 + j, hin, joined[:, j * width : (j + 1) * width])
        if j == 2:
            release(layer, "hin")

    def task9(layer, h):
        if h == 0:
            need(layer, "wq")
        add_product(grad_ref, gtwo, joined, wq, h)
        if h == 1:
            release(layer, "joined", "wq")

    tasks = {
        "t0": task0, "t1": task1, "t2": task2, "t3": task3, "t4": task4,
        "t5": task5, "t6": task6, "t7": task7, "t8": task8, "t9": task9,
    }
    for what, *at in BACK_ORDER:
        if what == "v":
            vstage(*at)
        elif what in tasks:
            tasks[what](*at)
        else:
            stages[what](*at)

    @pl.when(inner)
    def _():
        for n in range(len(items)):
            copy_z(n, 2).wait_send()

    @pl.when(outer)
    def _():
        for n in range(len(items) - Z_DEPTH, len(items)):
            copy_z(n, 2).wait_recv()


def backward(cotangent, segment_ids, vec, tokens, hlow, weights, kept):
    count, width = tokens.shape
    ff = weights[2].shape[2]
    rows_per = width // 8
    hbm = pl.BlockSpec(memory_space=pltpu.HBM)
    vmem = pl.BlockSpec(memory_space=pltpu.VMEM)
    small = vec.shape[0]
    out_shape = (
        jax.ShapeDtypeStruct((count, width), F32),
        jax.ShapeDtypeStruct((LAYERS * CHUNKS, rows_per, width), BF16),
        jax.ShapeDtypeStruct((small, LANES), BF16),
    )
    dma = pltpu.SemaphoreType.DMA
    z_sems = Z_DEPTH + DEPTH + len(reduce_items(width))
    scratch = [
        pltpu.VMEM((width, 3 * width), BF16), pltpu.VMEM((width, width), BF16),
        pltpu.VMEM((width, ff), BF16), pltpu.VMEM((ff, width), BF16),
        pltpu.VMEM((count, 3 * width), BF16), pltpu.VMEM((count, width), BF16),
        pltpu.VMEM((count, width), F32), pltpu.VMEM((count, LANES), F32),
        pltpu.VMEM((count, width), BF16), pltpu.VMEM((count, ff), BF16), pltpu.VMEM((count, ff), BF16),
        pltpu.VMEM((count, width), F32), pltpu.VMEM((count, LANES), F32),
        pltpu.VMEM((count, width), BF16),
        pltpu.VMEM((CHUNKS, 2, 2, 2, rows_per, width), BF16),
        pltpu.VMEM((DEPTH, 2, 2, rows_per, width), BF16),
        pltpu.VMEM((DEPTH, 2, 2, rows_per, width // 2), BF16),
        pltpu.VMEM((DEPTH, 2, rows_per, width // 2), BF16),
        pltpu.VMEM((Z_DEPTH, rows_per, width), BF16),
        pltpu.VMEM((DEPTH, rows_per, width), BF16),
        pltpu.VMEM((DEPTH, rows_per, width), BF16),
        pltpu.VMEM((count, width), F32), pltpu.VMEM((count, width), BF16),
        pltpu.VMEM((small, width), F32), pltpu.VMEM((1, ff), F32),
        pltpu.VMEM((segment_ids.shape[0], ROW, ROW), F32),
        pltpu.VMEM((2, 2, 2, small, LANES), BF16), pltpu.VMEM((2, 2, small, LANES), BF16),
        pltpu.VMEM((2, small, LANES), BF16), pltpu.VMEM((small, LANES), BF16),
        pltpu.VMEM((small, LANES), BF16), pltpu.VMEM((small, LANES), BF16),
        dma((14,)), dma((DEPTH,)), dma((DEPTH,)), dma((DEPTH, 2)), dma((DEPTH, 2)),
        dma((DEPTH, 2)), dma((DEPTH, 2)), dma((z_sems,)), dma((z_sems,)), dma((6,)), dma((6,)),
    ]
    return pl.pallas_call(
        backward_kernel,
        name="backward",
        out_shape=out_shape,
        in_specs=[vmem, vmem, vmem] + [hbm] * 15,
        out_specs=[vmem, vmem, vmem],
        scratch_shapes=scratch,
        compiler_params=pltpu.CompilerParams(
            collective_id=1, has_side_effects=True, vmem_limit_bytes=62 << 20
        ),
    )(cotangent, segment_ids, vec, tokens, hlow, *weights, *kept)


SLOTS = 4


def adam_rule(weight, gradient, moment_one, moment_two, step_rate):
    first_moment = BETA_FIRST * moment_one + (1.0 - BETA_FIRST) * gradient
    second_moment = BETA_SECOND * moment_two + (1.0 - BETA_SECOND) * gradient * gradient
    first_hat = first_moment / (1.0 - BETA_FIRST**STEP)
    second_hat = second_moment / (1.0 - BETA_SECOND**STEP)
    updated = weight - step_rate * (
        first_hat / (jnp.sqrt(second_hat) + ADAM_EPSILON) + WEIGHT_DECAY * weight
    )
    return updated, second_moment


def adam_kernel(
    total_ref, vtotal_ref, vectors_ref, vector_moments_ref, act_in, grad_in,
    q_w, o_w, i_w, b_w, q_m, o_m, i_m, b_m,
    act_out, grad_out, q_g, o_g, i_g, b_g, q_n, o_n, i_n, b_n, q_s, o_s, i_s, b_s, v_g, v_n, v_s,
    held, summed, made, act_held, grad_held, in_sem, out_sem, pass_sem,
):
    rows, width = held.shape[2:]
    kinds = {
        "q": (q_w, q_m, (q_g, q_n, q_s)), "o": (o_w, o_m, (o_g, o_n, o_s)),
        "i": (i_w, i_m, (i_g, i_n, i_s)), "b": (b_w, b_m, (b_g, b_n, b_s)),
    }
    chunks = []
    for n in range(LAYERS * CHUNKS):
        layer, at = LAYERS - 1 - n // CHUNKS, n % CHUNKS
        if at < 4:
            place = ("b", layer, slice(at * rows, (at + 1) * rows), slice(0, width))
        elif at < 8:
            place = ("i", layer, slice(0, rows), slice((at - 4) * width, (at - 3) * width))
        elif at == 8:
            place = ("o", layer, slice(0, rows), slice(0, width))
        else:
            place = ("q", layer, slice(0, rows), slice((at - 9) * width, (at - 8) * width))
        chunks.append(place)

    def reads(n):
        kind, layer, r, c = chunks[n]
        weight, moments, _ = kinds[kind]
        b = n % SLOTS
        sources = (weight.at[layer, r, c], moments.at[0, layer, r, c], moments.at[1, layer, r, c])
        return [
            pltpu.make_async_copy(source, held.at[b, k], in_sem.at[b, k])
            for k, source in enumerate(sources)
        ] + [pltpu.make_async_copy(total_ref.at[n], summed.at[b], in_sem.at[b, 3])]

    def writes(n):
        kind, layer, r, c = chunks[n]
        b = n % SLOTS
        return [
            pltpu.make_async_copy(made.at[b, k], target.at[layer, r, c], out_sem.at[b, k])
            for k, target in enumerate(kinds[kind][2])
        ]

    for n in range(SLOTS - 1):
        for copy in reads(n):
            copy.start()
    passing = (
        pltpu.make_async_copy(act_in, act_held, pass_sem.at[0]),
        pltpu.make_async_copy(grad_in, grad_held, pass_sem.at[1]),
    )
    passed = (
        pltpu.make_async_copy(act_held, act_out, pass_sem.at[2]),
        pltpu.make_async_copy(grad_held, grad_out, pass_sem.at[3]),
    )
    for copy in passing:
        copy.start()
    share = vectors_ref.shape[2]
    for layer in range(LAYERS):
        gradient = vtotal_ref[16 * layer : 16 * layer + 12, :share].astype(F32)
        updated, second = adam_rule(
            vectors_ref[:, layer, :], gradient, vector_moments_ref[0, :, layer, :],
            vector_moments_ref[1, :, layer, :], RATE_VECTOR,
        )
        v_g[:, layer, :] = gradient
        v_n[:, layer, :] = updated
        v_s[:, layer, :] = second
    tile = 32
    for n in range(LAYERS * CHUNKS):
        b = n % SLOTS
        if n == SLOTS:
            for early, late in zip(passing, passed):
                early.wait()
                late.start()
        if n + SLOTS - 1 < LAYERS * CHUNKS:
            for copy in reads(n + SLOTS - 1):
                copy.start()
        for copy in reads(n):
            copy.wait()
        if n >= SLOTS:
            for copy in writes(n - SLOTS):
                copy.wait()

        def step(t, carry, n=n, b=b):
            r = pl.ds(pl.multiple_of(t * tile, tile), tile)
            gradient = summed[b, r, :].astype(F32)
            updated, second = adam_rule(
                held[b, 0, r, :], gradient, held[b, 1, r, :], held[b, 2, r, :], RATE_MATRIX
            )
            made[b, 0, r, :] = gradient
            made[b, 1, r, :] = updated
            made[b, 2, r, :] = second
            return carry

        lax.fori_loop(0, rows // tile, step, 0)
        for copy in writes(n):
            copy.start()
    for n in range(LAYERS * CHUNKS - SLOTS, LAYERS * CHUNKS):
        for copy in writes(n):
            copy.wait()
    for copy in passed:
        copy.wait()


def adam(activations, grad, total, vtotal, masters, moments):
    rows, width = total.shape[1:]
    hbm = pl.BlockSpec(memory_space=pltpu.HBM)
    vmem = pl.BlockSpec(memory_space=pltpu.VMEM)
    matrices, vectors = masters[:4], masters[4].transpose(1, 0, 2)
    passed = [jax.ShapeDtypeStruct(p.shape, p.dtype) for p in (activations, grad)]
    matrix_shapes = [jax.ShapeDtypeStruct(m.shape, F32) for m in matrices]
    vector_shape = jax.ShapeDtypeStruct(vectors.shape, F32)
    out = pl.pallas_call(
        adam_kernel,
        name="adam",
        out_shape=passed + matrix_shapes * 3 + [vector_shape] * 3,
        in_specs=[hbm] + [vmem] * 3 + [hbm] * 10,
        out_specs=[hbm] * 14 + [vmem] * 3,
        scratch_shapes=[
            pltpu.VMEM((SLOTS, 3, rows, width), F32), pltpu.VMEM((SLOTS, rows, width), BF16),
            pltpu.VMEM((SLOTS, 3, rows, width), F32),
            pltpu.VMEM(activations.shape, BF16), pltpu.VMEM(grad.shape, F32),
            pltpu.SemaphoreType.DMA((SLOTS, 4)), pltpu.SemaphoreType.DMA((SLOTS, 3)),
            pltpu.SemaphoreType.DMA((4,)),
        ],
        compiler_params=pltpu.CompilerParams(vmem_limit_bytes=62 << 20),
    )(
        total, vtotal, vectors, moments[4].transpose(0, 2, 1, 3), activations, grad, *matrices,
        *moments[:4],
    )
    gradients, updates, states = out[2:6], out[6:10], out[10:14]
    vector_outs = [v.transpose(1, 0, 2) for v in out[14:]]
    return (
        out[0], out[1], *gradients, vector_outs[0], *updates, vector_outs[1], *states, vector_outs[2]
    )


def norm_forward(values, gain_row, shift_row):
    centered = values - jnp.mean(values, axis=-1, keepdims=True)
    inverse = lax.rsqrt(jnp.mean(centered * centered, axis=-1, keepdims=True) + EPSILON)
    scaled = centered * inverse
    return (scaled * gain_row + shift_row, scaled, inverse)


def norm_backward(grad_out, scaled, inverse, gain_row):
    grad_scaled = grad_out * gain_row
    grad_in = inverse * (
        grad_scaled
        - jnp.mean(grad_scaled, axis=-1, keepdims=True)
        - scaled * jnp.mean(grad_scaled * scaled, axis=-1, keepdims=True)
    )
    return (grad_in, jnp.sum(grad_out * scaled, axis=0), jnp.sum(grad_out, axis=0))


def score_block(queries, key_rows, same_segment):
    scores = jnp.einsum(
        "rqhe,rkhe->rhqk", queries, key_rows, preferred_element_type=jnp.float32
    ) * HEAD_DIM ** (-0.5)
    return jnp.where(same_segment, scores, NEGATIVE)


def layer_forward(hidden, same_segment, weights):
    qkv_used, out_used, in_used, back_used, vector_low = weights
    vector = vector_low.astype(jnp.float32)
    row_count = same_segment.shape[0]
    model_width = out_used.shape[0]
    hidden_low = hidden.astype(jnp.bfloat16)
    bias_qkv = jnp.concatenate([vector[0], jnp.zeros_like(vector[0]), vector[1]])
    joined = (jnp.dot(hidden_low, qkv_used, preferred_element_type=jnp.float32) + bias_qkv).astype(
        jnp.bfloat16
    )
    split_qkv = joined.reshape(row_count, -1, 3, HEADS, HEAD_DIM)
    scores = score_block(split_qkv[:, :, 0], split_qkv[:, :, 1], same_segment)
    row_top = jnp.max(scores, axis=-1, keepdims=True)
    log_total = row_top + jnp.log(jnp.sum(jnp.exp(scores - row_top), axis=-1, keepdims=True))
    prob_low = jnp.exp(scores - log_total).astype(jnp.bfloat16)
    attended = jnp.einsum(
        "rhqk,rkhe->rqhe", prob_low, split_qkv[:, :, 2], preferred_element_type=jnp.float32
    )
    attended_low = attended.reshape(-1, model_width).astype(jnp.bfloat16)
    branch = jnp.dot(attended_low, out_used, preferred_element_type=jnp.float32) + vector[2]
    first_norm, scaled_one, inverse_one = norm_forward(hidden + branch, vector[3], vector[4])
    first_low = first_norm.astype(jnp.bfloat16)
    inner_pre = jnp.dot(first_low, in_used, preferred_element_type=jnp.float32) + vector[
        5:9
    ].reshape(-1)
    active_low = jax.nn.gelu(inner_pre, approximate=False).astype(jnp.bfloat16)
    outer_out = jnp.dot(active_low, back_used, preferred_element_type=jnp.float32) + vector[9]
    output, scaled_two, inverse_two = norm_forward(first_norm + outer_out, vector[10], vector[11])
    kept_state = (
        hidden_low,
        joined,
        log_total,
        attended_low,
        scaled_one,
        inverse_one,
        first_low,
        inner_pre,
        active_low,
        scaled_two,
        inverse_two,
    )
    return (output, kept_state)


def layer_backward(grad_out, same_segment, weights, kept_state):
    qkv_used, out_used, in_used, back_used, vector_low = weights
    vector = vector_low.astype(jnp.float32)
    (
        hidden_low,
        joined,
        log_total,
        attended_low,
        scaled_one,
        inverse_one,
        first_low,
        inner_pre,
        active_low,
        scaled_two,
        inverse_two,
    ) = kept_state
    row_count = same_segment.shape[0]
    model_width = out_used.shape[0]
    grad_two, gain_two_grad, shift_two_grad = norm_backward(
        grad_out, scaled_two, inverse_two, vector[10]
    )
    grad_outer = grad_two.astype(jnp.bfloat16)
    back_bias_grad = jnp.sum(grad_two, axis=0)
    back_weight_grad = jnp.einsum(
        "tf,td->fd", active_low, grad_outer, preferred_element_type=jnp.float32
    )
    grad_active = jnp.einsum("td,fd->tf", grad_outer, back_used, preferred_element_type=jnp.float32)
    gelu_value, gelu_pull = jax.vjp(
        lambda values: jax.nn.gelu(values, approximate=False), inner_pre
    )
    grad_inner = gelu_pull(grad_active)[0].astype(jnp.bfloat16)
    in_bias_grad = jnp.sum(grad_inner, axis=0, dtype=jnp.float32)
    in_weight_grad = jnp.einsum(
        "td,tf->df", first_low, grad_inner, preferred_element_type=jnp.float32
    )
    grad_first = grad_two + jnp.einsum(
        "tf,df->td", grad_inner, in_used, preferred_element_type=jnp.float32
    )
    grad_one, gain_one_grad, shift_one_grad = norm_backward(
        grad_first, scaled_one, inverse_one, vector[3]
    )
    grad_branch = grad_one.astype(jnp.bfloat16)
    out_bias_grad = jnp.sum(grad_one, axis=0)
    out_weight_grad = jnp.einsum(
        "td,te->de", attended_low, grad_branch, preferred_element_type=jnp.float32
    )
    grad_mixed = jnp.einsum("te,de->td", grad_branch, out_used, preferred_element_type=jnp.float32)
    grad_mixed = grad_mixed.astype(jnp.bfloat16).reshape(row_count, -1, HEADS, HEAD_DIM)
    split_qkv = joined.reshape(row_count, -1, 3, HEADS, HEAD_DIM)
    queries = split_qkv[:, :, 0]
    key_rows = split_qkv[:, :, 1]
    value_rows = split_qkv[:, :, 2]
    prob_full = jnp.exp(score_block(queries, key_rows, same_segment) - log_total)
    prob_low = prob_full.astype(jnp.bfloat16)
    grad_values = jnp.einsum(
        "rhqk,rqhe->rkhe", prob_low, grad_mixed, preferred_element_type=jnp.float32
    )
    grad_probs = jnp.einsum(
        "rqhe,rkhe->rhqk", grad_mixed, value_rows, preferred_element_type=jnp.float32
    )
    centred = jnp.sum(prob_full * grad_probs, axis=-1, keepdims=True)
    grad_scores = (prob_full * (grad_probs - centred)).astype(jnp.bfloat16)
    grad_queries = jnp.einsum(
        "rhqk,rkhe->rqhe", grad_scores, key_rows, preferred_element_type=jnp.float32
    ) * HEAD_DIM ** (-0.5)
    grad_keys = jnp.einsum(
        "rhqk,rqhe->rkhe", grad_scores, queries, preferred_element_type=jnp.float32
    ) * HEAD_DIM ** (-0.5)
    grad_joined = (
        jnp.stack([grad_queries, grad_keys, grad_values], axis=2)
        .reshape(-1, 3 * model_width)
        .astype(jnp.bfloat16)
    )
    qkv_bias_grad = jnp.sum(grad_joined, axis=0, dtype=jnp.float32)
    qkv_weight_grad = jnp.einsum(
        "td,tc->dc", hidden_low, grad_joined, preferred_element_type=jnp.float32
    )
    grad_hidden = grad_one + jnp.einsum(
        "tc,dc->td", grad_joined, qkv_used, preferred_element_type=jnp.float32
    )
    vector_grad = jnp.concatenate(
        [
            qkv_bias_grad[:model_width][None],
            qkv_bias_grad[2 * model_width :][None],
            out_bias_grad[None],
            gain_one_grad[None],
            shift_one_grad[None],
            in_bias_grad.reshape(4, model_width),
            back_bias_grad[None],
            gain_two_grad[None],
            shift_two_grad[None],
        ],
        axis=0,
    )
    return (
        grad_hidden,
        (qkv_weight_grad, out_weight_grad, in_weight_grad, back_weight_grad, vector_grad),
    )


def adam_step(weight, gradient, moment_one, moment_two, step_rate):
    first_moment = BETA_FIRST * moment_one + (1.0 - BETA_FIRST) * gradient
    second_moment = BETA_SECOND * moment_two + (1.0 - BETA_SECOND) * gradient * gradient
    first_hat = first_moment / (1.0 - BETA_FIRST**STEP)
    second_hat = second_moment / (1.0 - BETA_SECOND**STEP)
    updated = weight - step_rate * (
        first_hat / (jnp.sqrt(second_hat) + ADAM_EPSILON) + WEIGHT_DECAY * weight
    )
    return gradient, updated, second_moment


def update_layer(summed, masters, moments, layer_at):
    outcome = []
    for kind_at in range(5):
        step_rate = RATE_VECTOR if kind_at == 4 else RATE_MATRIX
        outcome.append(
            adam_step(
                masters[kind_at][layer_at],
                summed[kind_at],
                moments[kind_at][0, layer_at],
                moments[kind_at][1, layer_at],
                step_rate,
            )
        )
    return outcome


def local_parts(masters, layer_at):
    return tuple((master[layer_at].astype(jnp.bfloat16) for master in masters))


def collect(results, kind_at, member):
    return jnp.stack([layer_result[kind_at][member] for layer_result in results])


def on_device_any(
    tokens,
    segment_ids,
    cotangent,
    qkv_weight,
    out_weight,
    in_weight,
    back_weight,
    vectors,
    qkv_moments,
    out_moments,
    in_moments,
    back_moments,
    vector_moments,
):
    masters = (qkv_weight, out_weight, in_weight, back_weight, vectors)
    moments = (qkv_moments, out_moments, in_moments, back_moments, vector_moments)
    same_segment = (segment_ids[:, :, None] == segment_ids[:, None, :])[:, None]
    hidden = tokens.astype(jnp.float32)
    saved_states = []
    for layer_at in range(LAYERS):
        parts_now = local_parts(masters, layer_at)
        weights = (
            lax.all_gather(parts_now[0], "fsdp", axis=0, tiled=True),
            lax.all_gather(parts_now[1], "fsdp", axis=0, tiled=True),
            lax.all_gather(parts_now[2], "fsdp", axis=0, tiled=True),
            lax.all_gather(parts_now[3], "fsdp", axis=0, tiled=True),
            lax.all_gather(parts_now[4], "fsdp", axis=1, tiled=True),
        )
        hidden, kept_state = layer_forward(hidden, same_segment, weights)
        saved_states.append(kept_state)
    activations = hidden.astype(jnp.bfloat16)
    grad_hidden = cotangent.astype(jnp.float32)
    results = [None] * LAYERS
    for layer_at in reversed(range(LAYERS)):
        parts_now = local_parts(masters, layer_at)
        weights = (
            lax.all_gather(parts_now[0], "fsdp", axis=0, tiled=True),
            lax.all_gather(parts_now[1], "fsdp", axis=0, tiled=True),
            lax.all_gather(parts_now[2], "fsdp", axis=0, tiled=True),
            lax.all_gather(parts_now[3], "fsdp", axis=0, tiled=True),
            lax.all_gather(parts_now[4], "fsdp", axis=1, tiled=True),
        )
        grad_hidden, weight_grads = layer_backward(
            grad_hidden, same_segment, weights, saved_states[layer_at]
        )
        shards = (
            lax.psum_scatter(
                weight_grads[0].astype(jnp.bfloat16), "fsdp", scatter_dimension=0, tiled=True
            ).astype(jnp.float32),
            lax.psum_scatter(
                weight_grads[1].astype(jnp.bfloat16), "fsdp", scatter_dimension=0, tiled=True
            ).astype(jnp.float32),
            lax.psum_scatter(
                weight_grads[2].astype(jnp.bfloat16), "fsdp", scatter_dimension=0, tiled=True
            ).astype(jnp.float32),
            lax.psum_scatter(
                weight_grads[3].astype(jnp.bfloat16), "fsdp", scatter_dimension=0, tiled=True
            ).astype(jnp.float32),
            lax.psum_scatter(
                weight_grads[4].astype(jnp.bfloat16), "fsdp", scatter_dimension=1, tiled=True
            ).astype(jnp.float32),
        )
        totals = (
            lax.psum(shards[0].astype(jnp.bfloat16), "dp").astype(jnp.float32),
            lax.psum(shards[1].astype(jnp.bfloat16), "dp").astype(jnp.float32),
            lax.psum(shards[2].astype(jnp.bfloat16), "dp").astype(jnp.float32),
            lax.psum(shards[3].astype(jnp.bfloat16), "dp").astype(jnp.float32),
            lax.psum(shards[4].astype(jnp.bfloat16), "dp").astype(jnp.float32),
        )
        results[layer_at] = update_layer(totals, masters, moments, layer_at)
    return (
        activations,
        grad_hidden,
        collect(results, 0, 0),
        collect(results, 1, 0),
        collect(results, 2, 0),
        collect(results, 3, 0),
        collect(results, 4, 0),
        collect(results, 0, 1),
        collect(results, 1, 1),
        collect(results, 2, 1),
        collect(results, 3, 1),
        collect(results, 4, 1),
        collect(results, 0, 2),
        collect(results, 1, 2),
        collect(results, 2, 2),
        collect(results, 3, 2),
        collect(results, 4, 2),
    )


def on_device(
    tokens,
    segment_ids,
    cotangent,
    qkv_weight,
    out_weight,
    in_weight,
    back_weight,
    vectors,
    qkv_moments,
    out_moments,
    in_moments,
    back_moments,
    vector_moments,
):
    masters = (qkv_weight, out_weight, in_weight, back_weight, vectors)
    moments = (qkv_moments, out_moments, in_moments, back_moments, vector_moments)
    activations, wq, wo, wi, wb, vec, *kept, hlow = forward(
        tokens, segment_ids, vectors.transpose(1, 0, 2), *masters[:4]
    )
    grad, total, vtotal = backward(
        cotangent, segment_ids, vec, tokens, hlow, (wq, wo, wi, wb), kept
    )
    return adam(activations, grad, total, vtotal, masters, moments)


def solution(mesh):
    in_specs = (
        P(("fsdp", "dp"), None),
        P(("fsdp", "dp"), None),
        P(("fsdp", "dp"), None),
        P(None, "fsdp", None),
        P(None, "fsdp", None),
        P(None, "fsdp", None),
        P(None, "fsdp", None),
        P(None, None, "fsdp"),
        P(None, None, "fsdp", None),
        P(None, None, "fsdp", None),
        P(None, None, "fsdp", None),
        P(None, None, "fsdp", None),
        P(None, None, None, "fsdp"),
    )
    out_specs = (
        P(("fsdp", "dp"), None),
        P(("fsdp", "dp"), None),
        P(None, "fsdp", None),
        P(None, "fsdp", None),
        P(None, "fsdp", None),
        P(None, "fsdp", None),
        P(None, None, "fsdp"),
        P(None, "fsdp", None),
        P(None, "fsdp", None),
        P(None, "fsdp", None),
        P(None, "fsdp", None),
        P(None, None, "fsdp"),
        P(None, "fsdp", None),
        P(None, "fsdp", None),
        P(None, "fsdp", None),
        P(None, "fsdp", None),
        P(None, None, "fsdp"),
    )
    body = on_device if dict(mesh.shape) == {"fsdp": 8, "dp": 4} else on_device_any
    return jax.shard_map(
        body, mesh=mesh, in_specs=in_specs, out_specs=out_specs, check_vma=False
    )
```

```python
import jax
import jax.numpy as jnp
from jax import lax
from jax.experimental import pallas as pl
from jax.experimental.pallas import tpu as pltpu
from jax.sharding import PartitionSpec as P

HEADS = 12
HEAD_DIM = 64
LAYERS = 2
STEP = 3
ROW = 128
LANES = 128

EPSILON = 1e-05
NEGATIVE = -1000000000.0
BETA_FIRST = 0.5
BETA_SECOND = 0.5
WEIGHT_DECAY = 0.01
ADAM_EPSILON = 1e-08
RATE_MATRIX = 0.06
RATE_VECTOR = 0.5
MESH_ID = pl.DeviceIdType.MESH
BF16 = jnp.bfloat16
F32 = jnp.float32


class Place:
    def __init__(self):
        f = lax.axis_index("fsdp")
        z = lax.axis_index("dp")
        core = lax.rem(f, 2)
        x = lax.rem(lax.div(f, 2), 2)
        y = lax.div(f, 4)
        self.f, self.z, self.core, self.x, self.y = f, z, core, x, y
        self.fc = f + 1 - 2 * core
        self.fx = f + 2 - 4 * x
        self.fy = f + 4 - 8 * y
        self.fd = self.fx + 4 - 8 * y
        self.q = lax.rem(z, 2)
        self.to_c = {"fsdp": self.fc}
        self.to_x = {"fsdp": self.fx}
        self.to_y = {"fsdp": self.fy}
        self.to_z = {"dp": z + 1 - 2 * self.q}


def greet(partners):
    barrier = pltpu.get_barrier_semaphore()
    for partner in partners:
        pl.semaphore_signal(barrier, inc=1, device_id=partner, device_id_type=MESH_ID)


def greeted(partners):
    pl.semaphore_wait(pltpu.get_barrier_semaphore(), len(partners))


def norm_rows(values, gain_row, shift_row):
    centered = values - jnp.mean(values, axis=-1, keepdims=True)
    inverse = lax.rsqrt(jnp.mean(centered * centered, axis=-1, keepdims=True) + EPSILON)
    scaled = centered * inverse
    return scaled * gain_row + shift_row, scaled, inverse


def gelu_pair(value):
    cdf = 0.5 * (1.0 + lax.erf(value * 0.7071067811865476))
    slope = cdf + value * (0.3989422804014327 * jnp.exp(-0.5 * value * value))
    return value * cdf, slope


SPLITS = (3, 1, 2, 2)
COPY_KINDS = 14
VEC_KINDS = 7


def gather_pieces(shards):
    pieces = []
    for layer in range(LAYERS):
        for kind, (rows, cols) in enumerate(shards):
            count = SPLITS[kind]
            for i in range(count):
                if kind == 3:
                    pieces.append((layer, kind, i * rows // count, rows // count, 0, cols))
                else:
                    pieces.append((layer, kind, 0, rows, i * cols // count, cols // count))
    return pieces


ORDER = (
    ("own", 0), ("pre", 0), ("own", 1), ("pre", 1), ("own", 2), ("pre", 2), ("own", 3), ("s1", 0),
    ("s1", 1), ("s1", 2), ("own", 4), ("s1", 3), ("s2", 0), ("s2", 1), ("s2", 2), ("own", 5),
    ("s1", 4), ("s3", 0), ("s2", 3), ("s3", 1), ("s4", 0), ("qkv", 0, 0), ("s3", 2), ("s4", 1),
    ("qkv", 0, 1), ("own", 6), ("s4", 2), ("qkv", 0, 2), ("s1", 5), ("att", 0, 0), ("att", 0, 1),
    ("s2", 4), ("s3", 3), ("att", 0, 2), ("att", 0, 3), ("own", 7), ("s4", 3), ("out", 0, 0),
    ("s1", 6), ("out", 0, 1), ("s2", 5), ("s3", 4), ("s4", 4), ("in", 0, 0), ("own", 8), ("s1", 7),
    ("in", 0, 1), ("own", 9), ("s2", 6), ("s3", 5), ("s1", 8), ("s4", 5), ("in", 0, 2), ("own", 10),
    ("s2", 7), ("own", 11), ("in", 0, 3), ("own", 12), ("s1", 9), ("s2", 8), ("s3", 6), ("s1", 10),
    ("s3", 7), ("s4", 6), ("s1", 11), ("s4", 7), ("back", 0, 0), ("back", 0, 1), ("own", 13),
    ("s1", 12), ("s3", 8), ("s2", 9), ("s2", 10), ("s4", 8), ("qkv", 1, 0), ("s2", 11), ("own", 14),
    ("s1", 13), ("s3", 9), ("s3", 10), ("s2", 12), ("s4", 9), ("qkv", 1, 1), ("s3", 11), ("s4", 10),
    ("qkv", 1, 2), ("att", 1, 0), ("own", 15), ("att", 1, 1), ("s1", 14), ("att", 1, 2), ("s2", 13),
    ("att", 1, 3), ("s3", 12), ("s4", 11), ("out", 1, 0), ("out", 1, 1), ("s4", 12), ("in", 1, 0),
    ("s1", 15), ("in", 1, 1), ("s2", 14), ("s3", 13), ("s2", 15), ("s4", 13), ("in", 1, 2),
    ("in", 1, 3), ("s3", 14), ("s4", 14), ("s3", 15), ("s4", 15), ("back", 1, 0), ("back", 1, 1),
)


def forward_kernel(
    tok_ref, seg_ref, vec_ref, q_w, o_w, i_w, b_w,
    act_out, wq_out, wo_out, wi_out, wb_out, vec_out,
    joined_out, att_out, xh1_out, r1_out, flow_out, active_out, slope_out, xh2_out, r2_out, hlow_out,
    wq0, wo0, wi0, wb0, wq1, wo1, wi1, wb1, st_q, st_o, st_i, st_b, vslots, vec,
    hid, hlow, joined, att, first, xh1, r1, flow, active, slope, xh2, r2, mask,
    send_sem, recv_sem, own_sem, wout_sem, save_sem,
):
    here = Place()
    masters = (q_w, o_w, i_w, b_w)
    stages = (st_q, st_o, st_i, st_b)
    bufs = ((wq0, wo0, wi0, wb0), (wq1, wo1, wi1, wb1))
    wouts = (wq_out, wo_out, wi_out, wb_out)
    f, fx, fy, fd = here.f, here.fx, here.fy, here.fd
    pieces = gather_pieces([m.shape[1:] for m in masters])
    tokens, width = hid.shape
    half = tokens // 2

    def stage_copy(layer, kind):
        return pltpu.make_async_copy(
            masters[kind].at[layer], stages[kind].at[layer], own_sem.at[4 * layer + kind]
        )

    partners = (here.to_c, here.to_x, here.to_y, here.to_z)
    greet(partners)
    stage_copy(0, 0).start()
    mine = jnp.zeros((1,) + vslots.shape[1:], BF16)
    vslots[pl.ds(f, 1)] = mine
    share = vec_ref.shape[2]
    for layer in range(LAYERS):
        vslots[pl.ds(f, 1), 16 * layer : 16 * layer + 12, :share] = vec_ref[:, layer, :].astype(BF16)[None]
    rows_here = seg_ref.shape[0]
    for r in range(rows_here):
        wide = jnp.broadcast_to(seg_ref[r : r + 1, :].astype(F32), (ROW, ROW))
        mask[r] = jnp.where(wide == wide.T, 1.0, 0.0)

    started = []
    copies = {}

    def make(p, kind):
        layer, matrix, row_at, rows, col_at, cols = pieces[p]
        buf = bufs[layer][matrix]
        shard_rows = masters[matrix].shape[1]
        third = cols // 3
        two = 2 * third
        c_xy = pl.multiple_of(col_at + here.q * third, LANES)
        c_b = pl.multiple_of(c_xy + third, LANES)
        c_z = pl.multiple_of(col_at + here.q * two, LANES)
        c_w = pl.multiple_of(col_at + (1 - here.q) * two, LANES)

        def win(owner, col, wide):
            at = pl.multiple_of(owner * shard_rows + row_at, 32)
            return buf.at[pl.ds(at, rows), pl.ds(col, wide)]

        owner, col, wide, device = (
            (f, col_at, cols, here.to_c), (f, c_xy, two, here.to_x), (f, c_xy, two, here.to_y),
            (fx, c_xy, two, here.to_c), (fx, c_xy, third, here.to_y), (fx, c_z, third, here.to_z),
            (fy, c_xy, two, here.to_c), (fy, c_b, third, here.to_x), (fy, c_z, third, here.to_z),
            (fd, c_xy, two, here.to_c), (fd, c_z, third, here.to_z),
            (fx, c_w, third, here.to_c), (fy, c_w, third, here.to_c), (fd, c_w, third, here.to_c),
        )[kind]
        window = win(owner, col, wide)
        slot = p * COPY_KINDS + kind
        return pltpu.make_async_remote_copy(
            src_ref=window, dst_ref=window, send_sem=send_sem.at[slot], recv_sem=recv_sem.at[slot],
            device_id=device, device_id_type=MESH_ID,
        )

    def start(p, *kinds):
        for kind in kinds:
            copy = make(p, kind)
            copy.start()
            copies[p, kind] = copy
            started.append(copy)

    def arrived(p, *kinds):
        for kind in kinds:
            copies[p, kind].wait_recv()

    def cast_own(p):
        layer, matrix, row_at, rows, col_at, cols = pieces[p]
        if row_at == 0 and col_at == 0:
            stage_copy(layer, matrix).wait()
        stage, buf = stages[matrix], bufs[layer][matrix]
        shard_rows = stage.shape[1]
        tile = 32

        def step(n, carry):
            at = pl.multiple_of(row_at + n * tile, tile)
            to = pl.multiple_of(f * shard_rows + row_at + n * tile, tile)
            buf[pl.ds(to, tile), col_at : col_at + cols] = stage[
                layer, pl.ds(at, tile), col_at : col_at + cols
            ].astype(BF16)
            return carry

        lax.fori_loop(0, rows // tile, step, 0)

    def send_own(p):
        if p > 0:
            cast_own(p)
        start(p, 1, 2, 0)
        if p == 0:
            for later in range(1, 4 * LAYERS):
                stage_copy(later // 4, later % 4).start()

    wcopies = []

    def comm(what, p):
        if what == "own":
            send_own(p)
        elif what == "s1":
            arrived(p, 1, 2)
            start(p, 4, 7, 5, 8, 3, 6)
        elif what == "s2":
            arrived(p, 4, 7)
            start(p, 10, 9)
        elif what == "s3":
            arrived(p, 5, 8, 10)
            start(p, 11, 12, 13)
        else:
            arrived(p, 0, 3, 6, 9, 11, 12, 13)
            layer, matrix = pieces[p][:2]
            if p + 1 == len(pieces) or pieces[p + 1][1] != matrix:
                copy = pltpu.make_async_copy(
                    bufs[layer][matrix], wouts[matrix].at[layer], wout_sem.at[4 * layer + matrix]
                )
                copy.start()
                wcopies.append(copy)

    def vcopy(kind):
        owner, dev = (
            (f, here.to_x), (f, here.to_y), (f, here.to_c),
            (fx, here.to_y), (fx, here.to_c), (fy, here.to_c), (fd, here.to_c),
        )[kind]
        slot = len(pieces) * COPY_KINDS + kind
        return pltpu.make_async_remote_copy(
            src_ref=vslots.at[owner], dst_ref=vslots.at[owner], send_sem=send_sem.at[slot],
            recv_sem=recv_sem.at[slot], device_id=dev, device_id_type=MESH_ID,
        )

    cast_own(0)
    greeted(partners)
    vc = [vcopy(kind) for kind in range(VEC_KINDS)]
    started.extend(vc)
    for kind in (0, 1, 2):
        vc[kind].start()

    def prepare(step):
        if step == 0:
            vc[0].wait_recv()
            vc[1].wait_recv()
            for kind in (3, 4, 5):
                vc[kind].start()
        elif step == 1:
            vc[3].wait_recv()
            vc[6].start()
        else:
            for kind in (2, 4, 5, 6):
                vc[kind].wait_recv()
            lane = lax.broadcasted_iota(jnp.int32, (LANES, width), 0)
            column = lax.broadcasted_iota(jnp.int32, (LANES, width), 1)
            whole = jnp.zeros(vec.shape, F32)
            for owner in range(8):
                pick = (column == lane + owner * share) & (lane < share)
                whole = whole + jnp.dot(
                    vslots[owner], jnp.where(pick, 1.0, 0.0).astype(BF16),
                    preferred_element_type=F32,
                )
            vec[...] = whole

    saves = {}

    def save(layer, at, src, dst):
        copy = pltpu.make_async_copy(src, dst, save_sem.at[layer, at])
        copy.start()
        saves[layer, at] = copy

    def saved(layer, *ats):
        if layer >= 0:
            for at in ats:
                saves[layer, at].wait()

    def row(layer, at):
        return vec[16 * layer + at : 16 * layer + at + 1, :]

    def qkv(layer, part):
        low_ref, wq = (tok_ref if layer == 0 else hlow), bufs[layer][0]
        if part == 0:
            saved(layer - 1, 0)
        cols = slice(part * width, (part + 1) * width)

        def step(n, carry):
            rows = pl.ds(pl.multiple_of(n * half, half), half)
            acc = jnp.dot(low_ref[rows, :], wq[:, cols], preferred_element_type=F32)
            if part != 1:
                acc = acc + row(layer, part // 2)
            joined[rows, cols] = acc.astype(BF16)
            return carry

        lax.fori_loop(0, 2, step, 0)
        if part == 2:
            save(layer, 0, joined, joined_out.at[layer])

    def attend(layer, r):
        if r == 0:
            saved(layer - 1, 1)
        rows = slice(r * ROW, (r + 1) * ROW)
        first_head = lax.broadcasted_iota(jnp.int32, (ROW, LANES), 1) < HEAD_DIM
        seen = mask[r]
        seen = jnp.concatenate([seen, seen], axis=1) > 0.5
        group = 3
        for at in range(0, HEADS // 2, group):
            lanes = [
                [slice(p * width + j * LANES, p * width + (j + 1) * LANES) for p in range(3)]
                for j in range(at, at + group)
            ]
            query, keys, value = ([joined[rows, lane[p]] for lane in lanes] for p in range(3))
            both = [
                jnp.concatenate(
                    [jnp.where(first_head, q, jnp.zeros_like(q)), jnp.where(first_head, jnp.zeros_like(q), q)],
                    axis=0,
                )
                for q in query
            ]
            scores = [
                lax.dot_general(k, q, (((1,), (1,)), ((), ())), preferred_element_type=F32)
                for k, q in zip(keys, both)
            ]
            scores = [jnp.where(seen, s * HEAD_DIM ** (-0.5), NEGATIVE) for s in scores]
            grown = [jnp.exp(s - jnp.max(s, axis=0, keepdims=True)) for s in scores]
            probs = [
                (e * (1.0 / jnp.sum(e, axis=0, keepdims=True))).astype(BF16) for e in grown
            ]
            mixed = [
                lax.dot_general(p, v, (((0,), (0,)), ((), ())), preferred_element_type=F32)
                for p, v in zip(probs, value)
            ]
            for m, lane in zip(mixed, lanes):
                att[rows, lane[0]] = jnp.where(first_head, m[:ROW], m[ROW:]).astype(BF16)
        if r == rows_here - 1:
            save(layer, 1, att, att_out.at[layer])

    norm_tile = 64

    def out_half(layer, h):
        wo = bufs[layer][1]
        if h == 0:
            saved(layer - 1, 2, 3, 4)
        top = slice(h * half, (h + 1) * half)
        first[top, :] = jnp.dot(att[top, :], wo[...], preferred_element_type=F32)

        def step(n):
            rows = slice(h * half + n * norm_tile, h * half + (n + 1) * norm_tile)
            before = tok_ref[rows, :].astype(F32) if layer == 0 else hid[rows, :]
            normed, scaled, inverse = norm_rows(
                before + first[rows, :] + row(layer, 2), row(layer, 3), row(layer, 4)
            )
            first[rows, :] = normed
            flow[rows, :] = normed.astype(BF16)
            xh1[rows, :] = scaled
            r1[rows, :] = jnp.broadcast_to(inverse, (norm_tile, LANES))

        for n in range(half // norm_tile):
            step(n)
        if h == 1:
            save(layer, 2, xh1, xh1_out.at[layer])
            save(layer, 3, r1, r1_out.at[layer])
            save(layer, 4, flow, flow_out.at[layer])

    def in_part(layer, part):
        wi = bufs[layer][2]
        if part == 0:
            saved(layer - 1, 5, 6)
        bias_row = row(layer, 5 + part)
        tile = 256
        for sub in range(width // tile):
            bias = bias_row[:, sub * tile : (sub + 1) * tile]
            cols = slice(part * width + sub * tile, part * width + (sub + 1) * tile)

            def step(n, carry, cols=cols, bias=bias):
                rows = pl.ds(pl.multiple_of(n * half, half), half)
                inner = jnp.dot(flow[rows, :], wi[:, cols], preferred_element_type=F32) + bias
                value, change = gelu_pair(inner)
                active[rows, cols] = value.astype(BF16)
                slope[rows, cols] = change.astype(BF16)
                return carry

            lax.fori_loop(0, 2, step, 0)
        if part == 3:
            save(layer, 5, active, active_out.at[layer])
            save(layer, 6, slope, slope_out.at[layer])

    def back_half(layer, h):
        wb = bufs[layer][3]
        if h == 0:
            saved(layer - 1, 7, 8)
        top = slice(h * half, (h + 1) * half)
        first[top, :] = first[top, :] + jnp.dot(
            active[top, :], wb[...], preferred_element_type=F32
        )

        def step(n):
            rows = slice(h * half + n * norm_tile, h * half + (n + 1) * norm_tile)
            normed, scaled, inverse = norm_rows(
                first[rows, :] + row(layer, 9), row(layer, 10), row(layer, 11)
            )
            xh2[rows, :] = scaled
            r2[rows, :] = jnp.broadcast_to(inverse, (norm_tile, LANES))
            if layer == LAYERS - 1:
                act_out[rows, :] = normed.astype(BF16)
            else:
                hid[rows, :] = normed
                hlow[rows, :] = normed.astype(BF16)

        for n in range(half // norm_tile):
            step(n)
        if h == 1:
            save(layer, 7, xh2, xh2_out.at[layer])
            save(layer, 8, r2, r2_out.at[layer])
            if layer == 0:
                save(layer, 9, hlow, hlow_out)

    compute = {"qkv": qkv, "att": attend, "out": out_half, "in": in_part, "back": back_half}
    for what, *at in ORDER:
        if what in compute:
            compute[what](*at)
        elif what == "pre":
            prepare(*at)
        else:
            comm(what, *at)
    vec_save = pltpu.make_async_copy(vec, vec_out, save_sem.at[1, 9])
    vec_save.start()
    for copy in started:
        copy.wait_send()
    for copy in wcopies:
        copy.wait()
    saved(0, 9)
    saved(1, *range(9))
    vec_save.wait()


def forward(tokens, segment_ids, vectors, *masters):
    count, width = tokens.shape
    ff = masters[2].shape[2]
    copies = len(gather_pieces([m.shape[1:] for m in masters])) * COPY_KINDS + VEC_KINDS
    any_spec = pl.BlockSpec(memory_space=pltpu.HBM)
    vmem = pl.BlockSpec(memory_space=pltpu.VMEM)

    def shape(dims, kind):
        return jax.ShapeDtypeStruct(dims, kind)

    out_shape = (
        shape((count, width), BF16),
        shape((LAYERS, width, 3 * width), BF16),
        shape((LAYERS, width, width), BF16),
        shape((LAYERS, width, ff), BF16),
        shape((LAYERS, ff, width), BF16),
        shape((16 * LAYERS, width), F32),
        shape((LAYERS, count, 3 * width), BF16),
        shape((LAYERS, count, width), BF16),
        shape((LAYERS, count, width), F32),
        shape((LAYERS, count, LANES), F32),
        shape((LAYERS, count, width), BF16),
        shape((LAYERS, count, ff), BF16),
        shape((LAYERS, count, ff), BF16),
        shape((LAYERS, count, width), F32),
        shape((LAYERS, count, LANES), F32),
        shape((count, width), BF16),
    )
    weights = [
        pltpu.VMEM((width, 3 * width), BF16), pltpu.VMEM((width, width), BF16),
        pltpu.VMEM((width, ff), BF16), pltpu.VMEM((ff, width), BF16),
    ]
    scratch = weights * LAYERS + [pltpu.VMEM(m.shape, F32) for m in masters] + [
        pltpu.VMEM((8, 16 * LAYERS, LANES), BF16),
        pltpu.VMEM((16 * LAYERS, width), F32),
        pltpu.VMEM((count, width), F32),
        pltpu.VMEM((count, width), BF16),
        pltpu.VMEM((count, 3 * width), BF16),
        pltpu.VMEM((count, width), BF16),
        pltpu.VMEM((count, width), F32),
        pltpu.VMEM((count, width), F32),
        pltpu.VMEM((count, LANES), F32),
        pltpu.VMEM((count, width), BF16),
        pltpu.VMEM((count, ff), BF16),
        pltpu.VMEM((count, ff), BF16),
        pltpu.VMEM((count, width), F32),
        pltpu.VMEM((count, LANES), F32),
        pltpu.VMEM((segment_ids.shape[0], ROW, ROW), F32),
        pltpu.SemaphoreType.DMA((copies,)),
        pltpu.SemaphoreType.DMA((copies,)),
        pltpu.SemaphoreType.DMA((8,)),
        pltpu.SemaphoreType.DMA((8,)),
        pltpu.SemaphoreType.DMA((LAYERS, 10)),
    ]
    return pl.pallas_call(
        forward_kernel,
        name="forward",
        out_shape=out_shape,
        in_specs=[vmem, vmem, vmem] + [any_spec] * 4,
        out_specs=[vmem] + [any_spec] * (len(out_shape) - 1),
        scratch_shapes=scratch,
        compiler_params=pltpu.CompilerParams(
            collective_id=0, has_side_effects=True, vmem_limit_bytes=62 << 20
        ),
    )(tokens, segment_ids, vectors, *masters)


DEPTH = 6
Z_DEPTH = 12
CHUNKS = 12
TAIL = {21: (512, 256), 22: (256, 256, 256), 23: (256, 256, 256)}
BACK_ORDER = (
    ("t0", 1), ("t1", 1, 0), ("t1", 1, 1), (0, 0), (0, 1), (0, 2), (0, 3), ("t2", 1, 0), ("t2", 1, 1),
    (1, 0), (1, 1), ("t2", 1, 2), (1, 2), (1, 3), ("t2", 1, 3), ("t3", 1, 0), (0, 4), ("t3", 1, 1),
    (2, 0), (0, 5), ("t3", 1, 2), ("t3", 1, 3), (1, 4), (0, 6), (0, 7), ("t4", 1, 0), (2, 1), (1, 5),
    ("t4", 1, 1), (2, 2), ("t5", 1), (0, 8), ("t6", 1), (2, 3), ("t7", 1, 0), (3, 0), ("t7", 1, 1),
    ("t7", 1, 2), ("t7", 1, 3), (2, 4), (1, 6), (3, 1), ("t8", 1, 0), (0, 9), (4, 0), ("t8", 1, 1),
    (0, 10), ("t8", 1, 2), ("t9", 1, 0), (2, 5), (1, 7), (3, 2), ("t9", 1, 1), (4, 1), ("t0", 0),
    (3, 3), (5, 0), (3, 4), (4, 2), (2, 6), (1, 8), (1, 9), (3, 5), (1, 10), (0, 11), (4, 3), (5, 1),
    ("t1", 0, 0), (2, 7), (1, 11), (4, 4), (5, 2), (3, 6), ("t1", 0, 1), (0, 12), (0, 13), (0, 14),
    (0, 15), (4, 5), (5, 3), ("t2", 0, 0), (2, 8), (1, 12), (5, 4), ("t2", 0, 1), (2, 9), (4, 6),
    ("t2", 0, 2), (5, 5), ("t2", 0, 3), (2, 10), ("t3", 0, 0), (3, 7), (0, 16), ("t3", 0, 1), (0, 17),
    ("t3", 0, 2), (5, 6), (2, 11), (1, 13), (3, 8), (4, 7), ("t3", 0, 3), ("t4", 0, 0), ("t4", 0, 1),
    (2, 12), (3, 9), (1, 14), (3, 10), (4, 8), (5, 7), ("t5", 0), (3, 11), ("t6", 0), ("t7", 0, 0),
    ("t7", 0, 1), (2, 13), (1, 15), (3, 12), (1, 16), (1, 17), (0, 18), (4, 9), (4, 10), (5, 8),
    ("t7", 0, 2), (2, 14), (1, 18), (0, 19), (3, 13), (0, 20), (4, 11), ("t7", 0, 3), ("v", 0), (5, 9),
    ("t8", 0, 0), (2, 15), (1, 19), (0, 21), (0, 22), (4, 12), ("v", 1), ("t8", 0, 1), (0, 23),
    (0, 24), (5, 10), ("t8", 0, 2), (2, 16), (4, 13), ("t9", 0, 0), ("t9", 0, 1), (5, 11), (2, 17),
    (3, 14), (5, 12), (2, 18), (1, 20), (5, 13), (3, 15), (4, 14), (2, 19), (1, 21), (0, 25), ("v", 2),
    (3, 16), (4, 15), (5, 14), (3, 17), (3, 18), (4, 16), (5, 15), (2, 20), (1, 22), (1, 23), (1, 24),
    (3, 19), (4, 17), ("v", 3), (2, 21), (1, 25), (0, 26), (0, 27), (5, 16), (3, 20), (4, 18), (2, 22),
    (1, 26), (0, 28), (2, 23), (5, 17), (2, 24), (4, 19), ("v", 4), (3, 21), (2, 25), (1, 27), (5, 18),
    (3, 22), (4, 20), (2, 26), (1, 28), (3, 23), (3, 24), (4, 21), (5, 19), (3, 25), ("v", 5), (2, 27),
    (4, 22), (4, 23), (5, 20), (3, 26), (2, 28), (4, 24), (5, 21), (3, 27), (5, 22), (3, 28), (4, 25),
    (5, 23), (5, 24), (4, 26), (5, 25), (4, 27), (4, 28), (5, 26), (5, 27), (5, 28),
)


def reduce_items(width):
    items = []
    for chunk in range(LAYERS * CHUNKS):
        at = 0
        for cols in TAIL.get(chunk, (width,)):
            items.append((chunk, at, cols))
            at += cols
    return items


def backward_kernel(
    cot_ref, seg_ref, vec_ref, tok_in, hlow_in, wq_in, wo_in, wi_in, wb_in,
    joined_in, att_in, xh1_in, r1_in, flow_in, active_in, slope_in, xh2_in, r2_in,
    grad_ref, total_ref, vtotal_ref,
    wq, wo, wi, wb, joined, att, xh1, r1, flow, active, slope, xh2, r2, hin,
    ring, got_d, got_a, got_b, got_z1, got_z2, part_sum, gtwo, glow, dvec, dbin, mask,
    vsend, vgot_d, vgot_a, vgot_b, vgot_z1, vgot_z2,
    load_sem, d_send, d_recv, a_send, a_recv, b_send, b_recv, z_send, z_recv, v_send, v_recv,
):
    here = Place()
    tokens, width = gtwo.shape
    ff = active.shape[1]
    rows_per = ring.shape[4]
    core, x, y = here.core, here.x, here.y
    other_core, other_x, other_y = 1 - core, 1 - x, 1 - y
    to_mid = {"dp": 3 - here.z}
    inner = lax.rem(here.z + 1, 4) >= 2
    outer = jnp.logical_not(inner)
    partners = (here.to_c, here.to_x, here.to_y, here.to_z, to_mid)
    greet(partners)

    sources = {
        "xh2": (xh2_in, xh2), "r2": (r2_in, r2), "active": (active_in, active), "wb": (wb_in, wb),
        "slope": (slope_in, slope), "flow": (flow_in, flow), "wi": (wi_in, wi),
        "xh1": (xh1_in, xh1), "r1": (r1_in, r1), "att": (att_in, att), "wo": (wo_in, wo),
        "joined": (joined_in, joined), "hin": (None, hin), "wq": (wq_in, wq),
    }
    order = list(sources)

    def load(layer, name):
        src, dst = sources[name]
        if name == "hin":
            src = tok_in if layer == 0 else hlow_in
        else:
            src = src.at[layer]
        return pltpu.make_async_copy(src, dst, load_sem.at[order.index(name)])

    early = 3
    for name in order[:early]:
        load(LAYERS - 1, name).start()

    def need(layer, *names):
        for name in names:
            load(layer, name).wait()

    def release(layer, *names):
        if layer > 0:
            for name in names:
                load(layer - 1, name).start()

    rows_here = seg_ref.shape[0]
    for r in range(rows_here):
        wide = jnp.broadcast_to(seg_ref[r : r + 1, :].astype(F32), (ROW, ROW))
        mask[r] = jnp.where(wide == wide.T, 1.0, 0.0)
    dvec[...] = jnp.zeros_like(dvec)

    def remote(src, dst, send, recv, device):
        return pltpu.make_async_remote_copy(
            src_ref=src, dst_ref=dst, send_sem=send, recv_sem=recv, device_id=device,
            device_id_type=MESH_ID,
        )

    items = reduce_items(width)

    def place(n):
        chunk, at, cols = items[n]
        return n % DEPTH, chunk % CHUNKS, cols // 2, slice(at, at + cols // 2), slice(at + cols // 2, at + cols)

    def copy_d(n):
        _, at, cols = items[n]
        b, s = place(n)[:2]
        src = ring.at[s, other_core, :, :, :, at : at + cols]
        return remote(src, got_d.at[b, :, :, :, :cols], d_send.at[b], d_recv.at[b], here.to_c)

    def copy_a(n, side):
        b, s, part, low, high = place(n)
        if side == 0:
            src, dev = ring.at[s, core, :, other_x, :, low], here.to_x
        else:
            src, dev = ring.at[s, core, other_y, :, :, high], here.to_y
        dst = got_a.at[b, side, :, :, :part]
        return remote(src, dst, a_send.at[b, side], a_recv.at[b, side], dev)

    def copy_b(n, side):
        b, s, part, low, high = place(n)
        if side == 0:
            src, dev = ring.at[s, core, other_y, x, :, low], here.to_y
        else:
            src, dev = ring.at[s, core, y, other_x, :, high], here.to_x
        dst = got_b.at[b, side, :, :part]
        return remote(src, dst, b_send.at[b, side], b_recv.at[b, side], dev)

    def copy_z(n, hop):
        chunk, at, cols = items[n]
        b, far = n % DEPTH, n % Z_DEPTH
        if hop == 0:
            src, dst, dev, sem = part_sum.at[b, :, :cols], got_z1.at[far, :, :cols], here.to_z, far
        elif hop == 1:
            src, dst, dev, sem = part_sum.at[b, :, :cols], got_z2.at[b, :, :cols], to_mid, Z_DEPTH + b
        else:
            src = total_ref.at[chunk, :, at : at + cols]
            dst, dev, sem = src, here.to_z, Z_DEPTH + DEPTH + n
        return remote(src, dst, z_send.at[sem], z_recv.at[sem], dev)

    def added(a, b):
        return (a.astype(F32) + b.astype(F32)).astype(BF16)

    def stage0(n):
        copy_d(n).start()

    def stage1(n):
        _, at, cols = items[n]
        b, s = place(n)[:2]
        cols_here = slice(at, at + cols)
        copy_d(n).wait_recv()

        def add_shard(i, carry):
            iy, ix = lax.div(i, 2), lax.rem(i, 2)
            ring[s, core, iy, ix, :, cols_here] = added(
                ring[s, core, iy, ix, :, cols_here], got_d[b, iy, ix, :, :cols]
            )
            return carry

        lax.fori_loop(0, 4, add_shard, 0)
        copy_a(n, 0).start()
        copy_a(n, 1).start()
        copy_d(n).wait_send()

    def stage2(n):
        b, s, part, low, high = place(n)
        copy_a(n, 0).wait_recv()
        for i in range(2):
            ring[s, core, i, x, :, low] = added(ring[s, core, i, x, :, low], got_a[b, 0, i, :, :part])
        copy_b(n, 0).start()
        copy_a(n, 1).wait_recv()
        for i in range(2):
            ring[s, core, y, i, :, high] = added(ring[s, core, y, i, :, high], got_a[b, 1, i, :, :part])
        copy_b(n, 1).start()
        copy_a(n, 0).wait_send()
        copy_a(n, 1).wait_send()

    def stage3(n):
        b, s, part, low, high = place(n)
        if n >= Z_DEPTH:
            @pl.when(outer)
            def _():
                copy_z(n - Z_DEPTH, 2).wait_recv()

        copy_b(n, 0).wait_recv()
        part_sum[b, :, :part] = added(ring[s, core, y, x, :, low], got_b[b, 0, :, :part])
        copy_b(n, 1).wait_recv()
        part_sum[b, :, part : 2 * part] = added(ring[s, core, y, x, :, high], got_b[b, 1, :, :part])

        @pl.when(outer)
        def _():
            copy_z(n, 0).start()

        copy_b(n, 0).wait_send()
        copy_b(n, 1).wait_send()

    def stage4(n):
        b, cols = n % DEPTH, items[n][2]

        @pl.when(outer)
        def _():
            copy_z(n, 0).wait_send()

        @pl.when(inner)
        def _():
            copy_z(n, 0).wait_recv()
            part_sum[b, :, :cols] = added(part_sum[b, :, :cols], got_z1[n % Z_DEPTH, :, :cols])
            copy_z(n, 1).start()

    def stage5(n):
        chunk, at, cols = items[n]
        b = n % DEPTH

        @pl.when(inner)
        def _():
            copy_z(n, 1).wait_recv()
            copy_z(n, 1).wait_send()
            total_ref[chunk, :, at : at + cols] = added(part_sum[b, :, :cols], got_z2[b, :, :cols])
            copy_z(n, 2).start()

    stages = (stage0, stage1, stage2, stage3, stage4, stage5)

    def vcopy(at):
        src, dst, dev = (
            (vsend.at[other_core], vgot_d, here.to_c),
            (vsend.at[core, :, other_x], vgot_a, here.to_x),
            (vsend.at[core, other_y, x], vgot_b, here.to_y),
            (vsend.at[core, y, x], vgot_z1, here.to_z),
            (vsend.at[core, y, x], vgot_z2, to_mid),
            (vtotal_ref, vtotal_ref, here.to_z),
        )[at]
        return remote(src, dst, v_send.at[at], v_recv.at[at], dev)

    def vstage(at):
        if at == 0:
            share = width // 8
            lane = lax.broadcasted_iota(jnp.int32, (width, LANES), 1)
            column = lax.broadcasted_iota(jnp.int32, (width, LANES), 0)
            low = dvec[...].astype(BF16)
            for owner in range(8):
                pick = (column == lane + owner * share) & (lane < share)
                vsend[owner % 2, owner // 4, (owner // 2) % 2] = jnp.dot(
                    low, jnp.where(pick, 1.0, 0.0).astype(BF16), preferred_element_type=F32
                ).astype(BF16)
            vcopy(0).start()
        elif at == 1:
            vcopy(0).wait_recv()
            for i in range(4):
                vsend[core, i // 2, i % 2] = added(vsend[core, i // 2, i % 2], vgot_d[i // 2, i % 2])
            vcopy(1).start()
        elif at == 2:
            vcopy(1).wait_recv()
            for i in range(2):
                vsend[core, i, x] = added(vsend[core, i, x], vgot_a[i])
            vcopy(2).start()
        elif at == 3:
            vcopy(2).wait_recv()
            vsend[core, y, x] = added(vsend[core, y, x], vgot_b[...])

            @pl.when(outer)
            def _():
                vcopy(3).start()
        elif at == 4:
            @pl.when(inner)
            def _():
                vcopy(3).wait_recv()
                vsend[core, y, x] = added(vsend[core, y, x], vgot_z1[...])
                vcopy(4).start()
        elif at == 5:
            @pl.when(inner)
            def _():
                vcopy(4).wait_recv()
                vcopy(4).wait_send()
                vtotal_ref[...] = added(vsend[core, y, x], vgot_z2[...])
                vcopy(5).start()
                vcopy(5).wait_send()

            @pl.when(outer)
            def _():
                vcopy(3).wait_send()
                vcopy(5).wait_recv()

            for early in range(3):
                vcopy(early).wait_send()

    tile = 64
    half = tokens // 2

    def norm_back(layer, first_row, grad_in, scaled, inverse, grad_out, bias_row):
        base = 16 * layer
        gain = vec_ref[base + first_row : base + first_row + 1, :]

        def step(n, carry):
            rows = pl.ds(pl.multiple_of(n * tile, tile), tile)
            grad = grad_in[rows, :]
            hat = scaled[rows, :]
            lifted = grad * gain
            left = jnp.mean(lifted, axis=-1, keepdims=True)
            right = jnp.mean(lifted * hat, axis=-1, keepdims=True)
            result = inverse[rows, :1] * (lifted - left - hat * right)
            grad_out[rows, :] = result
            glow[rows, :] = result.astype(BF16)
            return (
                carry[0] + jnp.sum(grad * hat, axis=0, keepdims=True),
                carry[1] + jnp.sum(grad, axis=0, keepdims=True),
                carry[2] + jnp.sum(result, axis=0, keepdims=True),
            )

        nil = jnp.zeros((1, width), F32)
        sums = lax.fori_loop(0, tokens // tile, step, (nil, nil, nil))
        dvec[base + first_row : base + first_row + 1, :] = sums[0]
        dvec[base + first_row + 1 : base + first_row + 2, :] = sums[1]
        dvec[base + bias_row : base + bias_row + 1, :] = sums[2]

    def tn(left, right):
        return lax.dot_general(left, right, (((0,), (0,)), ((), ())), preferred_element_type=F32)

    def nt(left, right):
        return lax.dot_general(left, right, (((1,), (1,)), ((), ())), preferred_element_type=F32)

    def task0(layer):
        need(layer, "xh2", "r2")
        if layer == LAYERS - 1:
            for name in order[early:]:
                load(layer, name).start()
            grad_ref[...] = cot_ref[...].astype(F32)
        norm_back(layer, 10, grad_ref, xh2, r2, gtwo, 9)
        release(layer, "xh2", "r2")

    def task1(layer, at):
        if at == 0:
            need(layer, "active")
        rows_f = ff // 8

        def step(owner, carry):
            part = tn(active[:, pl.ds(pl.multiple_of(owner * rows_f, LANES), rows_f)], glow[...])
            oc, ox, oy = lax.rem(owner, 2), lax.rem(lax.div(owner, 2), 2), lax.div(owner, 4)
            for j in range(rows_f // rows_per):
                ring[j, oc, oy, ox] = part[j * rows_per : (j + 1) * rows_per].astype(BF16)
            return carry

        lax.fori_loop(4 * at, 4 * at + 4, step, 0)
        if at == 1:
            release(layer, "active")

    def task2(layer, at, of=4):
        if at == 0:
            need(layer, "wb", "slope")
        cols_at = 256
        count = ff // cols_at // of

        def step(n, carry):
            cols = pl.ds(pl.multiple_of(n * cols_at, cols_at), cols_at)
            sums = jnp.zeros((1, cols_at), F32)
            for h in range(2):
                rows = slice(h * half, (h + 1) * half)
                inner_grad = (nt(glow[rows, :], wb[cols, :]) * slope[rows, cols].astype(F32)).astype(BF16)
                slope[rows, cols] = inner_grad
                sums = sums + jnp.sum(inner_grad.astype(F32), axis=0, keepdims=True)
            dbin[:, cols] = sums
            return carry

        lax.fori_loop(at * count, (at + 1) * count, step, 0)
        if at == of - 1:
            release(layer, "wb")
            for j in range(ff // width):
                dvec[16 * layer + 5 + j : 16 * layer + 6 + j, :] = dbin[:, j * width : (j + 1) * width]

    def weight_chunk(at, left, right):
        quarter = width // 2

        for iy in range(2):
            part = tn(left[:, iy * quarter : (iy + 1) * quarter], right)
            for i in range(4):
                ring[at, i % 2, iy, i // 2] = part[i * rows_per : (i + 1) * rows_per].astype(BF16)

    def task3(layer, j):
        if j == 0:
            need(layer, "flow")
        weight_chunk(4 + j, flow, slope[:, j * width : (j + 1) * width])
        if j == 3:
            release(layer, "flow")

    def add_product(target, base, left, right, h):
        rows = slice(h * half, (h + 1) * half)
        block = 256

        for j in range(width // block):
            cols = slice(j * block, (j + 1) * block)
            product = nt(left[rows, :], right[cols, :])
            if base is not None:
                product = base[rows, cols] + product
            target[rows, cols] = product.astype(target.dtype)

    def task4(layer, h):
        if h == 0:
            need(layer, "wi", "xh1", "r1")
        add_product(gtwo, gtwo, slope, wi, h)
        if h == 1:
            norm_back(layer, 3, gtwo, xh1, r1, gtwo, 2)
            release(layer, "slope", "wi", "xh1", "r1")

    def task5(layer):
        need(layer, "att")
        weight_chunk(8, att, glow[...])

    def task6(layer):
        need(layer, "wo")
        for h in range(2):
            add_product(att, None, glow, wo, h)
        release(layer, "wo")

    def task7(layer, r):
        if r == 0:
            need(layer, "joined")
        base = 16 * layer
        rows = slice(r * ROW, (r + 1) * ROW)
        first_head = lax.broadcasted_iota(jnp.int32, (ROW, LANES), 1) < HEAD_DIM
        seen = mask[r]
        seen = jnp.concatenate([seen, seen], axis=1) > 0.5

        def stacked(value):
            nil = jnp.zeros_like(value)
            return jnp.concatenate(
                [jnp.where(first_head, value, nil), jnp.where(first_head, nil, value)], axis=0
            )

        group = 3
        for first in range(0, HEADS // 2, group):
            lanes = [
                [slice(p * width + j * LANES, p * width + (j + 1) * LANES) for p in range(3)]
                for j in range(first, first + group)
            ]
            query, keys, value = ([joined[rows, lane[p]] for lane in lanes] for p in range(3))
            out_grad = [stacked(att[rows, lane[0]]) for lane in lanes]
            both = [stacked(q) for q in query]
            scores = [
                jnp.where(seen, nt(k, q) * HEAD_DIM ** (-0.5), NEGATIVE) for k, q in zip(keys, both)
            ]
            grad_probs = [nt(v, g) for v, g in zip(value, out_grad)]
            grown = [jnp.exp(s - jnp.max(s, axis=0, keepdims=True)) for s in scores]
            probs = [e * (1.0 / jnp.sum(e, axis=0, keepdims=True)) for e in grown]
            grad_value = [
                jnp.dot(p.astype(BF16), g, preferred_element_type=F32).astype(BF16)
                for p, g in zip(probs, out_grad)
            ]
            centre = [jnp.sum(p * g, axis=0, keepdims=True) for p, g in zip(probs, grad_probs)]
            grad_scores = [(p * (g - c)).astype(BF16) for p, g, c in zip(probs, grad_probs, centre)]
            wide = [tn(g, k) for g, k in zip(grad_scores, keys)]
            grad_key = [
                jnp.dot(g, q, preferred_element_type=F32) * HEAD_DIM ** (-0.5)
                for g, q in zip(grad_scores, both)
            ]
            grad_query = [
                (jnp.where(first_head, w[:ROW], w[ROW:]) * HEAD_DIM ** (-0.5)).astype(BF16) for w in wide
            ]
            for at, lane in enumerate(lanes):
                joined[rows, lane[0]] = grad_query[at]
                joined[rows, lane[1]] = grad_key[at].astype(BF16)
                joined[rows, lane[2]] = grad_value[at]
                dvec[base : base + 1, lane[0]] += jnp.sum(
                    grad_query[at].astype(F32), axis=0, keepdims=True
                )
                dvec[base + 1 : base + 2, lane[0]] += jnp.sum(
                    grad_value[at].astype(F32), axis=0, keepdims=True
                )
        if r == rows_here - 1:
            release(layer, "att")

    def task8(layer, j):
        if j == 0:
            need(layer, "hin")
        weight_chunk(9 + j, hin, joined[:, j * width : (j + 1) * width])
        if j == 2:
            release(layer, "hin")

    def task9(layer, h):
        if h == 0:
            need(layer, "wq")
        add_product(grad_ref, gtwo, joined, wq, h)
        if h == 1:
            release(layer, "joined", "wq")

    tasks = {
        "t0": task0, "t1": task1, "t2": task2, "t3": task3, "t4": task4,
        "t5": task5, "t6": task6, "t7": task7, "t8": task8, "t9": task9,
    }
    first_step = [what in tasks for what, *_ in BACK_ORDER].index(False)
    for when, (what, *at) in enumerate(BACK_ORDER):
        if when == first_step:
            greeted(partners)
        if what == "v":
            vstage(*at)
        elif what in tasks:
            tasks[what](*at)
        else:
            stages[what](*at)

    @pl.when(inner)
    def _():
        for n in range(len(items)):
            copy_z(n, 2).wait_send()

    @pl.when(outer)
    def _():
        for n in range(len(items) - Z_DEPTH, len(items)):
            copy_z(n, 2).wait_recv()


def backward(cotangent, segment_ids, vec, tokens, hlow, weights, kept):
    count, width = tokens.shape
    ff = weights[2].shape[2]
    rows_per = width // 8
    hbm = pl.BlockSpec(memory_space=pltpu.HBM)
    vmem = pl.BlockSpec(memory_space=pltpu.VMEM)
    small = vec.shape[0]
    out_shape = (
        jax.ShapeDtypeStruct((count, width), F32),
        jax.ShapeDtypeStruct((LAYERS * CHUNKS, rows_per, width), BF16),
        jax.ShapeDtypeStruct((small, LANES), BF16),
    )
    dma = pltpu.SemaphoreType.DMA
    z_sems = Z_DEPTH + DEPTH + len(reduce_items(width))
    scratch = [
        pltpu.VMEM((width, 3 * width), BF16), pltpu.VMEM((width, width), BF16),
        pltpu.VMEM((width, ff), BF16), pltpu.VMEM((ff, width), BF16),
        pltpu.VMEM((count, 3 * width), BF16), pltpu.VMEM((count, width), BF16),
        pltpu.VMEM((count, width), F32), pltpu.VMEM((count, LANES), F32),
        pltpu.VMEM((count, width), BF16), pltpu.VMEM((count, ff), BF16), pltpu.VMEM((count, ff), BF16),
        pltpu.VMEM((count, width), F32), pltpu.VMEM((count, LANES), F32),
        pltpu.VMEM((count, width), BF16),
        pltpu.VMEM((CHUNKS, 2, 2, 2, rows_per, width), BF16),
        pltpu.VMEM((DEPTH, 2, 2, rows_per, width), BF16),
        pltpu.VMEM((DEPTH, 2, 2, rows_per, width // 2), BF16),
        pltpu.VMEM((DEPTH, 2, rows_per, width // 2), BF16),
        pltpu.VMEM((Z_DEPTH, rows_per, width), BF16),
        pltpu.VMEM((DEPTH, rows_per, width), BF16),
        pltpu.VMEM((DEPTH, rows_per, width), BF16),
        pltpu.VMEM((count, width), F32), pltpu.VMEM((count, width), BF16),
        pltpu.VMEM((small, width), F32), pltpu.VMEM((1, ff), F32),
        pltpu.VMEM((segment_ids.shape[0], ROW, ROW), F32),
        pltpu.VMEM((2, 2, 2, small, LANES), BF16), pltpu.VMEM((2, 2, small, LANES), BF16),
        pltpu.VMEM((2, small, LANES), BF16), pltpu.VMEM((small, LANES), BF16),
        pltpu.VMEM((small, LANES), BF16), pltpu.VMEM((small, LANES), BF16),
        dma((14,)), dma((DEPTH,)), dma((DEPTH,)), dma((DEPTH, 2)), dma((DEPTH, 2)),
        dma((DEPTH, 2)), dma((DEPTH, 2)), dma((z_sems,)), dma((z_sems,)), dma((6,)), dma((6,)),
    ]
    return pl.pallas_call(
        backward_kernel,
        name="backward",
        out_shape=out_shape,
        in_specs=[vmem, vmem, vmem] + [hbm] * 15,
        out_specs=[vmem, vmem, vmem],
        scratch_shapes=scratch,
        compiler_params=pltpu.CompilerParams(
            collective_id=1, has_side_effects=True, vmem_limit_bytes=62 << 20
        ),
    )(cotangent, segment_ids, vec, tokens, hlow, *weights, *kept)


SLOTS = 4


def adam_rule(weight, gradient, moment_one, moment_two, step_rate):
    first_moment = BETA_FIRST * moment_one + (1.0 - BETA_FIRST) * gradient
    second_moment = BETA_SECOND * moment_two + (1.0 - BETA_SECOND) * gradient * gradient
    first_hat = first_moment / (1.0 - BETA_FIRST**STEP)
    second_hat = second_moment / (1.0 - BETA_SECOND**STEP)
    updated = weight - step_rate * (
        first_hat / (jnp.sqrt(second_hat) + ADAM_EPSILON) + WEIGHT_DECAY * weight
    )
    return updated, second_moment


def adam_kernel(
    total_ref, vtotal_ref, vectors_ref, vector_moments_ref, act_in, grad_in,
    q_w, o_w, i_w, b_w, q_m, o_m, i_m, b_m,
    act_out, grad_out, q_g, o_g, i_g, b_g, q_n, o_n, i_n, b_n, q_s, o_s, i_s, b_s, v_g, v_n, v_s,
    held, summed, made, act_held, grad_held, in_sem, out_sem, pass_sem,
):
    rows, width = held.shape[2:]
    kinds = {
        "q": (q_w, q_m, (q_g, q_n, q_s)), "o": (o_w, o_m, (o_g, o_n, o_s)),
        "i": (i_w, i_m, (i_g, i_n, i_s)), "b": (b_w, b_m, (b_g, b_n, b_s)),
    }
    chunks = []
    for n in range(LAYERS * CHUNKS):
        layer, at = LAYERS - 1 - n // CHUNKS, n % CHUNKS
        if at < 4:
            place = ("b", layer, slice(at * rows, (at + 1) * rows), slice(0, width))
        elif at < 8:
            place = ("i", layer, slice(0, rows), slice((at - 4) * width, (at - 3) * width))
        elif at == 8:
            place = ("o", layer, slice(0, rows), slice(0, width))
        else:
            place = ("q", layer, slice(0, rows), slice((at - 9) * width, (at - 8) * width))
        chunks.append(place)

    def reads(n):
        kind, layer, r, c = chunks[n]
        weight, moments, _ = kinds[kind]
        b = n % SLOTS
        sources = (weight.at[layer, r, c], moments.at[0, layer, r, c], moments.at[1, layer, r, c])
        return [
            pltpu.make_async_copy(source, held.at[b, k], in_sem.at[b, k])
            for k, source in enumerate(sources)
        ] + [pltpu.make_async_copy(total_ref.at[n], summed.at[b], in_sem.at[b, 3])]

    def writes(n):
        kind, layer, r, c = chunks[n]
        b = n % SLOTS
        return [
            pltpu.make_async_copy(made.at[b, k], target.at[layer, r, c], out_sem.at[b, k])
            for k, target in enumerate(kinds[kind][2])
        ]

    for n in range(SLOTS - 1):
        for copy in reads(n):
            copy.start()
    passing = (
        pltpu.make_async_copy(act_in, act_held, pass_sem.at[0]),
        pltpu.make_async_copy(grad_in, grad_held, pass_sem.at[1]),
    )
    passed = (
        pltpu.make_async_copy(act_held, act_out, pass_sem.at[2]),
        pltpu.make_async_copy(grad_held, grad_out, pass_sem.at[3]),
    )
    for copy in passing:
        copy.start()
    share = vectors_ref.shape[2]
    for layer in range(LAYERS):
        gradient = vtotal_ref[16 * layer : 16 * layer + 12, :share].astype(F32)
        updated, second = adam_rule(
            vectors_ref[:, layer, :], gradient, vector_moments_ref[0, :, layer, :],
            vector_moments_ref[1, :, layer, :], RATE_VECTOR,
        )
        v_g[:, layer, :] = gradient
        v_n[:, layer, :] = updated
        v_s[:, layer, :] = second
    tile = 32
    for n in range(LAYERS * CHUNKS):
        b = n % SLOTS
        if n == SLOTS:
            for early, late in zip(passing, passed):
                early.wait()
                late.start()
        if n + SLOTS - 1 < LAYERS * CHUNKS:
            for copy in reads(n + SLOTS - 1):
                copy.start()
        for copy in reads(n):
            copy.wait()
        if n >= SLOTS:
            for copy in writes(n - SLOTS):
                copy.wait()

        def step(t, carry, n=n, b=b):
            r = pl.ds(pl.multiple_of(t * tile, tile), tile)
            gradient = summed[b, r, :].astype(F32)
            updated, second = adam_rule(
                held[b, 0, r, :], gradient, held[b, 1, r, :], held[b, 2, r, :], RATE_MATRIX
            )
            made[b, 0, r, :] = gradient
            made[b, 1, r, :] = updated
            made[b, 2, r, :] = second
            return carry

        lax.fori_loop(0, rows // tile, step, 0)
        for copy in writes(n):
            copy.start()
    for n in range(LAYERS * CHUNKS - SLOTS, LAYERS * CHUNKS):
        for copy in writes(n):
            copy.wait()
    for copy in passed:
        copy.wait()


def adam(activations, grad, total, vtotal, masters, moments):
    rows, width = total.shape[1:]
    hbm = pl.BlockSpec(memory_space=pltpu.HBM)
    vmem = pl.BlockSpec(memory_space=pltpu.VMEM)
    matrices, vectors = masters[:4], masters[4].transpose(1, 0, 2)
    passed = [jax.ShapeDtypeStruct(p.shape, p.dtype) for p in (activations, grad)]
    matrix_shapes = [jax.ShapeDtypeStruct(m.shape, F32) for m in matrices]
    vector_shape = jax.ShapeDtypeStruct(vectors.shape, F32)
    out = pl.pallas_call(
        adam_kernel,
        name="adam",
        out_shape=passed + matrix_shapes * 3 + [vector_shape] * 3,
        in_specs=[hbm] + [vmem] * 3 + [hbm] * 10,
        out_specs=[hbm] * 14 + [vmem] * 3,
        scratch_shapes=[
            pltpu.VMEM((SLOTS, 3, rows, width), F32), pltpu.VMEM((SLOTS, rows, width), BF16),
            pltpu.VMEM((SLOTS, 3, rows, width), F32),
            pltpu.VMEM(activations.shape, BF16), pltpu.VMEM(grad.shape, F32),
            pltpu.SemaphoreType.DMA((SLOTS, 4)), pltpu.SemaphoreType.DMA((SLOTS, 3)),
            pltpu.SemaphoreType.DMA((4,)),
        ],
        compiler_params=pltpu.CompilerParams(vmem_limit_bytes=62 << 20),
    )(
        total, vtotal, vectors, moments[4].transpose(0, 2, 1, 3), activations, grad, *matrices,
        *moments[:4],
    )
    gradients, updates, states = out[2:6], out[6:10], out[10:14]
    vector_outs = [v.transpose(1, 0, 2) for v in out[14:]]
    return (
        out[0], out[1], *gradients, vector_outs[0], *updates, vector_outs[1], *states, vector_outs[2]
    )


def norm_forward(values, gain_row, shift_row):
    centered = values - jnp.mean(values, axis=-1, keepdims=True)
    inverse = lax.rsqrt(jnp.mean(centered * centered, axis=-1, keepdims=True) + EPSILON)
    scaled = centered * inverse
    return (scaled * gain_row + shift_row, scaled, inverse)


def norm_backward(grad_out, scaled, inverse, gain_row):
    grad_scaled = grad_out * gain_row
    grad_in = inverse * (
        grad_scaled
        - jnp.mean(grad_scaled, axis=-1, keepdims=True)
        - scaled * jnp.mean(grad_scaled * scaled, axis=-1, keepdims=True)
    )
    return (grad_in, jnp.sum(grad_out * scaled, axis=0), jnp.sum(grad_out, axis=0))


def score_block(queries, key_rows, same_segment):
    scores = jnp.einsum(
        "rqhe,rkhe->rhqk", queries, key_rows, preferred_element_type=jnp.float32
    ) * HEAD_DIM ** (-0.5)
    return jnp.where(same_segment, scores, NEGATIVE)


def layer_forward(hidden, same_segment, weights):
    qkv_used, out_used, in_used, back_used, vector_low = weights
    vector = vector_low.astype(jnp.float32)
    row_count = same_segment.shape[0]
    model_width = out_used.shape[0]
    hidden_low = hidden.astype(jnp.bfloat16)
    bias_qkv = jnp.concatenate([vector[0], jnp.zeros_like(vector[0]), vector[1]])
    joined = (jnp.dot(hidden_low, qkv_used, preferred_element_type=jnp.float32) + bias_qkv).astype(
        jnp.bfloat16
    )
    split_qkv = joined.reshape(row_count, -1, 3, HEADS, HEAD_DIM)
    scores = score_block(split_qkv[:, :, 0], split_qkv[:, :, 1], same_segment)
    row_top = jnp.max(scores, axis=-1, keepdims=True)
    log_total = row_top + jnp.log(jnp.sum(jnp.exp(scores - row_top), axis=-1, keepdims=True))
    prob_low = jnp.exp(scores - log_total).astype(jnp.bfloat16)
    attended = jnp.einsum(
        "rhqk,rkhe->rqhe", prob_low, split_qkv[:, :, 2], preferred_element_type=jnp.float32
    )
    attended_low = attended.reshape(-1, model_width).astype(jnp.bfloat16)
    branch = jnp.dot(attended_low, out_used, preferred_element_type=jnp.float32) + vector[2]
    first_norm, scaled_one, inverse_one = norm_forward(hidden + branch, vector[3], vector[4])
    first_low = first_norm.astype(jnp.bfloat16)
    inner_pre = jnp.dot(first_low, in_used, preferred_element_type=jnp.float32) + vector[
        5:9
    ].reshape(-1)
    active_low = jax.nn.gelu(inner_pre, approximate=False).astype(jnp.bfloat16)
    outer_out = jnp.dot(active_low, back_used, preferred_element_type=jnp.float32) + vector[9]
    output, scaled_two, inverse_two = norm_forward(first_norm + outer_out, vector[10], vector[11])
    kept_state = (
        hidden_low,
        joined,
        log_total,
        attended_low,
        scaled_one,
        inverse_one,
        first_low,
        inner_pre,
        active_low,
        scaled_two,
        inverse_two,
    )
    return (output, kept_state)


def layer_backward(grad_out, same_segment, weights, kept_state):
    qkv_used, out_used, in_used, back_used, vector_low = weights
    vector = vector_low.astype(jnp.float32)
    (
        hidden_low,
        joined,
        log_total,
        attended_low,
        scaled_one,
        inverse_one,
        first_low,
        inner_pre,
        active_low,
        scaled_two,
        inverse_two,
    ) = kept_state
    row_count = same_segment.shape[0]
    model_width = out_used.shape[0]
    grad_two, gain_two_grad, shift_two_grad = norm_backward(
        grad_out, scaled_two, inverse_two, vector[10]
    )
    grad_outer = grad_two.astype(jnp.bfloat16)
    back_bias_grad = jnp.sum(grad_two, axis=0)
    back_weight_grad = jnp.einsum(
        "tf,td->fd", active_low, grad_outer, preferred_element_type=jnp.float32
    )
    grad_active = jnp.einsum("td,fd->tf", grad_outer, back_used, preferred_element_type=jnp.float32)
    gelu_value, gelu_pull = jax.vjp(
        lambda values: jax.nn.gelu(values, approximate=False), inner_pre
    )
    grad_inner = gelu_pull(grad_active)[0].astype(jnp.bfloat16)
    in_bias_grad = jnp.sum(grad_inner, axis=0, dtype=jnp.float32)
    in_weight_grad = jnp.einsum(
        "td,tf->df", first_low, grad_inner, preferred_element_type=jnp.float32
    )
    grad_first = grad_two + jnp.einsum(
        "tf,df->td", grad_inner, in_used, preferred_element_type=jnp.float32
    )
    grad_one, gain_one_grad, shift_one_grad = norm_backward(
        grad_first, scaled_one, inverse_one, vector[3]
    )
    grad_branch = grad_one.astype(jnp.bfloat16)
    out_bias_grad = jnp.sum(grad_one, axis=0)
    out_weight_grad = jnp.einsum(
        "td,te->de", attended_low, grad_branch, preferred_element_type=jnp.float32
    )
    grad_mixed = jnp.einsum("te,de->td", grad_branch, out_used, preferred_element_type=jnp.float32)
    grad_mixed = grad_mixed.astype(jnp.bfloat16).reshape(row_count, -1, HEADS, HEAD_DIM)
    split_qkv = joined.reshape(row_count, -1, 3, HEADS, HEAD_DIM)
    queries = split_qkv[:, :, 0]
    key_rows = split_qkv[:, :, 1]
    value_rows = split_qkv[:, :, 2]
    prob_full = jnp.exp(score_block(queries, key_rows, same_segment) - log_total)
    prob_low = prob_full.astype(jnp.bfloat16)
    grad_values = jnp.einsum(
        "rhqk,rqhe->rkhe", prob_low, grad_mixed, preferred_element_type=jnp.float32
    )
    grad_probs = jnp.einsum(
        "rqhe,rkhe->rhqk", grad_mixed, value_rows, preferred_element_type=jnp.float32
    )
    centred = jnp.sum(prob_full * grad_probs, axis=-1, keepdims=True)
    grad_scores = (prob_full * (grad_probs - centred)).astype(jnp.bfloat16)
    grad_queries = jnp.einsum(
        "rhqk,rkhe->rqhe", grad_scores, key_rows, preferred_element_type=jnp.float32
    ) * HEAD_DIM ** (-0.5)
    grad_keys = jnp.einsum(
        "rhqk,rqhe->rkhe", grad_scores, queries, preferred_element_type=jnp.float32
    ) * HEAD_DIM ** (-0.5)
    grad_joined = (
        jnp.stack([grad_queries, grad_keys, grad_values], axis=2)
        .reshape(-1, 3 * model_width)
        .astype(jnp.bfloat16)
    )
    qkv_bias_grad = jnp.sum(grad_joined, axis=0, dtype=jnp.float32)
    qkv_weight_grad = jnp.einsum(
        "td,tc->dc", hidden_low, grad_joined, preferred_element_type=jnp.float32
    )
    grad_hidden = grad_one + jnp.einsum(
        "tc,dc->td", grad_joined, qkv_used, preferred_element_type=jnp.float32
    )
    vector_grad = jnp.concatenate(
        [
            qkv_bias_grad[:model_width][None],
            qkv_bias_grad[2 * model_width :][None],
            out_bias_grad[None],
            gain_one_grad[None],
            shift_one_grad[None],
            in_bias_grad.reshape(4, model_width),
            back_bias_grad[None],
            gain_two_grad[None],
            shift_two_grad[None],
        ],
        axis=0,
    )
    return (
        grad_hidden,
        (qkv_weight_grad, out_weight_grad, in_weight_grad, back_weight_grad, vector_grad),
    )


def adam_step(weight, gradient, moment_one, moment_two, step_rate):
    first_moment = BETA_FIRST * moment_one + (1.0 - BETA_FIRST) * gradient
    second_moment = BETA_SECOND * moment_two + (1.0 - BETA_SECOND) * gradient * gradient
    first_hat = first_moment / (1.0 - BETA_FIRST**STEP)
    second_hat = second_moment / (1.0 - BETA_SECOND**STEP)
    updated = weight - step_rate * (
        first_hat / (jnp.sqrt(second_hat) + ADAM_EPSILON) + WEIGHT_DECAY * weight
    )
    return gradient, updated, second_moment


def update_layer(summed, masters, moments, layer_at):
    outcome = []
    for kind_at in range(5):
        step_rate = RATE_VECTOR if kind_at == 4 else RATE_MATRIX
        outcome.append(
            adam_step(
                masters[kind_at][layer_at],
                summed[kind_at],
                moments[kind_at][0, layer_at],
                moments[kind_at][1, layer_at],
                step_rate,
            )
        )
    return outcome


def local_parts(masters, layer_at):
    return tuple((master[layer_at].astype(jnp.bfloat16) for master in masters))


def collect(results, kind_at, member):
    return jnp.stack([layer_result[kind_at][member] for layer_result in results])


def on_device_any(
    tokens,
    segment_ids,
    cotangent,
    qkv_weight,
    out_weight,
    in_weight,
    back_weight,
    vectors,
    qkv_moments,
    out_moments,
    in_moments,
    back_moments,
    vector_moments,
):
    masters = (qkv_weight, out_weight, in_weight, back_weight, vectors)
    moments = (qkv_moments, out_moments, in_moments, back_moments, vector_moments)
    same_segment = (segment_ids[:, :, None] == segment_ids[:, None, :])[:, None]
    hidden = tokens.astype(jnp.float32)
    saved_states = []
    for layer_at in range(LAYERS):
        parts_now = local_parts(masters, layer_at)
        weights = (
            lax.all_gather(parts_now[0], "fsdp", axis=0, tiled=True),
            lax.all_gather(parts_now[1], "fsdp", axis=0, tiled=True),
            lax.all_gather(parts_now[2], "fsdp", axis=0, tiled=True),
            lax.all_gather(parts_now[3], "fsdp", axis=0, tiled=True),
            lax.all_gather(parts_now[4], "fsdp", axis=1, tiled=True),
        )
        hidden, kept_state = layer_forward(hidden, same_segment, weights)
        saved_states.append(kept_state)
    activations = hidden.astype(jnp.bfloat16)
    grad_hidden = cotangent.astype(jnp.float32)
    results = [None] * LAYERS
    for layer_at in reversed(range(LAYERS)):
        parts_now = local_parts(masters, layer_at)
        weights = (
            lax.all_gather(parts_now[0], "fsdp", axis=0, tiled=True),
            lax.all_gather(parts_now[1], "fsdp", axis=0, tiled=True),
            lax.all_gather(parts_now[2], "fsdp", axis=0, tiled=True),
            lax.all_gather(parts_now[3], "fsdp", axis=0, tiled=True),
            lax.all_gather(parts_now[4], "fsdp", axis=1, tiled=True),
        )
        grad_hidden, weight_grads = layer_backward(
            grad_hidden, same_segment, weights, saved_states[layer_at]
        )
        shards = (
            lax.psum_scatter(
                weight_grads[0].astype(jnp.bfloat16), "fsdp", scatter_dimension=0, tiled=True
            ).astype(jnp.float32),
            lax.psum_scatter(
                weight_grads[1].astype(jnp.bfloat16), "fsdp", scatter_dimension=0, tiled=True
            ).astype(jnp.float32),
            lax.psum_scatter(
                weight_grads[2].astype(jnp.bfloat16), "fsdp", scatter_dimension=0, tiled=True
            ).astype(jnp.float32),
            lax.psum_scatter(
                weight_grads[3].astype(jnp.bfloat16), "fsdp", scatter_dimension=0, tiled=True
            ).astype(jnp.float32),
            lax.psum_scatter(
                weight_grads[4].astype(jnp.bfloat16), "fsdp", scatter_dimension=1, tiled=True
            ).astype(jnp.float32),
        )
        totals = (
            lax.psum(shards[0].astype(jnp.bfloat16), "dp").astype(jnp.float32),
            lax.psum(shards[1].astype(jnp.bfloat16), "dp").astype(jnp.float32),
            lax.psum(shards[2].astype(jnp.bfloat16), "dp").astype(jnp.float32),
            lax.psum(shards[3].astype(jnp.bfloat16), "dp").astype(jnp.float32),
            lax.psum(shards[4].astype(jnp.bfloat16), "dp").astype(jnp.float32),
        )
        results[layer_at] = update_layer(totals, masters, moments, layer_at)
    return (
        activations,
        grad_hidden,
        collect(results, 0, 0),
        collect(results, 1, 0),
        collect(results, 2, 0),
        collect(results, 3, 0),
        collect(results, 4, 0),
        collect(results, 0, 1),
        collect(results, 1, 1),
        collect(results, 2, 1),
        collect(results, 3, 1),
        collect(results, 4, 1),
        collect(results, 0, 2),
        collect(results, 1, 2),
        collect(results, 2, 2),
        collect(results, 3, 2),
        collect(results, 4, 2),
    )


def on_device(
    tokens,
    segment_ids,
    cotangent,
    qkv_weight,
    out_weight,
    in_weight,
    back_weight,
    vectors,
    qkv_moments,
    out_moments,
    in_moments,
    back_moments,
    vector_moments,
):
    masters = (qkv_weight, out_weight, in_weight, back_weight, vectors)
    moments = (qkv_moments, out_moments, in_moments, back_moments, vector_moments)
    activations, wq, wo, wi, wb, vec, *kept, hlow = forward(
        tokens, segment_ids, vectors.transpose(1, 0, 2), *masters[:4]
    )
    grad, total, vtotal = backward(
        cotangent, segment_ids, vec, tokens, hlow, (wq, wo, wi, wb), kept
    )
    return adam(activations, grad, total, vtotal, masters, moments)


def solution(mesh):
    in_specs = (
        P(("fsdp", "dp"), None),
        P(("fsdp", "dp"), None),
        P(("fsdp", "dp"), None),
        P(None, "fsdp", None),
        P(None, "fsdp", None),
        P(None, "fsdp", None),
        P(None, "fsdp", None),
        P(None, None, "fsdp"),
        P(None, None, "fsdp", None),
        P(None, None, "fsdp", None),
        P(None, None, "fsdp", None),
        P(None, None, "fsdp", None),
        P(None, None, None, "fsdp"),
    )
    out_specs = (
        P(("fsdp", "dp"), None),
        P(("fsdp", "dp"), None),
        P(None, "fsdp", None),
        P(None, "fsdp", None),
        P(None, "fsdp", None),
        P(None, "fsdp", None),
        P(None, None, "fsdp"),
        P(None, "fsdp", None),
        P(None, "fsdp", None),
        P(None, "fsdp", None),
        P(None, "fsdp", None),
        P(None, None, "fsdp"),
        P(None, "fsdp", None),
        P(None, "fsdp", None),
        P(None, "fsdp", None),
        P(None, "fsdp", None),
        P(None, None, "fsdp"),
    )
    body = on_device if dict(mesh.shape) == {"fsdp": 8, "dp": 4} else on_device_any
    return jax.shard_map(
        body, mesh=mesh, in_specs=in_specs, out_specs=out_specs, check_vma=False
    )
```
